32 devices in a mesh: week: 4 (over x, core), row: 4 (over z), col: 2 (over y).
Axes of the slice: x: 2, y: 2, z: 4, core: 2. Of those that a mesh axis runs over, the one named last changes fastest.
Arguments:
- sensitivity: bfloat16 [4, 3, 1024, 4096], P('week', None, None, ('row', 'col')), may hold values from -0.1875 to 0.1875
- reach: int32 [4, 1024], P('week'), may hold values from 0 to 2, as said below
- obs_weight: float32 [4, 1024], P('week'), may hold values from 0.25 to 4
- prior_precision: float32 [4, 4096], P('week', ('row', 'col')), may hold values from 0.5 to 4
- pivot_solve: bfloat16 [4096, 4096], P('week', ('row', 'col')), may hold values from -0.09375 to 0.09375
Outputs:
- hessian_band: float32 [4, 3, 4096, 4096], P('week', None, ('row', 'col'))
- panel: bfloat16 [4096, 4096], P(('row', 'col'), 'week')
- schur: float32 [4096, 4096], P(('row', 'col'), 'week')
The draws below stay inside these ranges and needn't reach their ends.
Inputs may be any that keep to these rules, and one draw needn't show every extreme that they name: The number of observations at each reach differs widely from week to week; in some week w >= 2 every observation has reach 2.
All inputs are finite; a program needn't handle non-finite values.
Results may differ from the reference program's by a relative error of at most 0.013.
Values may be sent and summed in bfloat16 or wider, within the bound.
A program may use at most 128 MiB of HBM per device.

```python
import math
import jax
import jax.numpy as jnp

REG = 4096
OBS = 1024
LAGS = 3
NW = 4
N_WEEK = 4


def draw_reach(key, part):
    base = jax.random.fold_in(key, 7)
    keys = jax.random.split(base, 7)
    heavy = LAGS - 1 + jax.random.randint(keys[0], (), 0, NW - LAGS + 1)
    light = jnp.where(heavy + 1 < NW, heavy + 1, heavy - 1)
    lower = jax.random.randint(keys[1], (NW, 1), 0, 1001)
    spread = jax.random.randint(keys[2], (NW, 1), 0, 1001)
    upper = jnp.minimum(lower + spread, 1000)
    unit = jax.random.randint(keys[3], (NW, OBS), 0, 1000)
    mixed = jnp.minimum((unit >= lower).astype(jnp.int32) + (unit >= upper).astype(jnp.int32), LAGS - 1)
    count = jax.random.randint(keys[4], (), 1, OBS // 8 + 1)
    order = jax.random.permutation(keys[5], OBS)
    low_reach = jax.random.randint(keys[6], (OBS,), 0, LAGS - 1)
    light_row = jnp.where(order < count, LAGS - 1, low_reach)
    weeks = jnp.arange(NW)[:, None]
    result = jnp.where(weeks == heavy, LAGS - 1, jnp.where(weeks == light, light_row[None, :], mixed))
    return result.astype(jnp.int32)


def block_scale(rng, dims, pieces, least, largest):
    factor_of = 1.0
    for axis_at, shards_of in pieces:
        steps = jax.random.uniform(jax.random.fold_in(jax.random.fold_in(rng, 6), axis_at), (shards_of,), jnp.float32, least / len(pieces), largest / len(pieces))
        factor_of = factor_of * jnp.repeat(jnp.exp(steps), dims[axis_at] // shards_of).reshape((-1,) + (1,) * (len(dims) - 1 - axis_at))
    return factor_of


def centred(key, shape, deviation, limit, shards=(), kind=jnp.bfloat16):
    level = block_scale(key, shape, shards, -0.22, 0.18) if shards else 1.0
    array = jax.random.normal(key, shape, jnp.float32) * deviation * level
    return jnp.minimum(jnp.maximum(array, -limit), limit).astype(kind)


def setup_inputs(seed: int = 0) -> dict:
    streams_of = jax.random.split(jax.random.key(seed), 6)
    return {
        "sensitivity": centred(streams_of[0], (NW, LAGS, OBS, REG), OBS ** -0.5, 0.1875, ((0, 4), (3, 8))),
        "reach": draw_reach(jax.random.fold_in(streams_of[5], 71), 0),
        "obs_weight": jnp.clip(jnp.exp(math.log(4.0) - 2.7725887 * jax.random.uniform(streams_of[2], (NW, OBS), jnp.float32) ** block_scale(streams_of[2], (NW, OBS), ((0, 4),), -0.2, 0.2)), 0.25, 4.0),
        "prior_precision": jnp.clip(jnp.exp(math.log(4.0) - 2.0794415 * jax.random.uniform(streams_of[3], (NW, REG), jnp.float32) ** block_scale(streams_of[3], (NW, REG), ((0, 4), (1, 8)), -0.2, 0.2)), 0.5, 4.0),
        "pivot_solve": centred(streams_of[4], (REG, REG), REG ** -0.5, 0.09375, ((0, 4), (1, 8))),
    }


def reference(sensitivity, reach, obs_weight, prior_precision, pivot_solve):
    block_rows = []
    for i in range(N_WEEK):
        blocks = []
        for d in range(LAGS):
            total = jnp.zeros((REG, REG), jnp.float32)
            if i - d >= 0:
                for a in range(LAGS - d):
                    w = i + a
                    b = a + d
                    if w < N_WEEK:
                        keep = (reach[w] >= b).astype(jnp.float32) * obs_weight[w]
                        scaled = (keep[:, None] * sensitivity[w, a].astype(jnp.float32)).astype(jnp.bfloat16)
                        total = total + jnp.dot(scaled.T, sensitivity[w, b], preferred_element_type=jnp.float32)
                if d == 0:
                    total = total + jnp.diag(prior_precision[i])
            blocks.append(total)
        block_rows.append(jnp.stack(blocks))
    hessian_band = jnp.stack(block_rows)
    coupling = hessian_band[1, 1].astype(jnp.bfloat16)
    panel = jnp.dot(coupling, pivot_solve.T, preferred_element_type=jnp.float32).astype(jnp.bfloat16)
    schur = hessian_band[1, 0] - jnp.dot(panel, panel.T, preferred_element_type=jnp.float32)
    return hessian_band, panel, schur
```

```python
import functools

import jax
import jax.numpy as jnp
from jax import lax
from jax.experimental import pallas as pl
from jax.experimental.pallas import tpu as pltpu
from jax.sharding import PartitionSpec as P

ROW, COL, WEEK = "row", "col", "week"
DMA = pltpu.SemaphoreType.DMA

UNITS = 5
UNIT_SLOT = ((0, 0, 0, 0), (0, 0, 0, 0), (1, 1, 3, 3), (1, 2, 2, 3), (2, 0, 0, 2))
UNIT_HALF = ((0, 0, 0, 0), (1, 1, 1, 1), (0, 0, 1, 0), (1, 0, 1, 1), (0, 0, 0, 1))
LOCAL = {
    0: ((0, 0),) * 4,
    1: ((0, 1),) * 4,
    2: (None, None, (1, 1), (1, 0)),
    3: (None, None, (2, 1), (1, 1)),
    4: (None, None, None, (2, 1)),
}
FIRST = ((1, 1, 0, 0, 2), (1, 1, 1, 0, 3), (2, 2, 0, 0, 4), (2, 1, 0, 1, 2), (3, 2, 0, 1, 3))
ONWARD = (
    ((2, 1, 3, 0), (3, 1, 3, 1), (4, 1, 4, 2), (4, 2, 2, 4)),
    ((2, 2, 3, 3), (3, 3, 2, 0)),
    ((2, 1, 1, 3), (3, 0, 2, 0)),
    ((2, 2, 1, 0), (3, 2, 1, 1), (4, 2, 4, 2), (4, 1, 2, 4)),
)
RELAY = {0: (1, 1, 4), 3: (0, 2, 4)}
FLOWS = 6


def pick(week, values):
    out = jnp.int32(values[0])
    for k, value in enumerate(values[1:], 1):
        out = jnp.where(week == k, jnp.int32(value), out)
    return out


def gather_kernel(n_row, n_col, x_ref, f_ref, own, put_sem, first_s, first_r, main_s, main_r, band_s, band_r,
                  side_s, side_r, rest_s, rest_r, pass_s, pass_r, flow_s, flow_r):
    row, col, week = lax.axis_index(ROW), lax.axis_index(COL), lax.axis_index(WEEK)
    _, length, width = x_ref.shape
    half = length // 2
    band = max(half * 5 // 32 // 16 * 16, 16)
    n = n_row * n_col
    peers = range(1, n_col)
    n_week = 4
    has = (row < n_row - 1, row > 0)
    target = (lax.rem(row + 1, n_row), lax.rem(row + n_row - 1, n_row))

    barrier = pltpu.get_barrier_semaphore()
    for d in range(2):
        pl.semaphore_signal(barrier, inc=1, device_id={ROW: target[d]})
    for k in peers:
        pl.semaphore_signal(barrier, inc=1, device_id={COL: lax.rem(col + k, n_col)})
    for k in range(1, n_week):
        pl.semaphore_signal(barrier, inc=1, device_id={WEEK: lax.rem(week + k, n_week)})
    pl.semaphore_wait(barrier, 2 + (n_col - 1) + (n_week - 1))

    slots = [pick(week, UNIT_SLOT[u]) for u in range(UNITS)]
    starts = [pl.multiple_of(pick(week, UNIT_HALF[u]) * half, half) for u in range(UNITS)]

    def slab(at_row, at_col):
        return at_row * n_col + at_col

    def cell(slot, start, s, first=0, count=half):
        at = pl.ds(pl.multiple_of(s * width, width), width)
        return f_ref.at[slot, pl.ds(pl.multiple_of(start + first, 16), count), at]

    def place(u, s, first=0, count=half):
        return cell(slots[u], starts[u], s, first, count)

    def active(u, body):
        if u < 4:
            body()
        else:
            pl.when((week == 0) | (week == n_week - 1))(body)

    def origin(step, d):
        return lax.rem(row + n_row - step if d == 0 else row + step, n_row)

    def arrives(step, d):
        return row >= step if d == 0 else row + step < n_row

    def other(k):
        return lax.rem(col + n_col - k, n_col)

    def remote(ref, s_sem, r_sem, device, to=None):
        return pltpu.make_async_remote_copy(ref, ref if to is None else to, s_sem, r_sem, device_id=device)

    def main(u, step, d):
        return remote(place(u, slab(origin(step, d), col)), main_s.at[u, step, d], main_r.at[u, step, d],
                      {ROW: target[d]})

    def strip(u, step, d, k):
        return remote(place(u, slab(origin(step, d), other(k)), 0, band), band_s.at[u, step, d, k - 1],
                      band_r.at[u, step, d, k - 1], {ROW: target[d]})

    def side(u, k):
        return remote(place(u, slab(row, col), 0, band), side_s.at[u, k - 1], side_r.at[u, k - 1],
                      {COL: lax.rem(col + k, n_col)})

    def rest(u, k):
        return remote(place(u, slab(row, col), band, half - band), rest_s.at[u, k - 1], rest_r.at[u, k - 1],
                      {COL: lax.rem(col + k, n_col)})

    def onward(u, step, d, k):
        return remote(place(u, slab(origin(step, d), col), band, half - band), pass_s.at[u, step - 1, d, k - 1],
                      pass_r.at[u, step - 1, d, k - 1], {COL: lax.rem(col + k, n_col)})

    def flows(w, u, s):
        sent = 0
        for i, (unit, to_week, to_slot, flow) in enumerate(ONWARD[w]):
            if unit == u:
                start = UNIT_HALF[u][w] * half
                yield remote(cell(UNIT_SLOT[u][w], start, s), flow_s.at[i, s], flow_r.at[flow, s],
                             {WEEK: jnp.int32(to_week)}, cell(to_slot, start, s))

    def spread(u, s, act="start"):
        for w in range(n_week):
            if any(unit == u for unit, *_ in ONWARD[w]):
                @pl.when(week == w)
                def _(w=w):
                    for copy in flows(w, u, s):
                        copy.start() if act == "start" else copy.wait_send()

    def relay(s, act):
        for w, (h, to_week, to_slot) in RELAY.items():
            @pl.when(week == w)
            def _(w=w, h=h, to_week=to_week, to_slot=to_slot):
                ref = cell(2, h * half, s)
                copy = remote(ref, flow_s.at[4, s], flow_r.at[5, s], {WEEK: jnp.int32(to_week)},
                              cell(to_slot, h * half, s))
                if act == "start":
                    remote(ref, flow_s.at[0, s], flow_r.at[0, s], {WEEK: jnp.int32(to_week)}).wait_recv()
                    copy.start()
                else:
                    copy.wait_send()

    mine = slab(row, col)

    def first(act):
        for i, (w, lag, h, to_week, u) in enumerate(FIRST):
            @pl.when(week == w)
            def _(w=w, lag=lag, h=h, to_week=to_week, u=u):
                copy = remote(x_ref.at[lag, pl.ds(h * half, half), :], first_s.at[u], first_r.at[u],
                              {WEEK: jnp.int32(to_week)}, cell(UNIT_SLOT[u][to_week], h * half, mine))
                copy.start() if act == "start" else copy.wait_send()

    def take(u, w):
        lag, h = LOCAL[u][w]
        return pltpu.make_async_copy(x_ref.at[lag, pl.ds(h * half, half), :], own.at[u], put_sem.at[u])

    def put(u):
        return pltpu.make_async_copy(own.at[u], place(u, mine), put_sem.at[u])

    def local(u, body):
        groups = {}
        for w in range(n_week):
            groups.setdefault(LOCAL[u][w], []).append(w)
        for what, weeks in groups.items():
            if what is None:
                continue
            if len(weeks) == n_week:
                body(weeks[0])
            else:
                for w in weeks:
                    pl.when(week == w)(functools.partial(body, w))

    first("start")
    for u in range(UNITS):
        local(u, lambda w, u=u: take(u, w).start())
    for u in range(UNITS):
        def move(w, u=u):
            take(u, w).wait()
            put(u).start()

        local(u, move)

    def begin(u):
        local(u, lambda w: put(u).wait())
        for _, _, _, to_week, unit in FIRST:
            if unit == u:
                @pl.when(week == to_week)
                def _():
                    remote(place(u, mine), first_s.at[u], first_r.at[u], {ROW: target[0]}).wait_recv()

        def go():
            for k in peers:
                side(u, k).start()
            for d in range(2):
                pl.when(has[d])(lambda d=d: main(u, 0, d).start())
            for k in peers:
                rest(u, k).start()

        active(u, go)
        spread(u, mine)

    for u in range(UNITS):
        begin(u)

    for u in range(UNITS):
        def spread_band(u=u):
            for k in peers:
                side(u, k).wait_recv()
                for d in range(2):
                    pl.when(has[d])(lambda d=d, k=k: strip(u, 0, d, k).start())

        active(u, spread_band)

    def across(step):
        for u in range(UNITS):
            if step == 0:
                def body(u=u):
                    for k in peers:
                        rest(u, k).wait_recv()
                        spread(u, slab(row, other(k)))

                active(u, body)
            else:
                for d in range(2):
                    def body(u=u, d=d):
                        for k in peers:
                            onward(u, step, d, k).wait_recv()
                            spread(u, slab(origin(step, d), other(k)))

                    active(u, lambda d=d, body=body: pl.when(arrives(step, d))(body))

    def relays(step, act):
        if step == 0:
            relay(mine, act)
            for k in peers:
                relay(slab(row, other(k)), act)
        else:
            for d in range(2):
                @pl.when(arrives(step, d))
                def _(d=d):
                    relay(slab(origin(step, d), col), act)
                    for k in peers:
                        relay(slab(origin(step, d), other(k)), act)

    for step in range(1, n_row):
        for u in range(UNITS):
            for d in range(2):
                def advance(u=u, d=d, step=step):
                    main(u, step - 1, d).wait_recv()
                    if step < n_row - 1:
                        pl.when(has[d])(lambda: main(u, step, d).start())
                    for k in peers:
                        onward(u, step, d, k).start()
                    spread(u, slab(origin(step, d), col))
                    for k in peers:
                        strip(u, step - 1, d, k).wait_recv()
                        if step < n_row - 1:
                            pl.when(has[d])(lambda k=k: strip(u, step, d, k).start())

                active(u, lambda d=d, step=step, advance=advance: pl.when(arrives(step, d))(advance))
        across(step - 1)
        if step > 1:
            relays(step - 2, "start")
    across(n_row - 1)
    for step in range(max(n_row - 2, 0), n_row):
        relays(step, "start")

    @pl.when((week == 1) | (week == 2))
    def _():
        for s in range(n):
            for flow in range(FLOWS):
                ref = cell(0, 0, s)
                remote(ref, flow_s.at[0, s], flow_r.at[flow, s], {ROW: target[0]}).wait_recv()

    first("wait")
    for u in range(UNITS):
        def finish(u=u):
            for k in peers:
                side(u, k).wait_send()
                rest(u, k).wait_send()
            for d in range(2):
                @pl.when(has[d])
                def _(d=d):
                    main(u, 0, d).wait_send()
                    for k in peers:
                        strip(u, 0, d, k).wait_send()
                for step in range(1, n_row):
                    @pl.when(arrives(step, d))
                    def _(d=d, step=step):
                        for k in peers:
                            onward(u, step, d, k).wait_send()
                        if step < n_row - 1:
                            @pl.when(has[d])
                            def _():
                                main(u, step, d).wait_send()
                                for k in peers:
                                    strip(u, step, d, k).wait_send()

        active(u, finish)
        if u >= 2:
            for s in range(n):
                spread(u, s, "wait")
    for s in range(n):
        relay(s, "wait")


def gather(x, collective_id):
    n_row, n_col = lax.axis_size(ROW), lax.axis_size(COL)
    _, length, width = x.shape
    n = n_row * n_col
    kinds = (UNITS, n_row - 1, 2)
    wide = (*kinds, n_col - 1)
    sides = (UNITS, n_col - 1)
    sent = length * width * 2 * (n - 1) * 9 // 4
    return pl.pallas_call(
        functools.partial(gather_kernel, n_row, n_col),
        out_shape=jax.ShapeDtypeStruct((5, length, width * n), x.dtype),
        in_specs=[pl.BlockSpec(memory_space=pl.ANY)],
        out_specs=pl.BlockSpec(memory_space=pl.ANY),
        scratch_shapes=[
            pltpu.VMEM((UNITS, length // 2, width), x.dtype), DMA((UNITS,)), DMA((UNITS,)), DMA((UNITS,)),
            DMA(kinds), DMA(kinds), DMA(wide), DMA(wide), DMA(sides), DMA(sides), DMA(sides), DMA(sides),
            DMA(wide), DMA(wide), DMA((5, n)), DMA((FLOWS, n)),
        ],
        compiler_params=pltpu.CompilerParams(collective_id=collective_id, has_side_effects=True),
        cost_estimate=pl.CostEstimate(flops=0, bytes_accessed=sent * 8, transcendentals=0),
    )(x)


def exchange_kernel(x_ref, e_ref, own, put_sem, send, recv):
    week = lax.axis_index(WEEK)
    n_week = 4
    barrier = pltpu.get_barrier_semaphore()
    for k in range(1, n_week):
        pl.semaphore_signal(barrier, inc=1, device_id={WEEK: lax.rem(week + k, n_week)})
    pl.semaphore_wait(barrier, n_week - 1)
    roles = ((1, ((1, 2), (0, 0)), 0, 2), (2, ((2, 3), (1, 1)), 3, 1))

    def copy(src, place, to, sem):
        return pltpu.make_async_remote_copy(src, e_ref.at[place], send.at[place, sem], recv.at[place],
                                            device_id={WEEK: jnp.int32(to)})

    for w, items, near, far in roles:
        @pl.when(week == w)
        def _(w=w, items=items, near=near, far=far):
            for lag, at in items:
                copy(x_ref.at[lag], at, far, 0).start()
            for lag, at in items:
                copy(x_ref.at[lag], at, near, 1).start()
                pltpu.make_async_copy(x_ref.at[lag], own.at[lag], put_sem.at[lag]).start()
            for lag, at in items:
                pltpu.make_async_copy(x_ref.at[lag], own.at[lag], put_sem.at[lag]).wait()
                pltpu.make_async_copy(own.at[lag], e_ref.at[at], put_sem.at[lag]).start()
            theirs = roles[2 - w][1]
            for _, at in theirs:
                copy(e_ref.at[at], at, near, 0).wait_recv()
                copy(e_ref.at[at], at, near, 0).start()
            for lag, at in items:
                copy(x_ref.at[lag], at, far, 0).wait_send()
                copy(x_ref.at[lag], at, near, 1).wait_send()
                pltpu.make_async_copy(own.at[lag], e_ref.at[at], put_sem.at[lag]).wait()
            for _, at in theirs:
                copy(e_ref.at[at], at, near, 0).wait_send()

    @pl.when((week == 0) | (week == n_week - 1))
    def _():
        for at in range(4):
            copy(e_ref.at[at], at, 0, 0).wait_recv()


def exchange(x, collective_id):
    _, length, width = x.shape
    return pl.pallas_call(
        exchange_kernel,
        out_shape=jax.ShapeDtypeStruct((4, length, width), x.dtype),
        in_specs=[pl.BlockSpec(memory_space=pl.ANY)],
        out_specs=pl.BlockSpec(memory_space=pl.ANY),
        scratch_shapes=[pltpu.VMEM(x.shape, x.dtype), DMA((3,)), DMA((4, 2)), DMA((4,))],
        compiler_params=pltpu.CompilerParams(collective_id=collective_id, has_side_effects=True),
    )(x)


PRODUCTS = ((0, 0, 0, (0, 3)), (0, 1, 1, (0, 2)), (0, 2, 2, (0, 1)), (1, 0, 3, (1, 3)), (1, 1, 4, (1, 2)),
            (2, 0, 2, (2, 3)))


def bands_kernel(at_ref, left_ref, weight_ref, prior_ref, full_ref, out_ref, turned):
    week, mine = at_ref[0], at_ref[1]
    tile = pl.program_id(0)
    width = left_ref.shape[2]
    columns = full_ref.shape[2]

    @pl.when(tile == 0)
    def _():
        for p, (_, slot, _, (lo, hi)) in enumerate(PRODUCTS):
            @pl.when((week >= lo) & (week <= hi))
            def _(p=p, slot=slot):
                flat = left_ref[slot].T.astype(jnp.float32) * weight_ref[p][None, :]
                turned[p] = flat.astype(turned.dtype)

    out_ref[...] = jnp.zeros_like(out_ref)
    for p, (band, _, slot, (lo, hi)) in enumerate(PRODUCTS):
        @pl.when((week >= lo) & (week <= hi))
        def _(p=p, band=band, slot=slot):
            out_ref[band] += jnp.dot(turned[p], full_ref[slot], preferred_element_type=jnp.float32)

    row_ids = lax.broadcasted_iota(jnp.int32, (width, columns), 0) + mine * width
    col_ids = lax.broadcasted_iota(jnp.int32, (width, columns), 1) + tile * columns
    out_ref[0] += jnp.where(row_ids == col_ids, prior_ref[:, :1], 0.0)


def bands(at, full, weights, prior):
    slots, length, regions = full.shape
    width = prior.shape[0]
    columns = min(512, regions)
    return pl.pallas_call(
        bands_kernel,
        out_shape=jax.ShapeDtypeStruct((3, width, regions), jnp.float32),
        grid_spec=pltpu.PrefetchScalarGridSpec(
            num_scalar_prefetch=1,
            grid=(regions // columns,),
            in_specs=[
                pl.BlockSpec((3, length, width), lambda j, at: (0, 0, at[1]), pipeline_mode=pl.Buffered(1)),
                pl.BlockSpec(weights.shape, lambda j, at: (0, 0)),
                pl.BlockSpec(prior.shape, lambda j, at: (0, 0)),
                pl.BlockSpec((slots, length, columns), lambda j, at: (0, 0, j)),
            ],
            out_specs=pl.BlockSpec((3, width, columns), lambda j, at: (0, 0, j)),
            scratch_shapes=[pltpu.VMEM((len(PRODUCTS), width, length), full.dtype)],
        ),
        compiler_params=pltpu.CompilerParams(dimension_semantics=("arbitrary",), vmem_limit_bytes=60 << 20),
        cost_estimate=pl.CostEstimate(
            flops=10 * width * length * regions, bytes_accessed=full.size * 2 + 12 * width * regions,
            transcendentals=0),
    )(at, full, weights, prior, full)


def contract_first(left, right):
    return lax.dot_general(left, right, (((0,), (0,)), ((), ())), preferred_element_type=jnp.float32)


def contract_last(left, right):
    return lax.dot_general(left, right, (((1,), (1,)), ((), ())), preferred_element_type=jnp.float32)


def body(sensitivity, reach, obs_weight, prior_precision, pivot_solve):
    week = lax.axis_index(WEEK)
    n_week, n_row, n_col = (lax.axis_size(name) for name in (WEEK, ROW, COL))
    assert n_week == 4
    local = sensitivity[0]
    lags, length, width = local.shape
    mine = lax.axis_index(ROW) * n_col + lax.axis_index(COL)

    lag = jnp.arange(lags)[:, None]
    own_weight = jnp.where((reach >= lag) & (week >= lag), obs_weight, 0.0)
    by_week = lax.all_gather(own_weight, WEEK)
    later = jnp.concatenate([by_week, jnp.zeros((lags, lags, length), by_week.dtype)])
    here = lax.dynamic_slice(later, (week, 0, 0), (lags, lags, length))
    weights = jnp.stack([here[0, 0], here[1, 1], here[2, 2], here[0, 1], here[1, 2], here[0, 2]])

    near = exchange(local, 1)
    low = jnp.concatenate([near[2], near[3]])
    part = contract_last(low, pivot_solve).astype(jnp.bfloat16)
    whole = lax.psum(part, (ROW, COL))
    part, local = lax.optimization_barrier((part, local))
    full = gather(local, 0)
    panel_weight = jnp.concatenate([by_week[1, 1], by_week[2, 2]])
    left = (panel_weight[:, None] * near[:2].reshape(2 * length, width).astype(jnp.float32)).astype(jnp.bfloat16)
    panel = contract_first(left, whole).astype(jnp.bfloat16)
    inner = contract_last(panel, whole).astype(jnp.bfloat16)
    inner = lax.psum(inner, WEEK)

    at = jnp.stack([week, mine]).astype(jnp.int32)
    prior = jnp.broadcast_to(prior_precision[0][:, None], (width, 128))
    h = bands(at, full, weights, prior)

    right = (inner.astype(jnp.float32) * panel_weight).astype(jnp.bfloat16)
    spent = right.shape[0]
    out = h[0] - (jnp.dot(right[:, :length], full[0], preferred_element_type=jnp.float32)
                  + jnp.dot(right[:, length:], full[1], preferred_element_type=jnp.float32))
    out = out.astype(jnp.bfloat16)
    quarter = out.shape[1] // n_week
    schur = out[:, quarter : 2 * quarter]
    for w in (0, 2, 3):
        moved = lax.ppermute(out[:, w * quarter : (w + 1) * quarter], WEEK, [(1, w)])
        schur = jnp.where(week == w, moved, schur)
    return (h[None], panel, schur.astype(jnp.float32))


def solution(mesh):
    placed = (
        P(WEEK, None, None, (ROW, COL)),
        P(WEEK, None),
        P(WEEK, None),
        P(WEEK, (ROW, COL)),
        P(WEEK, (ROW, COL)),
    )
    return jax.shard_map(
        body,
        mesh=mesh,
        in_specs=placed,
        out_specs=(
            P(WEEK, None, (ROW, COL), None),
            P((ROW, COL), WEEK),
            P((ROW, COL), WEEK),
        ),
        check_vma=False,
    )
```

```python
import functools

import jax
import jax.numpy as jnp
from jax import lax
from jax.experimental import pallas as pl
from jax.experimental.pallas import tpu as pltpu
from jax.sharding import PartitionSpec as P

ROW, COL, WEEK = "row", "col", "week"
DMA = pltpu.SemaphoreType.DMA

UNITS = 5
UNIT_SLOT = ((0, 0, 0, 0), (0, 0, 0, 0), (1, 1, 3, 3), (1, 2, 2, 3), (2, 0, 0, 2))
UNIT_HALF = ((0, 0, 0, 0), (1, 1, 1, 1), (0, 0, 1, 0), (1, 0, 1, 1), (0, 0, 0, 1))
LOCAL = {
    0: ((0, 0),) * 4,
    1: ((0, 1),) * 4,
    2: (None, None, (1, 1), (1, 0)),
    3: (None, None, (2, 1), (1, 1)),
    4: (None, None, None, (2, 1)),
}
FIRST = ((1, 1, 0, 0, 2), (1, 1, 1, 0, 3), (2, 2, 0, 0, 4), (2, 1, 0, 1, 2), (3, 2, 0, 1, 3))
ONWARD = (
    ((2, 1, 3, 0), (3, 1, 3, 1), (4, 1, 4, 2), (4, 2, 2, 4)),
    ((2, 2, 3, 3), (3, 3, 2, 0)),
    ((2, 1, 1, 3), (3, 0, 2, 0)),
    ((2, 2, 1, 0), (3, 2, 1, 1), (4, 2, 4, 2), (4, 1, 2, 4)),
)
RELAY = {0: (1, 1, 4), 3: (0, 2, 4)}
FLOWS = 6


def pick(week, values):
    out = jnp.int32(values[0])
    for k, value in enumerate(values[1:], 1):
        out = jnp.where(week == k, jnp.int32(value), out)
    return out


def contract_last(left, right):
    return lax.dot_general(left, right, (((1,), (1,)), ((), ())), preferred_element_type=jnp.float32)


def gather_kernel(n_row, n_col, x_ref, pivot_ref, weight_ref, f_ref, panel_ref, inner_ref, weights_ref,
                  own, put_sem, first_s, first_r, main_s, main_r, band_s, band_r,
                  side_s, side_r, rest_s, rest_r, pass_s, pass_r, flow_s, flow_r,
                  low, piv, high, part, came, whole, turned, pan, inn, inn_in, wall,
                  low_s, low_r, piv_s, piv_r, high_s, high_r, loc, sum_s, sum_r, all_s, all_r,
                  pan_s, pan_r, inn_s, inn_r, wt_s, wt_r):
    row, col, week = lax.axis_index(ROW), lax.axis_index(COL), lax.axis_index(WEEK)
    _, length, width = x_ref.shape
    half = length // 2
    band = max(half * 5 // 32 // 16 * 16, 16)
    n = n_row * n_col
    peers = range(1, n_col)
    n_week = 4
    has = (row < n_row - 1, row > 0)
    target = (lax.rem(row + 1, n_row), lax.rem(row + n_row - 1, n_row))

    barrier = pltpu.get_barrier_semaphore()
    for d in range(2):
        pl.semaphore_signal(barrier, inc=1, device_id={ROW: target[d]})
    for k in peers:
        pl.semaphore_signal(barrier, inc=1, device_id={COL: lax.rem(col + k, n_col)})
    for k in range(1, n_week):
        pl.semaphore_signal(barrier, inc=1, device_id={WEEK: lax.rem(week + k, n_week)})
    for k in peers:
        pl.semaphore_signal(barrier, inc=1, device_id={ROW: n_row - 1 - row, COL: lax.rem(col + k, n_col)})
    pair = row + 1 - 2 * lax.rem(row, 2)
    pl.semaphore_signal(barrier, inc=1, device_id={WEEK: n_week - 1 - week, ROW: pair})
    pl.semaphore_wait(barrier, 2 + 2 * (n_col - 1) + (n_week - 1) + 1)
    inside = (row > 0) & (row < n_row - 1)
    outside = (row == 0) | (row == n_row - 1)

    slots = [pick(week, UNIT_SLOT[u]) for u in range(UNITS)]
    starts = [pl.multiple_of(pick(week, UNIT_HALF[u]) * half, half) for u in range(UNITS)]

    def slab(at_row, at_col):
        return at_row * n_col + at_col

    def cell(slot, start, s, first=0, count=half):
        at = pl.ds(pl.multiple_of(s * width, width), width)
        return f_ref.at[slot, pl.ds(pl.multiple_of(start + first, 16), count), at]

    def place(u, s, first=0, count=half):
        return cell(slots[u], starts[u], s, first, count)

    def active(u, body):
        if u < 4:
            body()
        else:
            pl.when((week == 0) | (week == n_week - 1))(body)

    def origin(step, d):
        return lax.rem(row + n_row - step if d == 0 else row + step, n_row)

    def arrives(step, d):
        return row >= step if d == 0 else row + step < n_row

    def other(k):
        return lax.rem(col + n_col - k, n_col)

    def remote(ref, s_sem, r_sem, device, to=None):
        return pltpu.make_async_remote_copy(ref, ref if to is None else to, s_sem, r_sem, device_id=device)

    def main(u, step, d):
        return remote(place(u, slab(origin(step, d), col)), main_s.at[u, step, d], main_r.at[u, step, d],
                      {ROW: target[d]})

    def strip(u, step, d, k):
        return remote(place(u, slab(origin(step, d), other(k)), 0, band), band_s.at[u, step, d, k - 1],
                      band_r.at[u, step, d, k - 1], {ROW: target[d]})

    def side(u, k):
        return remote(place(u, slab(row, col), 0, band), side_s.at[u, k - 1], side_r.at[u, k - 1],
                      {COL: lax.rem(col + k, n_col)})

    def rest(u, k):
        return remote(place(u, slab(row, col), band, half - band), rest_s.at[u, k - 1], rest_r.at[u, k - 1],
                      {COL: lax.rem(col + k, n_col)})

    def onward(u, step, d, k):
        return remote(place(u, slab(origin(step, d), col), band, half - band), pass_s.at[u, step - 1, d, k - 1],
                      pass_r.at[u, step - 1, d, k - 1], {COL: lax.rem(col + k, n_col)})

    def flows(w, u, s):
        sent = 0
        for i, (unit, to_week, to_slot, flow) in enumerate(ONWARD[w]):
            if unit == u:
                start = UNIT_HALF[u][w] * half
                yield remote(cell(UNIT_SLOT[u][w], start, s), flow_s.at[i, s], flow_r.at[flow, s],
                             {WEEK: jnp.int32(to_week)}, cell(to_slot, start, s))

    def spread(u, s, act="start"):
        for w in range(n_week):
            if any(unit == u for unit, *_ in ONWARD[w]):
                @pl.when(week == w)
                def _(w=w):
                    for copy in flows(w, u, s):
                        copy.start() if act == "start" else copy.wait_send()

    def relay(s, act):
        for w, (h, to_week, to_slot) in RELAY.items():
            @pl.when(week == w)
            def _(w=w, h=h, to_week=to_week, to_slot=to_slot):
                ref = cell(2, h * half, s)
                copy = remote(ref, flow_s.at[4, s], flow_r.at[5, s], {WEEK: jnp.int32(to_week)},
                              cell(to_slot, h * half, s))
                if act == "start":
                    remote(ref, flow_s.at[0, s], flow_r.at[0, s], {WEEK: jnp.int32(to_week)}).wait_recv()
                    copy.start()
                else:
                    copy.wait_send()

    mine = slab(row, col)

    def first(act):
        for i, (w, lag, h, to_week, u) in enumerate(FIRST):
            @pl.when(week == w)
            def _(w=w, lag=lag, h=h, to_week=to_week, u=u):
                copy = remote(x_ref.at[lag, pl.ds(h * half, half), :], first_s.at[u], first_r.at[u],
                              {WEEK: jnp.int32(to_week)}, cell(UNIT_SLOT[u][to_week], h * half, mine))
                copy.start() if act == "start" else copy.wait_send()

    def take(u, w):
        lag, h = LOCAL[u][w]
        return pltpu.make_async_copy(x_ref.at[lag, pl.ds(h * half, half), :], own.at[u], put_sem.at[u])

    def put(u):
        return pltpu.make_async_copy(own.at[u], place(u, mine), put_sem.at[u])

    def local(u, body):
        groups = {}
        for w in range(n_week):
            groups.setdefault(LOCAL[u][w], []).append(w)
        for what, weeks in groups.items():
            if what is None:
                continue
            if len(weeks) == n_week:
                body(weeks[0])
            else:
                for w in weeks:
                    pl.when(week == w)(functools.partial(body, w))

    far = slab(pair, col)
    slabs = (mine, far)
    members = 2 * n_col
    me = (row - 1) * n_col + col
    chunk = 2 * length // members
    slices = pivot_ref.shape[0]

    def op_rows(op):
        return pl.ds(op * length, length)

    def low_copy(src, j, op, i, device):
        return remote(src, low_s.at[j, op, i], low_r.at[j, op], device, low.at[j, op_rows(op), :])

    def high_copy(src, j, op, i, device):
        return remote(src, high_s.at[j, op, i], high_r.at[j, op], device, high.at[j, op_rows(op), :])

    def to_week(w):
        return {WEEK: jnp.int32(w)}

    def pivot_out():
        return remote(pivot_ref, piv_s.at[0], piv_r.at[0], {ROW: pair}, piv.at[1])

    def local_copy(src, dst, i):
        return pltpu.make_async_copy(src, dst, loc.at[i])

    def weight_copy(k):
        return remote(weight_ref, wt_s.at[k - 1], wt_r.at[k - 1], {WEEK: lax.rem(week + k, n_week)}, wall.at[week])

    ROLES = ((1, 0, 1, 0, 2, 1), (2, 1, 2, 3, 1, 0))

    def early():
        for k in range(1, n_week):
            weight_copy(k).start()
        pltpu.make_async_copy(weight_ref, wall.at[week], wt_s.at[n_week - 1]).start()

        @pl.when(outside)
        def _():
            for w, op, lag, *_ in ROLES:
                @pl.when(week == w)
                def _(op=op, lag=lag):
                    low_copy(x_ref.at[lag], 1, op, 0, {ROW: pair}).start()
            pivot_out().start()

        @pl.when(inside)
        def _():
            local_copy(pivot_ref, piv.at[0], 0).start()
            for w, op, lag, near, across, _ in ROLES:
                @pl.when(week == w)
                def _(op=op, lag=lag, near=near, across=across):
                    low_copy(x_ref.at[lag], 0, op, 0, to_week(across)).start()
                    low_copy(x_ref.at[lag], 0, op, 1, to_week(near)).start()
                    local_copy(x_ref.at[lag], low.at[0, op_rows(op), :], 1).start()

    def spread_low():
        for w, op, lag, near, across, theirs in ROLES:
            @pl.when(week == w)
            def _(op=op, lag=lag, near=near, across=across, theirs=theirs):
                ref = low.at[1, op_rows(op), :]
                low_copy(ref, 1, op, 0, to_week(across)).wait_recv()
                low_copy(ref, 1, op, 0, to_week(across)).start()
                low_copy(ref, 1, op, 1, to_week(near)).start()
                for j in range(2):
                    ref = low.at[j, op_rows(theirs), :]
                    low_copy(ref, j, theirs, 0, to_week(near)).wait_recv()
                    low_copy(ref, j, theirs, 0, to_week(near)).start()
                local_copy(x_ref.at[lag], low.at[0, op_rows(op), :], 1).wait()

        @pl.when((week == 0) | (week == n_week - 1))
        def _():
            for j in range(2):
                for op in range(2):
                    low_copy(low.at[j, op_rows(op), :], j, op, 0, to_week(1)).wait_recv()

        pivot_out().wait_recv()
        local_copy(pivot_ref, piv.at[0], 0).wait()

    def rows_of(m):
        return pl.ds(pl.multiple_of(m * chunk, chunk), chunk)

    def member(k):
        m = lax.rem(me + k, members)
        return m, {ROW: 1 + m // n_col, COL: lax.rem(m, n_col)}

    def sum_copy(k):
        m, device = member(k)
        return remote(part.at[rows_of(m), :], sum_s.at[k - 1], sum_r.at[k - 1], device, came.at[k - 1])

    def all_copy(k):
        _, device = member(k)
        return remote(whole.at[rows_of(me), :], all_s.at[k - 1], all_r.at[k - 1], device)

    def make_part():
        @pl.loop(0, members)
        def _(m):
            at = rows_of(m)
            total = contract_last(low[0, at, :], piv[0]) + contract_last(low[1, at, :], piv[1])
            part[at, :] = total.astype(part.dtype)

        for k in range(1, members):
            sum_copy(k).start()

    def make_whole():
        for k in range(1, members):
            sum_copy(k).wait_recv()
        total = part[rows_of(me), :].astype(jnp.float32)
        for k in range(1, members):
            total = total + came[k - 1].astype(jnp.float32)
        whole[rows_of(me), :] = total.astype(whole.dtype)
        for k in range(1, members):
            all_copy(k).start()

    def column(slot, s):
        return f_ref.at[slot, :, pl.ds(pl.multiple_of(s * width, width), width)]

    def early_flow(s):
        ref = cell(0, 0, s)
        return remote(ref, flow_s.at[0, s], flow_r.at[3, s], {ROW: target[0]})

    def start_high():
        @pl.when((week == 1) | (week == 2))
        def _():
            for s in slabs:
                early_flow(s).wait_recv()

        @pl.when(week == 1)
        def _():
            for j, s in enumerate(slabs):
                high_copy(column(0, s), j, 0, 0, to_week(2)).start()
                high_copy(column(0, s), j, 0, 1, to_week(0)).start()
                high_copy(column(1, s), j, 1, 0, to_week(0)).start()
                local_copy(column(0, s), high.at[j, op_rows(0), :], 2 + j).start()
                local_copy(column(1, s), high.at[j, op_rows(1), :], 4 + j).start()

        @pl.when(week == 2)
        def _():
            for j, s in enumerate(slabs):
                high_copy(column(3, s), j, 1, 0, to_week(3)).start()
                local_copy(column(3, s), high.at[j, op_rows(1), :], 4 + j).start()

    def wait_high():
        for j, s in enumerate(slabs):
            @pl.when(week == 1)
            def _(j=j, s=s):
                local_copy(column(0, s), high.at[j, op_rows(0), :], 2 + j).wait()

            @pl.when(week != 1)
            def _(j=j):
                high_copy(high.at[j, op_rows(0), :], j, 0, 0, to_week(3)).wait_recv()

            @pl.when(week == 2)
            def _(j=j):
                high_copy(high.at[j, op_rows(0), :], j, 0, 0, to_week(3)).start()

            @pl.when((week == 1) | (week == 2))
            def _(j=j, s=s):
                local_copy(column(1, s), high.at[j, op_rows(1), :], 4 + j).wait()

            @pl.when((week == 0) | (week == n_week - 1))
            def _(j=j):
                high_copy(high.at[j, op_rows(1), :], j, 1, 0, to_week(3)).wait_recv()

    def panel_out():
        return remote(pan.at[1], pan_s.at[0], pan_r.at[0], {ROW: pair}, panel_ref)

    def inner_near(j):
        return remote(inn.at[j], inn_s.at[j], inn_r.at[j], {WEEK: jnp.where(week == 0, 1, 2)}, inn_in.at[j])

    def inner_far(j, i):
        device = {WEEK: jnp.int32(1)} if j == 0 else {WEEK: jnp.int32(1), ROW: pair}
        return remote(inn.at[j], inn_s.at[j], inn_r.at[2 + i], device, inner_ref.at[i])

    def make_panel():
        for k in range(1, members):
            all_copy(k).wait_recv()
        wait_high()
        for k in range(1, n_week):
            weight_copy(k).wait_recv()
        pltpu.make_async_copy(weight_ref, wall.at[week], wt_s.at[n_week - 1]).wait()
        step = min(length, 512)
        for j in range(2):
            for op in range(2):
                for at in range(0, length, step):
                    rows = pl.ds(op * length + at, step)
                    flat = high[j, rows, :].T.astype(jnp.float32) * wall[1 + op, 1 + op, pl.ds(at, step)][None, :]
                    turned[j, :, rows] = flat.astype(turned.dtype)
        tile = min(slices, 256)
        for j in range(2):
            @pl.loop(0, slices // tile)
            def _(i, j=j):
                at = pl.ds(pl.multiple_of(i * tile, tile), tile)
                pan[j, :, at] = jnp.dot(turned[j], whole[:, at], preferred_element_type=jnp.float32).astype(pan.dtype)

            if j == 0:
                local_copy(pan.at[0], panel_ref, 0).start()
            else:
                panel_out().start()
        for j in (1, 0):
            @pl.loop(0, 2 * length // tile)
            def _(i, j=j):
                at = pl.ds(pl.multiple_of(i * tile, tile), tile)
                inn[j, :, at] = contract_last(pan[j], whole[at, :]).astype(inn.dtype)

            @pl.when((week == 0) | (week == n_week - 1))
            def _(j=j):
                inner_near(j).start()

    def join_inner():
        @pl.when((week == 1) | (week == 2))
        def _():
            for j in (1, 0):
                inner_near(j).wait_recv()
                inn[j] = (inn[j].astype(jnp.float32) + inn_in[j].astype(jnp.float32)).astype(inn.dtype)

                @pl.when(week == 2)
                def _(j=j):
                    inner_far(j, 1).start()

                @pl.when(week == 1)
                def _(j=j):
                    if j == 1:
                        inner_far(1, 0).start()
                    else:
                        local_copy(inn.at[0], inner_ref.at[0], 1).start()

    def end_inner():
        @pl.when(week == 1)
        def _():
            inner_far(1, 1).wait_recv()
            pl.when(outside)(lambda: inner_far(1, 0).wait_recv())

        @pl.when(outside)
        def _():
            panel_out().wait_recv()
            for k in range(1, n_week):
                weight_copy(k).wait_recv()
            pltpu.make_async_copy(weight_ref, wall.at[week], wt_s.at[n_week - 1]).wait()
            for w, op, lag, *_ in ROLES:
                @pl.when(week == w)
                def _(op=op, lag=lag):
                    low_copy(x_ref.at[lag], 1, op, 0, {ROW: pair}).wait_send()
            pivot_out().wait_send()

        for k in range(1, n_week):
            weight_copy(k).wait_send()

        @pl.when(inside)
        def _():
            for w, op, lag, near, across, theirs in ROLES:
                @pl.when(week == w)
                def _(op=op, theirs=theirs):
                    for j in range(2):
                        for i in range(2):
                            low_copy(x_ref.at[0], j, op, i, to_week(0)).wait_send()
                        low_copy(x_ref.at[0], j, theirs, 0, to_week(0)).wait_send()
            for k in range(1, members):
                sum_copy(k).wait_send()
                all_copy(k).wait_send()

            @pl.when(week == 1)
            def _():
                for j, s in enumerate(slabs):
                    high_copy(column(0, s), j, 0, 0, to_week(2)).wait_send()
                    high_copy(column(0, s), j, 0, 1, to_week(0)).wait_send()
                    high_copy(column(1, s), j, 1, 0, to_week(0)).wait_send()

            @pl.when(week == 2)
            def _():
                for j, s in enumerate(slabs):
                    high_copy(column(3, s), j, 1, 0, to_week(3)).wait_send()
                    high_copy(high.at[j, op_rows(0), :], j, 0, 0, to_week(3)).wait_send()

            local_copy(pan.at[0], panel_ref, 0).wait()
            panel_out().wait_send()
            for j in range(2):
                @pl.when((week == 0) | (week == n_week - 1))
                def _(j=j):
                    inner_near(j).wait_send()

                @pl.when(week == 2)
                def _(j=j):
                    inner_far(j, 1).wait_send()

            @pl.when(week == 1)
            def _():
                inner_far(1, 0).wait_send()
                local_copy(inn.at[0], inner_ref.at[0], 1).wait()

        pltpu.make_async_copy(wall, weights_ref, wt_s.at[n_week - 1]).start()
        pltpu.make_async_copy(wall, weights_ref, wt_s.at[n_week - 1]).wait()

    early()
    first("start")
    for u in range(UNITS):
        local(u, lambda w, u=u: take(u, w).start())
    for u in range(UNITS):
        def move(w, u=u):
            take(u, w).wait()
            put(u).start()

        local(u, move)

    def begin(u):
        local(u, lambda w: put(u).wait())
        for _, _, _, to_week, unit in FIRST:
            if unit == u:
                @pl.when(week == to_week)
                def _():
                    remote(place(u, mine), first_s.at[u], first_r.at[u], {ROW: target[0]}).wait_recv()

        def go():
            for k in peers:
                side(u, k).start()
            for d in range(2):
                pl.when(has[d])(lambda d=d: main(u, 0, d).start())
            for k in peers:
                rest(u, k).start()

        active(u, go)
        spread(u, mine)

    for u in range(UNITS):
        begin(u)

    for u in range(UNITS):
        def spread_band(u=u):
            for k in peers:
                side(u, k).wait_recv()
                for d in range(2):
                    pl.when(has[d])(lambda d=d, k=k: strip(u, 0, d, k).start())

        active(u, spread_band)

    @pl.when(inside)
    def _():
        spread_low()
        make_part()

    def across(step):
        for u in range(UNITS):
            if step == 0:
                def body(u=u):
                    for k in peers:
                        rest(u, k).wait_recv()
                        spread(u, slab(row, other(k)))

                active(u, body)
            else:
                for d in range(2):
                    def body(u=u, d=d):
                        for k in peers:
                            onward(u, step, d, k).wait_recv()
                            spread(u, slab(origin(step, d), other(k)))

                    active(u, lambda d=d, body=body: pl.when(arrives(step, d))(body))

    def relays(step, act):
        if step == 0:
            relay(mine, act)
            for k in peers:
                relay(slab(row, other(k)), act)
        else:
            for d in range(2):
                @pl.when(arrives(step, d))
                def _(d=d):
                    relay(slab(origin(step, d), col), act)
                    for k in peers:
                        relay(slab(origin(step, d), other(k)), act)

    for step in range(1, n_row):
        for u in range(UNITS):
            for d in range(2):
                def advance(u=u, d=d, step=step):
                    main(u, step - 1, d).wait_recv()
                    if step < n_row - 1:
                        pl.when(has[d])(lambda: main(u, step, d).start())
                    for k in peers:
                        onward(u, step, d, k).start()
                    spread(u, slab(origin(step, d), col))
                    for k in peers:
                        strip(u, step - 1, d, k).wait_recv()
                        if step < n_row - 1:
                            pl.when(has[d])(lambda k=k: strip(u, step, d, k).start())

                active(u, lambda d=d, step=step, advance=advance: pl.when(arrives(step, d))(advance))
        across(step - 1)
        if step > 1:
            relays(step - 2, "start")
        if step == 1:
            @pl.when(inside)
            def _():
                make_whole()
                start_high()
        if step == n_row - 2:
            pl.when(inside)(make_panel)
        if step == n_row - 1:
            pl.when(inside)(join_inner)
    across(n_row - 1)
    for step in range(max(n_row - 2, 0), n_row):
        relays(step, "start")

    @pl.when((week == 1) | (week == 2))
    def _():
        for s in range(n):
            for flow in range(FLOWS):
                def arrive(s=s, flow=flow):
                    ref = cell(0, 0, s)
                    remote(ref, flow_s.at[0, s], flow_r.at[flow, s], {ROW: target[0]}).wait_recv()

                if flow == 3:
                    pl.when(outside | ((mine != s) & (far != s)))(arrive)
                else:
                    arrive()

    end_inner()
    first("wait")
    for u in range(UNITS):
        def finish(u=u):
            for k in peers:
                side(u, k).wait_send()
                rest(u, k).wait_send()
            for d in range(2):
                @pl.when(has[d])
                def _(d=d):
                    main(u, 0, d).wait_send()
                    for k in peers:
                        strip(u, 0, d, k).wait_send()
                for step in range(1, n_row):
                    @pl.when(arrives(step, d))
                    def _(d=d, step=step):
                        for k in peers:
                            onward(u, step, d, k).wait_send()
                        if step < n_row - 1:
                            @pl.when(has[d])
                            def _():
                                main(u, step, d).wait_send()
                                for k in peers:
                                    strip(u, step, d, k).wait_send()

        active(u, finish)
        if u >= 2:
            for s in range(n):
                spread(u, s, "wait")
    for s in range(n):
        relay(s, "wait")


def gather(x, pivot, weight, collective_id):
    n_row, n_col = lax.axis_size(ROW), lax.axis_size(COL)
    _, length, width = x.shape
    slices = pivot.shape[0]
    n = n_row * n_col
    assert n_row == 4 and lax.axis_size(WEEK) == 4
    kinds = (UNITS, n_row - 1, 2)
    wide = (*kinds, n_col - 1)
    sides = (UNITS, n_col - 1)
    members = 2 * n_col
    vmem = functools.partial(lambda *shape: pltpu.VMEM(shape, x.dtype))
    sent = length * width * 2 * (n - 1) * 9 // 4
    hbm = pl.BlockSpec(memory_space=pl.ANY)
    return pl.pallas_call(
        functools.partial(gather_kernel, n_row, n_col),
        out_shape=(
            jax.ShapeDtypeStruct((5, length, width * n), x.dtype),
            jax.ShapeDtypeStruct((width, slices), x.dtype),
            jax.ShapeDtypeStruct((2, width, 2 * length), x.dtype),
            jax.ShapeDtypeStruct((4, *weight.shape), weight.dtype),
        ),
        in_specs=[hbm] * 3,
        out_specs=(hbm,) * 4,
        scratch_shapes=[
            pltpu.VMEM((UNITS, length // 2, width), x.dtype), DMA((UNITS,)), DMA((UNITS,)), DMA((UNITS,)),
            DMA(kinds), DMA(kinds), DMA(wide), DMA(wide), DMA(sides), DMA(sides), DMA(sides), DMA(sides),
            DMA(wide), DMA(wide), DMA((5, n)), DMA((FLOWS, n)),
            vmem(2, 2 * length, width), vmem(2, slices, width), vmem(2, 2 * length, width),
            vmem(2 * length, slices), vmem(members - 1, 2 * length // members, slices), vmem(2 * length, slices),
            vmem(2, width, 2 * length), vmem(2, width, slices), vmem(2, width, 2 * length),
            vmem(2, width, 2 * length), pltpu.VMEM((4, *weight.shape), weight.dtype),
            DMA((2, 2, 2)), DMA((2, 2)), DMA((1,)), DMA((1,)), DMA((2, 2, 2)), DMA((2, 2)), DMA((6,)),
            DMA((members - 1,)), DMA((members - 1,)), DMA((members - 1,)), DMA((members - 1,)),
            DMA((1,)), DMA((1,)), DMA((2,)), DMA((4,)), DMA((4,)), DMA((3,)),
        ],
        compiler_params=pltpu.CompilerParams(
            collective_id=collective_id, has_side_effects=True, vmem_limit_bytes=60 << 20),
        cost_estimate=pl.CostEstimate(flops=0, bytes_accessed=sent * 8, transcendentals=0),
    )(x, pivot, weight)


PRODUCTS = ((0, 0, 0, (0, 3)), (0, 1, 1, (0, 2)), (0, 2, 2, (0, 1)), (1, 0, 3, (1, 3)), (1, 1, 4, (1, 2)),
            (2, 0, 2, (2, 3)))


def bands_kernel(at_ref, left_ref, weight_ref, prior_ref, full_ref, out_ref, turned):
    week, mine = at_ref[0], at_ref[1]
    tile = pl.program_id(0)
    width = left_ref.shape[2]
    columns = full_ref.shape[2]

    @pl.when(tile == 0)
    def _():
        for p, (_, slot, _, (lo, hi)) in enumerate(PRODUCTS):
            @pl.when((week >= lo) & (week <= hi))
            def _(p=p, slot=slot):
                flat = left_ref[slot].T.astype(jnp.float32) * weight_ref[p][None, :]
                turned[p] = flat.astype(turned.dtype)

    out_ref[...] = jnp.zeros_like(out_ref)
    for p, (band, _, slot, (lo, hi)) in enumerate(PRODUCTS):
        @pl.when((week >= lo) & (week <= hi))
        def _(p=p, band=band, slot=slot):
            out_ref[band] += jnp.dot(turned[p], full_ref[slot], preferred_element_type=jnp.float32)

    row_ids = lax.broadcasted_iota(jnp.int32, (width, columns), 0) + mine * width
    col_ids = lax.broadcasted_iota(jnp.int32, (width, columns), 1) + tile * columns
    out_ref[0] += jnp.where(row_ids == col_ids, prior_ref[:, :1], 0.0)


def bands(at, full, weights, prior):
    slots, length, regions = full.shape
    width = prior.shape[0]
    columns = min(512, regions)
    return pl.pallas_call(
        bands_kernel,
        out_shape=jax.ShapeDtypeStruct((3, width, regions), jnp.float32),
        grid_spec=pltpu.PrefetchScalarGridSpec(
            num_scalar_prefetch=1,
            grid=(regions // columns,),
            in_specs=[
                pl.BlockSpec((3, length, width), lambda j, at: (0, 0, at[1]), pipeline_mode=pl.Buffered(1)),
                pl.BlockSpec(weights.shape, lambda j, at: (0, 0)),
                pl.BlockSpec(prior.shape, lambda j, at: (0, 0)),
                pl.BlockSpec((slots, length, columns), lambda j, at: (0, 0, j)),
            ],
            out_specs=pl.BlockSpec((3, width, columns), lambda j, at: (0, 0, j)),
            scratch_shapes=[pltpu.VMEM((len(PRODUCTS), width, length), full.dtype)],
        ),
        compiler_params=pltpu.CompilerParams(dimension_semantics=("arbitrary",), vmem_limit_bytes=60 << 20),
        cost_estimate=pl.CostEstimate(
            flops=10 * width * length * regions, bytes_accessed=full.size * 2 + 12 * width * regions,
            transcendentals=0),
    )(at, full, weights, prior, full)


def schur_kernel(at_ref, left_ref, weight_ref, prior_ref, inner_ref, full_ref, out_ref, turned):
    week, mine = at_ref[0], at_ref[1]
    tile = pl.program_id(0)
    slots, length, width = left_ref.shape
    columns = full_ref.shape[2]

    @pl.when(week == 1)
    def _():
        @pl.when(tile == 0)
        def _():
            for k in range(slots):
                flat = left_ref[k].T.astype(jnp.float32) * weight_ref[k][None, :]
                if k < 2:
                    at = pl.ds(k * length, length)
                    inner = inner_ref[0, :, at].astype(jnp.float32) + inner_ref[1, :, at].astype(jnp.float32)
                    flat = flat - inner * weight_ref[3 + k][None, :]
                turned[k] = flat.astype(turned.dtype)

        total = jnp.dot(turned[0], full_ref[0], preferred_element_type=jnp.float32)
        for k in range(1, slots):
            total = total + jnp.dot(turned[k], full_ref[k], preferred_element_type=jnp.float32)
        row_ids = lax.broadcasted_iota(jnp.int32, (width, columns), 0) + mine * width
        col_ids = lax.broadcasted_iota(jnp.int32, (width, columns), 1) + tile * columns
        total = total + jnp.where(row_ids == col_ids, prior_ref[:, :1], 0.0)
        out_ref[...] = total.astype(out_ref.dtype)


def schur_rows(at, full, weights, prior, inner):
    _, length, regions = full.shape
    width = prior.shape[0]
    columns = min(512, regions)
    whole = pl.Buffered(1)
    return pl.pallas_call(
        schur_kernel,
        out_shape=jax.ShapeDtypeStruct((width, regions), jnp.bfloat16),
        grid_spec=pltpu.PrefetchScalarGridSpec(
            num_scalar_prefetch=1,
            grid=(regions // columns,),
            in_specs=[
                pl.BlockSpec((3, length, width), lambda j, at: (0, 0, at[1]), pipeline_mode=whole),
                pl.BlockSpec(weights.shape, lambda j, at: (0, 0)),
                pl.BlockSpec(prior.shape, lambda j, at: (0, 0)),
                pl.BlockSpec(inner.shape, lambda j, at: (0, 0, 0), pipeline_mode=whole),
                pl.BlockSpec((3, length, columns), lambda j, at: (0, 0, jnp.where(at[0] == 1, j, 0))),
            ],
            out_specs=pl.BlockSpec((width, columns), lambda j, at: (0, j)),
            scratch_shapes=[pltpu.VMEM((3, width, length), full.dtype)],
        ),
        compiler_params=pltpu.CompilerParams(dimension_semantics=("arbitrary",), vmem_limit_bytes=60 << 20),
        cost_estimate=pl.CostEstimate(
            flops=6 * width * length * regions, bytes_accessed=6 * length * regions, transcendentals=0),
    )(at, full, weights, prior, inner, full)


def body(sensitivity, reach, obs_weight, prior_precision, pivot_solve):
    week = lax.axis_index(WEEK)
    n_week, n_col = lax.axis_size(WEEK), lax.axis_size(COL)
    local = sensitivity[0]
    lags, length, width = local.shape
    mine = lax.axis_index(ROW) * n_col + lax.axis_index(COL)

    lag = jnp.arange(8)[:, None]
    own_weight = jnp.where((reach >= lag) & (week >= lag) & (lag < lags), obs_weight, 0.0)
    full, panel, inner, by_week = gather(local, pivot_solve, own_weight, 0)
    by_week = by_week[:, :lags]
    later = jnp.concatenate([by_week, jnp.zeros((lags, lags, length), by_week.dtype)])
    here = lax.dynamic_slice(later, (week, 0, 0), (lags, lags, length))
    weights = jnp.stack([here[0, 0], here[1, 1], here[2, 2], here[0, 1], here[1, 2], here[0, 2]])

    at = jnp.stack([week, mine]).astype(jnp.int32)
    prior = jnp.broadcast_to(prior_precision[0][:, None], (width, 128))
    out = schur_rows(at, full, weights, prior, inner)
    quarter = out.shape[1] // n_week
    schur = out[:, quarter : 2 * quarter]
    moved = [(w, lax.ppermute(out[:, w * quarter : (w + 1) * quarter], WEEK, [(1, w)])) for w in (2, 3, 0)]
    h = bands(at, full, weights, prior)
    for w, block in moved:
        schur = jnp.where(week == w, block, schur)
    return (h[None], panel, schur.astype(jnp.float32))


def solution(mesh):
    placed = (
        P(WEEK, None, None, (ROW, COL)),
        P(WEEK, None),
        P(WEEK, None),
        P(WEEK, (ROW, COL)),
        P(WEEK, (ROW, COL)),
    )
    return jax.shard_map(
        body,
        mesh=mesh,
        in_specs=placed,
        out_specs=(
            P(WEEK, None, (ROW, COL), None),
            P((ROW, COL), WEEK),
            P((ROW, COL), WEEK),
        ),
        check_vma=False,
    )
```

```python
import functools

import jax
import jax.numpy as jnp
from jax import lax
from jax.experimental import pallas as pl
from jax.experimental.pallas import tpu as pltpu
from jax.sharding import PartitionSpec as P

ROW, COL, WEEK = "row", "col", "week"
DMA = pltpu.SemaphoreType.DMA

UNITS = 5
UNIT_SLOT = ((0, 0, 0, 0), (0, 0, 0, 0), (1, 1, 3, 3), (1, 2, 2, 3), (2, 0, 0, 2))
UNIT_HALF = ((0, 0, 0, 0), (1, 1, 1, 1), (0, 0, 1, 0), (1, 0, 1, 1), (0, 0, 0, 1))
LOCAL = {
    0: ((0, 0),) * 4,
    1: ((0, 1),) * 4,
    2: (None, None, (1, 1), (1, 0)),
    3: (None, None, (2, 1), (1, 1)),
    4: (None, None, None, (2, 1)),
}
FIRST = ((1, 1, 0, 0, 2), (1, 1, 1, 0, 3), (2, 2, 0, 0, 4), (2, 1, 0, 1, 2), (3, 2, 0, 1, 3))
ONWARD = (
    ((2, 1, 3, 0), (3, 1, 3, 1), (4, 1, 4, 2), (4, 2, 2, 4)),
    ((2, 2, 3, 3), (3, 3, 2, 0)),
    ((2, 1, 1, 3), (3, 0, 2, 0)),
    ((2, 2, 1, 0), (3, 2, 1, 1), (4, 2, 4, 2), (4, 1, 2, 4)),
)
RELAY = {0: (1, 1, 4), 3: (0, 2, 4)}
FLOWS = 6


def pick(week, values):
    out = jnp.int32(values[0])
    for k, value in enumerate(values[1:], 1):
        out = jnp.where(week == k, jnp.int32(value), out)
    return out


def contract_last(left, right):
    return lax.dot_general(left, right, (((1,), (1,)), ((), ())), preferred_element_type=jnp.float32)


def gather_kernel(n_row, n_col, x_ref, pivot_ref, weight_ref, f_ref, panel_ref, inner_ref, weights_ref,
                  own, put_sem, first_s, first_r, z_s, z_r, pair_s, cross_s, cross_r, y_s, y_r, flow_s, flow_r,
                  low, piv, high, part, came_z, came_y, whole, turned, pan, inn, inn_in, wall,
                  low_s, low_r, piv_s, piv_r, high_s, high_r, loc, half_s, half_r, sum_s, sum_r,
                  all_s, all_r, back_s, back_r, pan_s, pan_r, inn_s, inn_r, wt_s, wt_r):
    row, col, week = lax.axis_index(ROW), lax.axis_index(COL), lax.axis_index(WEEK)
    _, length, width = x_ref.shape
    half = length // 2
    n = n_row * n_col
    peers = range(1, n_col)
    n_week = 4
    pair = row + 1 - 2 * lax.rem(row, 2)
    opp = jnp.where(row < 2, 2, 1)
    end = jnp.where(row < 2, 3, 0)
    inside = (row == 1) | (row == 2)
    outside = (row == 0) | (row == 3)
    middle = (week == 1) | (week == 2)
    edge = (week == 0) | (week == n_week - 1)

    barrier = pltpu.get_barrier_semaphore()
    for k in (1, n_row - 1):
        pl.semaphore_signal(barrier, inc=1, device_id={ROW: lax.rem(row + k, n_row)})
    for k in peers:
        pl.semaphore_signal(barrier, inc=1, device_id={COL: lax.rem(col + k, n_col)})
    for k in range(1, n_week):
        pl.semaphore_signal(barrier, inc=1, device_id={WEEK: lax.rem(week + k, n_week)})
    pl.semaphore_signal(barrier, inc=1, device_id={WEEK: n_week - 1 - week, ROW: pair})
    pl.semaphore_wait(barrier, 2 + (n_col - 1) + (n_week - 1) + 1)

    slots = [pick(week, UNIT_SLOT[u]) for u in range(UNITS)]
    starts = [pl.multiple_of(pick(week, UNIT_HALF[u]) * half, half) for u in range(UNITS)]

    def slab(at_row, at_col):
        return at_row * n_col + at_col

    mine, far = slab(row, col), slab(pair, col)

    def cell(slot, start, s):
        at = pl.ds(pl.multiple_of(s * width, width), width)
        return f_ref.at[slot, pl.ds(start, half), at]

    def place(u, s):
        return cell(slots[u], starts[u], s)

    def active(u, body):
        if u < 4:
            body()
        else:
            pl.when(edge)(body)

    def other(k):
        return lax.rem(col + n_col - k, n_col)

    def remote(ref, s_sem, r_sem, device, to=None):
        return pltpu.make_async_remote_copy(ref, ref if to is None else to, s_sem, r_sem, device_id=device)

    def to_pair(u, s, hop):
        return remote(place(u, s), pair_s.at[u, hop], z_r.at[u, hop], {ROW: pair})

    def to_opp(u, s, hop):
        return remote(place(u, s), z_s.at[u, hop], z_r.at[u, hop], {ROW: opp})

    def cross(u, k):
        return remote(place(u, slab(row, other(k))), cross_s.at[u, k - 1], cross_r.at[u, k - 1], {ROW: pair})

    def side(u, s, hop, k):
        return remote(place(u, s), y_s.at[u, hop, k - 1], y_r.at[u, hop, k - 1], {COL: lax.rem(col + k, n_col)})

    def aside(u, s, hop):
        for k in peers:
            side(u, s, hop, k).start()

    def flows(w, u, s):
        for i, (unit, to_week, to_slot, flow) in enumerate(ONWARD[w]):
            if unit == u:
                start = UNIT_HALF[u][w] * half
                yield remote(cell(UNIT_SLOT[u][w], start, s), flow_s.at[i, s], flow_r.at[flow, s],
                             {WEEK: jnp.int32(to_week)}, cell(to_slot, start, s))

    def spread(u, s, act="start"):
        for w in range(n_week):
            if any(unit == u for unit, *_ in ONWARD[w]):
                @pl.when(week == w)
                def _(w=w):
                    for copy in flows(w, u, s):
                        copy.start() if act == "start" else copy.wait_send()

    def relay(s, act="start"):
        for w, (h, to_week, to_slot) in RELAY.items():
            @pl.when(week == w)
            def _(w=w, h=h, to_week=to_week, to_slot=to_slot):
                ref = cell(2, h * half, s)
                copy = remote(ref, flow_s.at[4, s], flow_r.at[5, s], {WEEK: jnp.int32(to_week)},
                              cell(to_slot, h * half, s))
                if act == "start":
                    remote(ref, flow_s.at[0, s], flow_r.at[0, s], {WEEK: jnp.int32(to_week)}).wait_recv()
                    copy.start()
                else:
                    copy.wait_send()

    def relays(at_row):
        relay(slab(at_row, col))
        for k in peers:
            relay(slab(at_row, other(k)))

    def first(act):
        for w, lag, h, to_week, u in FIRST:
            @pl.when(week == w)
            def _(lag=lag, h=h, to_week=to_week, u=u):
                copy = remote(x_ref.at[lag, pl.ds(h * half, half), :], first_s.at[u], first_r.at[u],
                              {WEEK: jnp.int32(to_week)}, cell(UNIT_SLOT[u][to_week], h * half, mine))
                copy.start() if act == "start" else copy.wait_send()

    def take(u, w):
        lag, h = LOCAL[u][w]
        return pltpu.make_async_copy(x_ref.at[lag, pl.ds(h * half, half), :], own.at[u], put_sem.at[u])

    def put(u):
        return pltpu.make_async_copy(own.at[u], place(u, mine), put_sem.at[u])

    def local(u, body):
        weeks = [w for w in range(n_week) if LOCAL[u][w] is not None]
        if len({LOCAL[u][w] for w in weeks}) == 1 and len(weeks) == n_week:
            body(weeks[0])
        else:
            for w in weeks:
                pl.when(week == w)(functools.partial(body, w))

    slabs = (mine, far)
    side_of = jnp.where(row == 2, 1, 0)
    members = 2 * n_col
    chunk = 2 * length // members
    slices = pivot_ref.shape[0]

    def op_rows(op):
        return pl.ds(op * length, length)

    def low_copy(src, j, op, i, device):
        return remote(src, low_s.at[j, op, i], low_r.at[j, op], device, low.at[j, op_rows(op), :])

    def high_copy(src, j, op, i, device):
        return remote(src, high_s.at[j, op, i], high_r.at[j, op], device, high.at[j, op_rows(op), :])

    def to_week(w):
        return {WEEK: jnp.int32(w)}

    def pivot_out():
        return remote(pivot_ref, piv_s.at[0], piv_r.at[0], {ROW: pair}, piv.at[1])

    def local_copy(src, dst, i):
        return pltpu.make_async_copy(src, dst, loc.at[i])

    def weight_copy(k):
        return remote(weight_ref, wt_s.at[k - 1], wt_r.at[k - 1], {WEEK: lax.rem(week + k, n_week)}, wall.at[week])

    ROLES = ((1, 0, 1, 0, 2, 1), (2, 1, 2, 3, 1, 0))

    def by_role(body):
        for w, *role in ROLES:
            pl.when(week == w)(functools.partial(body, *role))

    def early():
        for k in range(1, n_week):
            weight_copy(k).start()
        pltpu.make_async_copy(weight_ref, wall.at[week], wt_s.at[n_week - 1]).start()

        @pl.when(outside)
        def _():
            by_role(lambda op, lag, *_: low_copy(x_ref.at[lag], 1, op, 0, {ROW: pair}).start())
            pivot_out().start()

        @pl.when(inside)
        def _():
            local_copy(pivot_ref, piv.at[0], 0).start()

            def send(op, lag, near, across, _):
                low_copy(x_ref.at[lag], 0, op, 0, to_week(across)).start()
                low_copy(x_ref.at[lag], 0, op, 1, to_week(near)).start()
                local_copy(x_ref.at[lag], low.at[0, op_rows(op), :], 1).start()

            by_role(send)

    def spread_low():
        def send(op, lag, near, across, theirs):
            ref = low.at[1, op_rows(op), :]
            low_copy(ref, 1, op, 0, to_week(across)).wait_recv()
            low_copy(ref, 1, op, 0, to_week(across)).start()
            low_copy(ref, 1, op, 1, to_week(near)).start()
            for j in range(2):
                ref = low.at[j, op_rows(theirs), :]
                low_copy(ref, j, theirs, 0, to_week(near)).wait_recv()
                low_copy(ref, j, theirs, 0, to_week(near)).start()
            local_copy(x_ref.at[lag], low.at[0, op_rows(op), :], 1).wait()

        by_role(send)

        @pl.when(edge)
        def _():
            for j in range(2):
                for op in range(2):
                    low_copy(low.at[j, op_rows(op), :], j, op, 0, to_week(1)).wait_recv()

        pivot_out().wait_recv()
        local_copy(pivot_ref, piv.at[0], 0).wait()

    def rows_of(m, count=1):
        return pl.ds(pl.multiple_of(m * chunk, chunk), count * chunk)

    def half_copy():
        away = rows_of((1 - side_of) * n_col, n_col)
        return remote(part.at[away, :], half_s.at[0], half_r.at[0], {ROW: opp}, came_z)

    def sum_copy(k):
        to = lax.rem(col + k, n_col)
        return remote(part.at[rows_of(side_of * n_col + to), :], sum_s.at[k - 1], sum_r.at[k - 1], {COL: to},
                      came_y.at[k - 1])

    me = side_of * n_col + col

    def all_copy(k):
        return remote(whole.at[rows_of(me), :], all_s.at[k - 1], all_r.at[k - 1], {COL: lax.rem(col + k, n_col)})

    def back_copy(k):
        ref = whole.at[rows_of(side_of * n_col + other(k)), :]
        return remote(ref, back_s.at[k], back_r.at[k], {ROW: opp})

    def make_part():
        def fill(m):
            at = rows_of(m)
            total = contract_last(low[0, at, :], piv[0]) + contract_last(low[1, at, :], piv[1])
            part[at, :] = total.astype(part.dtype)

        @pl.loop(0, n_col)
        def _(m):
            fill((1 - side_of) * n_col + m)

        half_copy().start()

        @pl.loop(0, n_col)
        def _(m):
            fill(side_of * n_col + m)

    def add_half():
        half_copy().wait_recv()

        @pl.loop(0, n_col)
        def _(m):
            at, here = rows_of(side_of * n_col + m), rows_of(m)
            total = part[at, :].astype(jnp.float32) + came_z[here, :].astype(jnp.float32)
            part[at, :] = total.astype(part.dtype)

        for k in peers:
            sum_copy(k).start()

    def make_whole():
        for k in peers:
            sum_copy(k).wait_recv()
        total = part[rows_of(me), :].astype(jnp.float32)
        for k in peers:
            total = total + came_y[k - 1].astype(jnp.float32)
        whole[rows_of(me), :] = total.astype(whole.dtype)
        back_copy(0).start()
        for k in peers:
            all_copy(k).start()

    def pass_whole():
        for k in peers:
            all_copy(k).wait_recv()
            back_copy(k).start()

    def column(slot, s):
        return f_ref.at[slot, :, pl.ds(pl.multiple_of(s * width, width), width)]

    def start_high():
        @pl.when(middle)
        def _():
            for s in slabs:
                ref = cell(0, 0, s)
                remote(ref, flow_s.at[0, s], flow_r.at[3, s], {ROW: pair}).wait_recv()

        @pl.when(week == 1)
        def _():
            for j, s in enumerate(slabs):
                high_copy(column(0, s), j, 0, 0, to_week(2)).start()
                high_copy(column(0, s), j, 0, 1, to_week(0)).start()
                high_copy(column(1, s), j, 1, 0, to_week(0)).start()
                local_copy(column(0, s), high.at[j, op_rows(0), :], 2 + j).start()
                local_copy(column(1, s), high.at[j, op_rows(1), :], 4 + j).start()

        @pl.when(week == 2)
        def _():
            for j, s in enumerate(slabs):
                high_copy(column(3, s), j, 1, 0, to_week(3)).start()
                local_copy(column(3, s), high.at[j, op_rows(1), :], 4 + j).start()

    def wait_high():
        for j, s in enumerate(slabs):
            @pl.when(week == 1)
            def _(j=j, s=s):
                local_copy(column(0, s), high.at[j, op_rows(0), :], 2 + j).wait()

            @pl.when(week != 1)
            def _(j=j):
                high_copy(high.at[j, op_rows(0), :], j, 0, 0, to_week(3)).wait_recv()

            @pl.when(week == 2)
            def _(j=j):
                high_copy(high.at[j, op_rows(0), :], j, 0, 0, to_week(3)).start()

            @pl.when(middle)
            def _(j=j, s=s):
                local_copy(column(1, s), high.at[j, op_rows(1), :], 4 + j).wait()

            @pl.when(edge)
            def _(j=j):
                high_copy(high.at[j, op_rows(1), :], j, 1, 0, to_week(3)).wait_recv()

    def panel_out():
        return remote(pan.at[1], pan_s.at[0], pan_r.at[0], {ROW: pair}, panel_ref)

    def inner_near(j):
        return remote(inn.at[j], inn_s.at[j], inn_r.at[j], {WEEK: jnp.where(week == 0, 1, 2)}, inn_in.at[j])

    def inner_far(j, i):
        device = {WEEK: jnp.int32(1)} if j == 0 else {WEEK: jnp.int32(1), ROW: pair}
        return remote(inn.at[j], inn_s.at[j], inn_r.at[2 + i], device, inner_ref.at[i])

    def own_weight():
        return pltpu.make_async_copy(weight_ref, wall.at[week], wt_s.at[n_week - 1])

    def turn_high():
        wait_high()
        for k in range(1, n_week):
            weight_copy(k).wait_recv()
        own_weight().wait()
        step = min(length, 512)
        for j in range(2):
            for op in range(2):
                for at in range(0, length, step):
                    rows = pl.ds(op * length + at, step)
                    flat = high[j, rows, :].T.astype(jnp.float32) * wall[1 + op, 1 + op, pl.ds(at, step)][None, :]
                    turned[j, :, rows] = flat.astype(turned.dtype)

    tile = min(slices, 256)

    def wait_whole():
        for k in range(n_col):
            back_copy(k).wait_recv()

    def make_panel(j):
        @pl.loop(0, slices // tile)
        def _(i):
            at = pl.ds(pl.multiple_of(i * tile, tile), tile)
            pan[j, :, at] = jnp.dot(turned[j], whole[:, at], preferred_element_type=jnp.float32).astype(pan.dtype)

        if j == 0:
            local_copy(pan.at[0], panel_ref, 0).start()
        else:
            panel_out().start()

    def make_inner(j):
        @pl.loop(0, 2 * length // tile)
        def _(i):
            at = pl.ds(pl.multiple_of(i * tile, tile), tile)
            inn[j, :, at] = contract_last(pan[j], whole[at, :]).astype(inn.dtype)

        pl.when(edge)(lambda: inner_near(j).start())

    def join_inner(j):
        @pl.when(middle)
        def _():
            inner_near(j).wait_recv()
            inn[j] = (inn[j].astype(jnp.float32) + inn_in[j].astype(jnp.float32)).astype(inn.dtype)
            pl.when(week == 2)(lambda: inner_far(j, 1).start())

            @pl.when(week == 1)
            def _():
                if j == 1:
                    inner_far(1, 0).start()
                else:
                    local_copy(inn.at[0], inner_ref.at[0], 1).start()

    first("start")
    for u in range(UNITS):
        local(u, lambda w, u=u: take(u, w).start())
    early()
    for u in range(UNITS):
        def move(w, u=u):
            take(u, w).wait()
            put(u).start()

        local(u, move)

    for u in range(UNITS):
        local(u, lambda w, u=u: put(u).wait())
        for _, _, _, week_of, unit in FIRST:
            if unit == u:
                @pl.when(week == week_of)
                def _(u=u):
                    remote(place(u, mine), first_s.at[u], first_r.at[u], {ROW: pair}).wait_recv()

        def begin(u=u):
            @pl.when(inside)
            def _():
                to_opp(u, mine, 0).start()
                to_pair(u, mine, 0).start()

            pl.when(outside)(lambda: to_pair(u, mine, 1).start())
            aside(u, mine, 0)

        active(u, begin)
        spread(u, mine)

    def from_side(u, at_row, hop, onward=None):
        def body():
            for k in peers:
                side(u, mine, hop, k).wait_recv()
                if onward is not None:
                    onward(k)
                spread(u, slab(at_row, other(k)))

        active(u, body)

    def arrived(u, s, hop, then):
        def body():
            to_pair(u, s, hop).wait_recv()
            then()
            spread(u, s)

        active(u, body)

    @pl.when(outside)
    def _():
        for u in range(UNITS):
            from_side(u, row, 0, lambda k, u=u: cross(u, k).start())
        for hop, at_row in enumerate((pair, opp, end)):
            s = slab(at_row, col)
            for u in range(UNITS):
                arrived(u, s, hop, lambda u=u, s=s, hop=hop: aside(u, s, hop + 1))
                if hop:
                    from_side(u, (pair, opp)[hop - 1], hop)
            if hop:
                relays((row, pair)[hop - 1])
        for u in range(UNITS):
            from_side(u, end, 3)
        relays(opp)
        relays(end)

    @pl.when(inside)
    def _():
        def cross_in(u):
            def body():
                for k in peers:
                    cross(u, k).wait_recv()
                    spread(u, slab(pair, other(k)))

            active(u, body)

        def near_one(u):
            s = slab(opp, col)

            def then():
                to_pair(u, s, 1).start()
                aside(u, s, 1)

            arrived(u, s, 0, then)

        def far_one(u):
            s = slab(end, col)

            def then():
                to_pair(u, s, 2).start()
                aside(u, s, 2)

            arrived(u, s, 2, then)

        for u in range(UNITS):
            near_one(u)
        spread_low()
        make_part()
        for u in range(UNITS):
            arrived(u, far, 1, lambda u=u: to_opp(u, far, 2).start())
            from_side(u, row, 0)
            if u == 2:
                add_half()
        make_whole()
        start_high()
        for u in range(UNITS):
            far_one(u)
            if u == 0:
                pass_whole()
            if u == 1:
                turn_high()
            if u == 2:
                wait_whole()
                make_panel(1)
                make_panel(0)
        make_inner(1)
        make_inner(0)
        for u in range(UNITS):
            cross_in(u)
            from_side(u, opp, 1)
        for j in (1, 0):
            join_inner(j)
        relays(row)
        relays(pair)
        for u in range(UNITS):
            from_side(u, end, 2)
        relays(opp)
        relays(end)

    @pl.when(middle)
    def _():
        for s in range(n):
            for flow in range(FLOWS):
                def arrive(s=s, flow=flow):
                    ref = cell(0, 0, s)
                    remote(ref, flow_s.at[0, s], flow_r.at[flow, s], {ROW: pair}).wait_recv()

                if flow == 3:
                    pl.when(outside | ((mine != s) & (far != s)))(arrive)
                else:
                    arrive()

    @pl.when(week == 1)
    def _():
        inner_far(1, 1).wait_recv()
        pl.when(outside)(lambda: inner_far(1, 0).wait_recv())

    @pl.when(outside)
    def _():
        panel_out().wait_recv()
        for k in range(1, n_week):
            weight_copy(k).wait_recv()
        own_weight().wait()
        by_role(lambda op, lag, *_: low_copy(x_ref.at[lag], 1, op, 0, {ROW: pair}).wait_send())
        pivot_out().wait_send()

    weights_out = pltpu.make_async_copy(wall, weights_ref, wt_s.at[n_week - 1])
    weights_out.start()
    for k in range(1, n_week):
        weight_copy(k).wait_send()

    @pl.when(inside)
    def _():
        def sent(op, lag, near, across, theirs):
            for j in range(2):
                for i in range(2):
                    low_copy(x_ref.at[0], j, op, i, to_week(0)).wait_send()
                low_copy(x_ref.at[0], j, theirs, 0, to_week(0)).wait_send()

        by_role(sent)
        half_copy().wait_send()
        for k in peers:
            sum_copy(k).wait_send()
            all_copy(k).wait_send()
        for k in range(n_col):
            back_copy(k).wait_send()

        @pl.when(week == 1)
        def _():
            for j, s in enumerate(slabs):
                high_copy(column(0, s), j, 0, 0, to_week(2)).wait_send()
                high_copy(column(0, s), j, 0, 1, to_week(0)).wait_send()
                high_copy(column(1, s), j, 1, 0, to_week(0)).wait_send()

        @pl.when(week == 2)
        def _():
            for j, s in enumerate(slabs):
                high_copy(column(3, s), j, 1, 0, to_week(3)).wait_send()
                high_copy(high.at[j, op_rows(0), :], j, 0, 0, to_week(3)).wait_send()

        local_copy(pan.at[0], panel_ref, 0).wait()
        panel_out().wait_send()
        for j in range(2):
            pl.when(edge)(lambda j=j: inner_near(j).wait_send())
            pl.when(week == 2)(lambda j=j: inner_far(j, 1).wait_send())

        @pl.when(week == 1)
        def _():
            inner_far(1, 0).wait_send()
            local_copy(inn.at[0], inner_ref.at[0], 1).wait()

    first("wait")
    for u in range(UNITS):
        def finish(u=u):
            for k in peers:
                for hop in range(3):
                    side(u, mine, hop, k).wait_send()

            @pl.when(outside)
            def _():
                to_pair(u, mine, 1).wait_send()
                for k in peers:
                    side(u, mine, 3, k).wait_send()
                    cross(u, k).wait_send()

            @pl.when(inside)
            def _():
                to_opp(u, mine, 0).wait_send()
                to_opp(u, far, 2).wait_send()
                for hop in range(3):
                    to_pair(u, mine, hop).wait_send()

        active(u, finish)
        if u >= 2:
            for s in range(n):
                spread(u, s, "wait")
    for s in range(n):
        relay(s, "wait")
    weights_out.wait()


def gather(x, pivot, weight, collective_id):
    n_row, n_col = lax.axis_size(ROW), lax.axis_size(COL)
    _, length, width = x.shape
    slices = pivot.shape[0]
    n = n_row * n_col
    assert n_row == 4 and lax.axis_size(WEEK) == 4
    sides = (UNITS, n_col - 1)
    vmem = functools.partial(lambda *shape: pltpu.VMEM(shape, x.dtype))
    sent = length * width * 2 * (n - 1) * 9 // 4
    hbm = pl.BlockSpec(memory_space=pl.ANY)
    return pl.pallas_call(
        functools.partial(gather_kernel, n_row, n_col),
        out_shape=(
            jax.ShapeDtypeStruct((5, length, width * n), x.dtype),
            jax.ShapeDtypeStruct((width, slices), x.dtype),
            jax.ShapeDtypeStruct((2, width, 2 * length), x.dtype),
            jax.ShapeDtypeStruct((4, *weight.shape), weight.dtype),
        ),
        in_specs=[hbm] * 3,
        out_specs=(hbm,) * 4,
        scratch_shapes=[
            pltpu.VMEM((UNITS, length // 2, width), x.dtype), DMA((UNITS,)), DMA((UNITS,)), DMA((UNITS,)),
            DMA((UNITS, 3)), DMA((UNITS, 3)), DMA((UNITS, 3)), DMA(sides), DMA(sides),
            DMA((UNITS, 4, n_col - 1)), DMA((UNITS, 4, n_col - 1)), DMA((5, n)), DMA((FLOWS, n)),
            vmem(2, 2 * length, width), vmem(2, slices, width), vmem(2, 2 * length, width),
            vmem(2 * length, slices), vmem(length, slices), vmem(n_col - 1, length // n_col, slices),
            vmem(2 * length, slices),
            vmem(2, width, 2 * length), vmem(2, width, slices), vmem(2, width, 2 * length),
            vmem(2, width, 2 * length), pltpu.VMEM((4, *weight.shape), weight.dtype),
            DMA((2, 2, 2)), DMA((2, 2)), DMA((1,)), DMA((1,)), DMA((2, 2, 2)), DMA((2, 2)), DMA((6,)),
            DMA((1,)), DMA((1,)), DMA((n_col - 1,)), DMA((n_col - 1,)),
            DMA((n_col - 1,)), DMA((n_col - 1,)), DMA((n_col,)), DMA((n_col,)),
            DMA((1,)), DMA((1,)), DMA((2,)), DMA((4,)), DMA((4,)), DMA((3,)),
        ],
        compiler_params=pltpu.CompilerParams(
            collective_id=collective_id, has_side_effects=True, vmem_limit_bytes=60 << 20),
        cost_estimate=pl.CostEstimate(flops=0, bytes_accessed=sent * 8, transcendentals=0),
    )(x, pivot, weight)


PRODUCTS = ((0, 0, 0, (0, 3)), (0, 1, 1, (0, 2)), (0, 2, 2, (0, 1)), (1, 0, 3, (1, 3)), (1, 1, 4, (1, 2)),
            (2, 0, 2, (2, 3)))


def bands_kernel(at_ref, left_ref, weight_ref, prior_ref, full_ref, out_ref, turned):
    week, mine = at_ref[0], at_ref[1]
    tile = pl.program_id(0)
    width = left_ref.shape[2]
    columns = full_ref.shape[2]

    @pl.when(tile == 0)
    def _():
        for p, (_, slot, _, (lo, hi)) in enumerate(PRODUCTS):
            @pl.when((week >= lo) & (week <= hi))
            def _(p=p, slot=slot):
                flat = left_ref[slot].T.astype(jnp.float32) * weight_ref[p][None, :]
                turned[p] = flat.astype(turned.dtype)

    out_ref[...] = jnp.zeros_like(out_ref)
    for p, (band, _, slot, (lo, hi)) in enumerate(PRODUCTS):
        @pl.when((week >= lo) & (week <= hi))
        def _(p=p, band=band, slot=slot):
            out_ref[band] += jnp.dot(turned[p], full_ref[slot], preferred_element_type=jnp.float32)

    row_ids = lax.broadcasted_iota(jnp.int32, (width, columns), 0) + mine * width
    col_ids = lax.broadcasted_iota(jnp.int32, (width, columns), 1) + tile * columns
    out_ref[0] += jnp.where(row_ids == col_ids, prior_ref[:, :1], 0.0)


def bands(at, full, weights, prior):
    slots, length, regions = full.shape
    width = prior.shape[0]
    columns = min(512, regions)
    return pl.pallas_call(
        bands_kernel,
        out_shape=jax.ShapeDtypeStruct((3, width, regions), jnp.float32),
        grid_spec=pltpu.PrefetchScalarGridSpec(
            num_scalar_prefetch=1,
            grid=(regions // columns,),
            in_specs=[
                pl.BlockSpec((3, length, width), lambda j, at: (0, 0, at[1]), pipeline_mode=pl.Buffered(1)),
                pl.BlockSpec(weights.shape, lambda j, at: (0, 0)),
                pl.BlockSpec(prior.shape, lambda j, at: (0, 0)),
                pl.BlockSpec((slots, length, columns), lambda j, at: (0, 0, j)),
            ],
            out_specs=pl.BlockSpec((3, width, columns), lambda j, at: (0, 0, j)),
            scratch_shapes=[pltpu.VMEM((len(PRODUCTS), width, length), full.dtype)],
        ),
        compiler_params=pltpu.CompilerParams(dimension_semantics=("arbitrary",), vmem_limit_bytes=60 << 20),
        cost_estimate=pl.CostEstimate(
            flops=10 * width * length * regions, bytes_accessed=full.size * 2 + 12 * width * regions,
            transcendentals=0),
    )(at, full, weights, prior, full)


def schur_kernel(at_ref, left_ref, weight_ref, prior_ref, inner_ref, full_ref, out_ref, turned):
    week, mine = at_ref[0], at_ref[1]
    tile = pl.program_id(0)
    slots, length, width = left_ref.shape
    columns = full_ref.shape[2]

    @pl.when(week == 1)
    def _():
        @pl.when(tile == 0)
        def _():
            for k in range(slots):
                flat = left_ref[k].T.astype(jnp.float32) * weight_ref[k][None, :]
                if k < 2:
                    at = pl.ds(k * length, length)
                    inner = inner_ref[0, :, at].astype(jnp.float32) + inner_ref[1, :, at].astype(jnp.float32)
                    flat = flat - inner * weight_ref[3 + k][None, :]
                turned[k] = flat.astype(turned.dtype)

        total = jnp.dot(turned[0], full_ref[0], preferred_element_type=jnp.float32)
        for k in range(1, slots):
            total = total + jnp.dot(turned[k], full_ref[k], preferred_element_type=jnp.float32)
        row_ids = lax.broadcasted_iota(jnp.int32, (width, columns), 0) + mine * width
        col_ids = lax.broadcasted_iota(jnp.int32, (width, columns), 1) + tile * columns
        total = total + jnp.where(row_ids == col_ids, prior_ref[:, :1], 0.0)
        out_ref[...] = total.astype(out_ref.dtype)


def schur_rows(at, full, weights, prior, inner):
    _, length, regions = full.shape
    width = prior.shape[0]
    columns = min(512, regions)
    whole = pl.Buffered(1)
    return pl.pallas_call(
        schur_kernel,
        out_shape=jax.ShapeDtypeStruct((width, regions), jnp.bfloat16),
        grid_spec=pltpu.PrefetchScalarGridSpec(
            num_scalar_prefetch=1,
            grid=(regions // columns,),
            in_specs=[
                pl.BlockSpec((3, length, width), lambda j, at: (0, 0, at[1]), pipeline_mode=whole),
                pl.BlockSpec(weights.shape, lambda j, at: (0, 0)),
                pl.BlockSpec(prior.shape, lambda j, at: (0, 0)),
                pl.BlockSpec(inner.shape, lambda j, at: (0, 0, 0), pipeline_mode=whole),
                pl.BlockSpec((3, length, columns), lambda j, at: (0, 0, jnp.where(at[0] == 1, j, 0))),
            ],
            out_specs=pl.BlockSpec((width, columns), lambda j, at: (0, j)),
            scratch_shapes=[pltpu.VMEM((3, width, length), full.dtype)],
        ),
        compiler_params=pltpu.CompilerParams(dimension_semantics=("arbitrary",), vmem_limit_bytes=60 << 20),
        cost_estimate=pl.CostEstimate(
            flops=6 * width * length * regions, bytes_accessed=6 * length * regions, transcendentals=0),
    )(at, full, weights, prior, inner, full)


def body(sensitivity, reach, obs_weight, prior_precision, pivot_solve):
    week = lax.axis_index(WEEK)
    n_week, n_col = lax.axis_size(WEEK), lax.axis_size(COL)
    local = sensitivity[0]
    lags, length, width = local.shape
    mine = lax.axis_index(ROW) * n_col + lax.axis_index(COL)

    lag = jnp.arange(8)[:, None]
    own_weight = jnp.where((reach >= lag) & (week >= lag) & (lag < lags), obs_weight, 0.0)
    full, panel, inner, by_week = gather(local, pivot_solve, own_weight, 0)
    by_week = by_week[:, :lags]
    later = jnp.concatenate([by_week, jnp.zeros((lags, lags, length), by_week.dtype)])
    here = lax.dynamic_slice(later, (week, 0, 0), (lags, lags, length))
    weights = jnp.stack([here[0, 0], here[1, 1], here[2, 2], here[0, 1], here[1, 2], here[0, 2]])

    at = jnp.stack([week, mine]).astype(jnp.int32)
    prior = jnp.broadcast_to(prior_precision[0][:, None], (width, 128))
    out = schur_rows(at, full, weights, prior, inner)
    quarter = out.shape[1] // n_week
    schur = out[:, quarter : 2 * quarter]
    moved = [(w, lax.ppermute(out[:, w * quarter : (w + 1) * quarter], WEEK, [(1, w)])) for w in (2, 3, 0)]
    h = bands(at, full, weights, prior)
    for w, block in moved:
        schur = jnp.where(week == w, block, schur)
    return (h[None], panel, schur.astype(jnp.float32))


def solution(mesh):
    placed = (
        P(WEEK, None, None, (ROW, COL)),
        P(WEEK, None),
        P(WEEK, None),
        P(WEEK, (ROW, COL)),
        P(WEEK, (ROW, COL)),
    )
    return jax.shard_map(
        body,
        mesh=mesh,
        in_specs=placed,
        out_specs=(
            P(WEEK, None, (ROW, COL), None),
            P((ROW, COL), WEEK),
            P((ROW, COL), WEEK),
        ),
        check_vma=False,
    )
```

```python
import functools

import jax
import jax.numpy as jnp
from jax import lax
from jax.experimental import pallas as pl
from jax.experimental.pallas import tpu as pltpu
from jax.sharding import PartitionSpec as P

ROW, COL, WEEK = "row", "col", "week"
DMA = pltpu.SemaphoreType.DMA

UNITS = 5
UNIT_SLOT = ((0, 0, 0, 0), (0, 0, 0, 0), (1, 1, 3, 3), (1, 2, 2, 3), (2, 0, 0, 2))
UNIT_HALF = ((0, 0, 0, 0), (1, 1, 1, 1), (0, 0, 1, 0), (1, 0, 1, 1), (0, 0, 0, 1))
LOCAL = {
    0: ((0, 0),) * 4,
    1: ((0, 1),) * 4,
    2: (None, None, (1, 1), (1, 0)),
    3: (None, None, (2, 1), (1, 1)),
    4: (None, None, None, (2, 1)),
}
FIRST = ((1, 1, 0, 0, 2), (1, 1, 1, 0, 3), (2, 2, 0, 0, 4), (2, 1, 0, 1, 2), (3, 2, 0, 1, 3))
ONWARD = (
    ((2, 1, 3, 0), (3, 1, 3, 1), (4, 1, 4, 2), (4, 2, 2, 4)),
    ((2, 2, 3, 3), (3, 3, 2, 0)),
    ((2, 1, 1, 3), (3, 0, 2, 0)),
    ((2, 2, 1, 0), (3, 2, 1, 1), (4, 2, 4, 2), (4, 1, 2, 4)),
)
RELAY = {0: (1, 1, 4), 3: (0, 2, 4)}
FLOWS = 6


def pick(week, values):
    out = jnp.int32(values[0])
    for k, value in enumerate(values[1:], 1):
        out = jnp.where(week == k, jnp.int32(value), out)
    return out


def contract_last(left, right):
    return lax.dot_general(left, right, (((1,), (1,)), ((), ())), preferred_element_type=jnp.float32)


def gather_kernel(n_row, n_col, x_ref, pivot_ref, weight_ref, f_ref, panel_ref, inner_ref, weights_ref,
                  own, put_sem, first_s, first_r, z_s, z_r, pair_s, cross_s, cross_r, y_s, y_r, flow_s, flow_r,
                  low, piv, high, part, came_z, came_y, whole, turned, pan, inn, inn_in, wall,
                  low_s, low_r, piv_s, piv_r, high_s, high_r, loc, half_s, half_r, sum_s, sum_r,
                  all_s, all_r, back_s, back_r, pan_s, pan_r, inn_s, inn_r, wt_s, wt_r):
    row, col, week = lax.axis_index(ROW), lax.axis_index(COL), lax.axis_index(WEEK)
    _, length, width = x_ref.shape
    half = length // 2
    n = n_row * n_col
    peers = range(1, n_col)
    n_week = 4
    pair = row + 1 - 2 * lax.rem(row, 2)
    opp = jnp.where(row < 2, 2, 1)
    end = jnp.where(row < 2, 3, 0)
    inside = (row == 1) | (row == 2)
    outside = (row == 0) | (row == 3)
    middle = (week == 1) | (week == 2)
    edge = (week == 0) | (week == n_week - 1)

    barrier = pltpu.get_barrier_semaphore()
    for k in (1, n_row - 1):
        pl.semaphore_signal(barrier, inc=1, device_id={ROW: lax.rem(row + k, n_row)})
    for k in peers:
        pl.semaphore_signal(barrier, inc=1, device_id={COL: lax.rem(col + k, n_col)})
    for k in range(1, n_week):
        pl.semaphore_signal(barrier, inc=1, device_id={WEEK: lax.rem(week + k, n_week)})
    pl.semaphore_signal(barrier, inc=1, device_id={WEEK: n_week - 1 - week, ROW: pair})
    pl.semaphore_wait(barrier, 2 + (n_col - 1) + (n_week - 1) + 1)

    slots = [pick(week, UNIT_SLOT[u]) for u in range(UNITS)]
    starts = [pl.multiple_of(pick(week, UNIT_HALF[u]) * half, half) for u in range(UNITS)]

    def slab(at_row, at_col):
        return at_row * n_col + at_col

    mine, far = slab(row, col), slab(pair, col)

    def cell(slot, start, s):
        at = pl.ds(pl.multiple_of(s * width, width), width)
        return f_ref.at[slot, pl.ds(start, half), at]

    def place(u, s):
        return cell(slots[u], starts[u], s)

    def active(u, body):
        if u < 4:
            body()
        else:
            pl.when(edge)(body)

    def other(k):
        return lax.rem(col + n_col - k, n_col)

    def remote(ref, s_sem, r_sem, device, to=None):
        return pltpu.make_async_remote_copy(ref, ref if to is None else to, s_sem, r_sem, device_id=device)

    def to_pair(u, s, hop):
        return remote(place(u, s), pair_s.at[u, hop], z_r.at[u, hop], {ROW: pair})

    def to_opp(u, s, hop):
        return remote(place(u, s), z_s.at[u, hop], z_r.at[u, hop], {ROW: opp})

    def cross(u, k):
        return remote(place(u, slab(row, other(k))), cross_s.at[u, k - 1], cross_r.at[u, k - 1], {ROW: pair})

    def side(u, s, hop, k):
        return remote(place(u, s), y_s.at[u, hop, k - 1], y_r.at[u, hop, k - 1], {COL: lax.rem(col + k, n_col)})

    def aside(u, s, hop):
        for k in peers:
            side(u, s, hop, k).start()

    def flows(w, u, s):
        for i, (unit, to_week, to_slot, flow) in enumerate(ONWARD[w]):
            if unit == u:
                start = UNIT_HALF[u][w] * half
                yield remote(cell(UNIT_SLOT[u][w], start, s), flow_s.at[i, s], flow_r.at[flow, s],
                             {WEEK: jnp.int32(to_week)}, cell(to_slot, start, s))

    def spread(u, s, act="start"):
        for w in range(n_week):
            if any(unit == u for unit, *_ in ONWARD[w]):
                @pl.when(week == w)
                def _(w=w):
                    for copy in flows(w, u, s):
                        copy.start() if act == "start" else copy.wait_send()

    def relay(s, act="start"):
        for w, (h, to_week, to_slot) in RELAY.items():
            @pl.when(week == w)
            def _(w=w, h=h, to_week=to_week, to_slot=to_slot):
                ref = cell(2, h * half, s)
                copy = remote(ref, flow_s.at[4, s], flow_r.at[5, s], {WEEK: jnp.int32(to_week)},
                              cell(to_slot, h * half, s))
                if act == "start":
                    remote(ref, flow_s.at[0, s], flow_r.at[0, s], {WEEK: jnp.int32(to_week)}).wait_recv()
                    copy.start()
                else:
                    copy.wait_send()

    def relays(at_row):
        relay(slab(at_row, col))
        for k in peers:
            relay(slab(at_row, other(k)))

    def first(act):
        for w, lag, h, to_week, u in FIRST:
            @pl.when(week == w)
            def _(lag=lag, h=h, to_week=to_week, u=u):
                copy = remote(x_ref.at[lag, pl.ds(h * half, half), :], first_s.at[u], first_r.at[u],
                              {WEEK: jnp.int32(to_week)}, cell(UNIT_SLOT[u][to_week], h * half, mine))
                copy.start() if act == "start" else copy.wait_send()

    def take(u, w):
        lag, h = LOCAL[u][w]
        return pltpu.make_async_copy(x_ref.at[lag, pl.ds(h * half, half), :], own.at[u], put_sem.at[u])

    def put(u):
        return pltpu.make_async_copy(own.at[u], place(u, mine), put_sem.at[u])

    def local(u, body):
        weeks = [w for w in range(n_week) if LOCAL[u][w] is not None]
        if len({LOCAL[u][w] for w in weeks}) == 1 and len(weeks) == n_week:
            body(weeks[0])
        else:
            for w in weeks:
                pl.when(week == w)(functools.partial(body, w))

    slabs = (mine, far)
    side_of = jnp.where(row == 2, 1, 0)
    members = 2 * n_col
    chunk = 2 * length // members
    slices = pivot_ref.shape[0]

    def op_rows(op):
        return pl.ds(op * length, length)

    def low_copy(src, j, op, i, device):
        return remote(src, low_s.at[j, op, i], low_r.at[j, op], device, low.at[j, op_rows(op), :])

    def high_copy(src, j, op, i, device):
        return remote(src, high_s.at[j, op, i], high_r.at[j, op], device, high.at[j, op_rows(op), :])

    def to_week(w):
        return {WEEK: jnp.int32(w)}

    def pivot_out():
        return remote(pivot_ref, piv_s.at[0], piv_r.at[0], {ROW: pair}, piv.at[1])

    def local_copy(src, dst, i):
        return pltpu.make_async_copy(src, dst, loc.at[i])

    def weight_copy(k):
        return remote(weight_ref, wt_s.at[k - 1], wt_r.at[k - 1], {WEEK: lax.rem(week + k, n_week)}, wall.at[week])

    ROLES = ((1, 0, 1, 0, 2, 1), (2, 1, 2, 3, 1, 0))

    def by_role(body):
        for w, *role in ROLES:
            pl.when(week == w)(functools.partial(body, *role))

    def early():
        for k in range(1, n_week):
            weight_copy(k).start()
        pltpu.make_async_copy(weight_ref, wall.at[week], wt_s.at[n_week - 1]).start()

        @pl.when(outside)
        def _():
            by_role(lambda op, lag, *_: low_copy(x_ref.at[lag], 1, op, 0, {ROW: pair}).start())
            pivot_out().start()

        @pl.when(inside)
        def _():
            local_copy(pivot_ref, piv.at[0], 0).start()

            def send(op, lag, near, across, _):
                low_copy(x_ref.at[lag], 0, op, 0, to_week(across)).start()
                low_copy(x_ref.at[lag], 0, op, 1, to_week(near)).start()
                local_copy(x_ref.at[lag], low.at[0, op_rows(op), :], 1).start()

            by_role(send)

    def spread_low():
        def send(op, lag, near, across, theirs):
            ref = low.at[1, op_rows(op), :]
            low_copy(ref, 1, op, 0, to_week(across)).wait_recv()
            low_copy(ref, 1, op, 0, to_week(across)).start()
            low_copy(ref, 1, op, 1, to_week(near)).start()
            for j in range(2):
                ref = low.at[j, op_rows(theirs), :]
                low_copy(ref, j, theirs, 0, to_week(near)).wait_recv()
                low_copy(ref, j, theirs, 0, to_week(near)).start()
            local_copy(x_ref.at[lag], low.at[0, op_rows(op), :], 1).wait()

        by_role(send)

        @pl.when(edge)
        def _():
            for j in range(2):
                for op in range(2):
                    low_copy(low.at[j, op_rows(op), :], j, op, 0, to_week(1)).wait_recv()

        pivot_out().wait_recv()
        local_copy(pivot_ref, piv.at[0], 0).wait()

    def rows_of(m, count=1):
        return pl.ds(pl.multiple_of(m * chunk, chunk), count * chunk)

    def half_copy(k):
        away = rows_of((1 - side_of) * n_col + lax.rem(col + k, n_col))
        return remote(part.at[away, :], half_s.at[k], half_r.at[k], {ROW: opp}, came_z.at[k])

    def sum_copy(k):
        to = lax.rem(col + k, n_col)
        return remote(part.at[rows_of(side_of * n_col + to), :], sum_s.at[k - 1], sum_r.at[k - 1], {COL: to},
                      came_y.at[k - 1])

    me = side_of * n_col + col

    def all_copy(k):
        return remote(whole.at[rows_of(me), :], all_s.at[k - 1], all_r.at[k - 1], {COL: lax.rem(col + k, n_col)})

    def back_copy(k):
        ref = whole.at[rows_of(side_of * n_col + other(k)), :]
        return remote(ref, back_s.at[k], back_r.at[k], {ROW: opp})

    by_turn = (*peers, 0)

    def make_part():
        def fill(m):
            at = rows_of(m)
            total = contract_last(low[0, at, :], piv[0]) + contract_last(low[1, at, :], piv[1])
            part[at, :] = total.astype(part.dtype)

        for k in by_turn:
            fill((1 - side_of) * n_col + lax.rem(col + k, n_col))
            half_copy(k).start()

        @pl.loop(0, n_col)
        def _(m):
            fill(side_of * n_col + m)

    def add_half(k):
        half_copy(k).wait_recv()
        at = rows_of(side_of * n_col + lax.rem(col + k, n_col))
        total = part[at, :].astype(jnp.float32) + came_z[k].astype(jnp.float32)
        part[at, :] = total.astype(part.dtype)
        if k:
            sum_copy(k).start()

    def make_whole():
        for k in peers:
            sum_copy(k).wait_recv()
        total = part[rows_of(me), :].astype(jnp.float32)
        for k in peers:
            total = total + came_y[k - 1].astype(jnp.float32)
        whole[rows_of(me), :] = total.astype(whole.dtype)
        back_copy(0).start()
        for k in peers:
            all_copy(k).start()

    def pass_whole():
        for k in peers:
            all_copy(k).wait_recv()
            back_copy(k).start()

    def column(slot, s):
        return f_ref.at[slot, :, pl.ds(pl.multiple_of(s * width, width), width)]

    def start_high():
        @pl.when(middle)
        def _():
            for s in slabs:
                ref = cell(0, 0, s)
                remote(ref, flow_s.at[0, s], flow_r.at[3, s], {ROW: pair}).wait_recv()

        @pl.when(week == 1)
        def _():
            for j, s in enumerate(slabs):
                high_copy(column(0, s), j, 0, 0, to_week(2)).start()
                high_copy(column(0, s), j, 0, 1, to_week(0)).start()
                high_copy(column(1, s), j, 1, 0, to_week(0)).start()
                local_copy(column(0, s), high.at[j, op_rows(0), :], 2 + j).start()
                local_copy(column(1, s), high.at[j, op_rows(1), :], 4 + j).start()

        @pl.when(week == 2)
        def _():
            for j, s in enumerate(slabs):
                high_copy(column(3, s), j, 1, 0, to_week(3)).start()
                local_copy(column(3, s), high.at[j, op_rows(1), :], 4 + j).start()

    def wait_high():
        for j, s in enumerate(slabs):
            @pl.when(week == 1)
            def _(j=j, s=s):
                local_copy(column(0, s), high.at[j, op_rows(0), :], 2 + j).wait()

            @pl.when(week != 1)
            def _(j=j):
                high_copy(high.at[j, op_rows(0), :], j, 0, 0, to_week(3)).wait_recv()

            @pl.when(week == 2)
            def _(j=j):
                high_copy(high.at[j, op_rows(0), :], j, 0, 0, to_week(3)).start()

            @pl.when(middle)
            def _(j=j, s=s):
                local_copy(column(1, s), high.at[j, op_rows(1), :], 4 + j).wait()

            @pl.when(edge)
            def _(j=j):
                high_copy(high.at[j, op_rows(1), :], j, 1, 0, to_week(3)).wait_recv()

    def panel_out():
        return remote(pan.at[1], pan_s.at[0], pan_r.at[0], {ROW: pair}, panel_ref)

    def inner_near(j):
        return remote(inn.at[j], inn_s.at[j], inn_r.at[j], {WEEK: jnp.where(week == 0, 1, 2)}, inn_in.at[j])

    def inner_far(j, i):
        device = {WEEK: jnp.int32(1)} if j == 0 else {WEEK: jnp.int32(1), ROW: pair}
        return remote(inn.at[j], inn_s.at[j], inn_r.at[2 + i], device, inner_ref.at[i])

    def own_weight():
        return pltpu.make_async_copy(weight_ref, wall.at[week], wt_s.at[n_week - 1])

    def turn_high():
        wait_high()
        for k in range(1, n_week):
            weight_copy(k).wait_recv()
        own_weight().wait()
        step = min(length, 512)
        for j in range(2):
            for op in range(2):
                for at in range(0, length, step):
                    rows = pl.ds(op * length + at, step)
                    flat = high[j, rows, :].T.astype(jnp.float32) * wall[1 + op, 1 + op, pl.ds(at, step)][None, :]
                    turned[j, :, rows] = flat.astype(turned.dtype)

    tile = min(slices, 256)

    def wait_whole():
        for k in range(n_col):
            back_copy(k).wait_recv()

    def make_panel(j):
        @pl.loop(0, slices // tile)
        def _(i):
            at = pl.ds(pl.multiple_of(i * tile, tile), tile)
            pan[j, :, at] = jnp.dot(turned[j], whole[:, at], preferred_element_type=jnp.float32).astype(pan.dtype)

        if j == 0:
            local_copy(pan.at[0], panel_ref, 0).start()
        else:
            panel_out().start()

    def make_inner(j):
        @pl.loop(0, 2 * length // tile)
        def _(i):
            at = pl.ds(pl.multiple_of(i * tile, tile), tile)
            inn[j, :, at] = contract_last(pan[j], whole[at, :]).astype(inn.dtype)

        pl.when(edge)(lambda: inner_near(j).start())

    def join_inner(j):
        @pl.when(middle)
        def _():
            inner_near(j).wait_recv()
            inn[j] = (inn[j].astype(jnp.float32) + inn_in[j].astype(jnp.float32)).astype(inn.dtype)
            pl.when(week == 2)(lambda: inner_far(j, 1).start())

            @pl.when(week == 1)
            def _():
                if j == 1:
                    inner_far(1, 0).start()
                else:
                    local_copy(inn.at[0], inner_ref.at[0], 1).start()

    first("start")
    for u in range(UNITS):
        local(u, lambda w, u=u: take(u, w).start())
    early()
    for u in range(UNITS):
        def move(w, u=u):
            take(u, w).wait()
            put(u).start()

        local(u, move)

    for u in range(UNITS):
        local(u, lambda w, u=u: put(u).wait())
        for _, _, _, week_of, unit in FIRST:
            if unit == u:
                @pl.when(week == week_of)
                def _(u=u):
                    remote(place(u, mine), first_s.at[u], first_r.at[u], {ROW: pair}).wait_recv()

        def begin(u=u):
            @pl.when(inside)
            def _():
                to_opp(u, mine, 0).start()
                to_pair(u, mine, 0).start()

            pl.when(outside)(lambda: to_pair(u, mine, 1).start())
            aside(u, mine, 0)

        active(u, begin)
        pl.when(outside)(lambda u=u: spread(u, mine))

    def from_side(u, at_row, hop, onward=None):
        def body():
            for k in peers:
                side(u, mine, hop, k).wait_recv()
                if onward is not None:
                    onward(k)
                spread(u, slab(at_row, other(k)))

        active(u, body)

    def arrived(u, s, hop, then):
        def body():
            to_pair(u, s, hop).wait_recv()
            then()
            spread(u, s)

        active(u, body)

    @pl.when(outside)
    def _():
        for u in range(UNITS):
            from_side(u, row, 0, lambda k, u=u: cross(u, k).start())
        for hop, at_row in enumerate((pair, opp, end)):
            s = slab(at_row, col)
            for u in range(UNITS):
                arrived(u, s, hop, lambda u=u, s=s, hop=hop: aside(u, s, hop + 1))
                if hop:
                    from_side(u, (pair, opp)[hop - 1], hop)
                if hop == 2 and u == 2:
                    relays(row)
                    relays(pair)
        for u in range(UNITS):
            from_side(u, end, 3)
        relays(opp)
        relays(end)

    @pl.when(inside)
    def _():
        def cross_in(u):
            def body():
                for k in peers:
                    cross(u, k).wait_recv()
                    spread(u, slab(pair, other(k)))

            active(u, body)

        def near_one(u):
            s = slab(opp, col)

            def then():
                to_pair(u, s, 1).start()
                aside(u, s, 1)

            arrived(u, s, 0, then)

        def far_one(u):
            s = slab(end, col)

            def then():
                to_pair(u, s, 2).start()
                aside(u, s, 2)

            arrived(u, s, 2, then)

        def pass_on(u):
            active(u, lambda: to_opp(u, far, 2).start())

        def outer_one(u):
            arrived(u, far, 1, lambda: None)

        near_one(0)
        near_one(1)
        spread_low()
        make_part()
        for u in range(UNITS):
            spread(u, mine)
        near_one(2)
        for u in range(2):
            outer_one(u)
            pass_on(u)
        for k in peers:
            add_half(k)
        for u in range(3, UNITS):
            near_one(u)
        for u in range(2, UNITS):
            outer_one(u)
        for u in range(UNITS):
            from_side(u, row, 0)
        add_half(0)
        make_whole()
        far_one(0)
        pass_on(2)
        far_one(1)
        pass_whole()
        for u in range(3, UNITS):
            pass_on(u)
        start_high()
        for u in range(UNITS):
            from_side(u, opp, 1)
        for u in range(UNITS):
            cross_in(u)
        far_one(2)
        turn_high()
        wait_whole()
        make_panel(1)
        make_inner(1)
        make_panel(0)
        make_inner(0)
        for u in range(3, UNITS):
            far_one(u)
        relays(row)
        relays(pair)
        join_inner(1)
        join_inner(0)
        for u in range(UNITS):
            from_side(u, end, 2)
        relays(opp)
        relays(end)

    @pl.when(middle)
    def _():
        for s in range(n):
            for flow in range(FLOWS):
                def arrive(s=s, flow=flow):
                    ref = cell(0, 0, s)
                    remote(ref, flow_s.at[0, s], flow_r.at[flow, s], {ROW: pair}).wait_recv()

                if flow == 3:
                    pl.when(outside | ((mine != s) & (far != s)))(arrive)
                else:
                    arrive()

    @pl.when(week == 1)
    def _():
        inner_far(1, 1).wait_recv()
        pl.when(outside)(lambda: inner_far(1, 0).wait_recv())

    @pl.when(outside)
    def _():
        panel_out().wait_recv()
        for k in range(1, n_week):
            weight_copy(k).wait_recv()
        own_weight().wait()
        by_role(lambda op, lag, *_: low_copy(x_ref.at[lag], 1, op, 0, {ROW: pair}).wait_send())
        pivot_out().wait_send()

    weights_out = pltpu.make_async_copy(wall, weights_ref, wt_s.at[n_week - 1])
    weights_out.start()
    for k in range(1, n_week):
        weight_copy(k).wait_send()

    @pl.when(inside)
    def _():
        def sent(op, lag, near, across, theirs):
            for j in range(2):
                for i in range(2):
                    low_copy(x_ref.at[0], j, op, i, to_week(0)).wait_send()
                low_copy(x_ref.at[0], j, theirs, 0, to_week(0)).wait_send()

        by_role(sent)
        for k in range(n_col):
            half_copy(k).wait_send()
        for k in peers:
            sum_copy(k).wait_send()
            all_copy(k).wait_send()
        for k in range(n_col):
            back_copy(k).wait_send()

        @pl.when(week == 1)
        def _():
            for j, s in enumerate(slabs):
                high_copy(column(0, s), j, 0, 0, to_week(2)).wait_send()
                high_copy(column(0, s), j, 0, 1, to_week(0)).wait_send()
                high_copy(column(1, s), j, 1, 0, to_week(0)).wait_send()

        @pl.when(week == 2)
        def _():
            for j, s in enumerate(slabs):
                high_copy(column(3, s), j, 1, 0, to_week(3)).wait_send()
                high_copy(high.at[j, op_rows(0), :], j, 0, 0, to_week(3)).wait_send()

        local_copy(pan.at[0], panel_ref, 0).wait()
        panel_out().wait_send()
        for j in range(2):
            pl.when(edge)(lambda j=j: inner_near(j).wait_send())
            pl.when(week == 2)(lambda j=j: inner_far(j, 1).wait_send())

        @pl.when(week == 1)
        def _():
            inner_far(1, 0).wait_send()
            local_copy(inn.at[0], inner_ref.at[0], 1).wait()

    first("wait")
    for u in range(UNITS):
        def finish(u=u):
            for k in peers:
                for hop in range(3):
                    side(u, mine, hop, k).wait_send()

            @pl.when(outside)
            def _():
                to_pair(u, mine, 1).wait_send()
                for k in peers:
                    side(u, mine, 3, k).wait_send()
                    cross(u, k).wait_send()

            @pl.when(inside)
            def _():
                to_opp(u, mine, 0).wait_send()
                to_opp(u, far, 2).wait_send()
                for hop in range(3):
                    to_pair(u, mine, hop).wait_send()

        active(u, finish)
        if u >= 2:
            for s in range(n):
                spread(u, s, "wait")
    for s in range(n):
        relay(s, "wait")
    weights_out.wait()


def gather(x, pivot, weight, collective_id):
    n_row, n_col = lax.axis_size(ROW), lax.axis_size(COL)
    _, length, width = x.shape
    slices = pivot.shape[0]
    n = n_row * n_col
    assert n_row == 4 and lax.axis_size(WEEK) == 4
    sides = (UNITS, n_col - 1)
    vmem = functools.partial(lambda *shape: pltpu.VMEM(shape, x.dtype))
    sent = length * width * 2 * (n - 1) * 9 // 4
    hbm = pl.BlockSpec(memory_space=pl.ANY)
    return pl.pallas_call(
        functools.partial(gather_kernel, n_row, n_col),
        out_shape=(
            jax.ShapeDtypeStruct((5, length, width * n), x.dtype),
            jax.ShapeDtypeStruct((width, slices), x.dtype),
            jax.ShapeDtypeStruct((2, width, 2 * length), x.dtype),
            jax.ShapeDtypeStruct((4, *weight.shape), weight.dtype),
        ),
        in_specs=[hbm] * 3,
        out_specs=(hbm,) * 4,
        scratch_shapes=[
            pltpu.VMEM((UNITS, length // 2, width), x.dtype), DMA((UNITS,)), DMA((UNITS,)), DMA((UNITS,)),
            DMA((UNITS, 3)), DMA((UNITS, 3)), DMA((UNITS, 3)), DMA(sides), DMA(sides),
            DMA((UNITS, 4, n_col - 1)), DMA((UNITS, 4, n_col - 1)), DMA((5, n)), DMA((FLOWS, n)),
            vmem(2, 2 * length, width), vmem(2, slices, width), vmem(2, 2 * length, width),
            vmem(2 * length, slices), vmem(n_col, length // n_col, slices),
            vmem(n_col - 1, length // n_col, slices),
            vmem(2 * length, slices),
            vmem(2, width, 2 * length), vmem(2, width, slices), vmem(2, width, 2 * length),
            vmem(2, width, 2 * length), pltpu.VMEM((4, *weight.shape), weight.dtype),
            DMA((2, 2, 2)), DMA((2, 2)), DMA((1,)), DMA((1,)), DMA((2, 2, 2)), DMA((2, 2)), DMA((6,)),
            DMA((n_col,)), DMA((n_col,)), DMA((n_col - 1,)), DMA((n_col - 1,)),
            DMA((n_col - 1,)), DMA((n_col - 1,)), DMA((n_col,)), DMA((n_col,)),
            DMA((1,)), DMA((1,)), DMA((2,)), DMA((4,)), DMA((4,)), DMA((3,)),
        ],
        compiler_params=pltpu.CompilerParams(
            collective_id=collective_id, has_side_effects=True, vmem_limit_bytes=60 << 20),
        cost_estimate=pl.CostEstimate(flops=0, bytes_accessed=sent * 8, transcendentals=0),
    )(x, pivot, weight)


PRODUCTS = ((0, 0, 0, (0, 3)), (0, 1, 1, (0, 2)), (0, 2, 2, (0, 1)), (1, 0, 3, (1, 3)), (1, 1, 4, (1, 2)),
            (2, 0, 2, (2, 3)))


def bands_kernel(at_ref, left_ref, weight_ref, prior_ref, full_ref, out_ref, turned):
    week, mine = at_ref[0], at_ref[1]
    tile = pl.program_id(0)
    width = left_ref.shape[2]
    columns = full_ref.shape[2]

    @pl.when(tile == 0)
    def _():
        for p, (_, slot, _, (lo, hi)) in enumerate(PRODUCTS):
            @pl.when((week >= lo) & (week <= hi))
            def _(p=p, slot=slot):
                flat = left_ref[slot].T.astype(jnp.float32) * weight_ref[p][None, :]
                turned[p] = flat.astype(turned.dtype)

    out_ref[...] = jnp.zeros_like(out_ref)
    for p, (band, _, slot, (lo, hi)) in enumerate(PRODUCTS):
        @pl.when((week >= lo) & (week <= hi))
        def _(p=p, band=band, slot=slot):
            out_ref[band] += jnp.dot(turned[p], full_ref[slot], preferred_element_type=jnp.float32)

    row_ids = lax.broadcasted_iota(jnp.int32, (width, columns), 0) + mine * width
    col_ids = lax.broadcasted_iota(jnp.int32, (width, columns), 1) + tile * columns
    out_ref[0] += jnp.where(row_ids == col_ids, prior_ref[:, :1], 0.0)


def bands(at, full, weights, prior):
    slots, length, regions = full.shape
    width = prior.shape[0]
    columns = min(512, regions)
    return pl.pallas_call(
        bands_kernel,
        out_shape=jax.ShapeDtypeStruct((3, width, regions), jnp.float32),
        grid_spec=pltpu.PrefetchScalarGridSpec(
            num_scalar_prefetch=1,
            grid=(regions // columns,),
            in_specs=[
                pl.BlockSpec((3, length, width), lambda j, at: (0, 0, at[1]), pipeline_mode=pl.Buffered(1)),
                pl.BlockSpec(weights.shape, lambda j, at: (0, 0)),
                pl.BlockSpec(prior.shape, lambda j, at: (0, 0)),
                pl.BlockSpec((slots, length, columns), lambda j, at: (0, 0, j)),
            ],
            out_specs=pl.BlockSpec((3, width, columns), lambda j, at: (0, 0, j)),
            scratch_shapes=[pltpu.VMEM((len(PRODUCTS), width, length), full.dtype)],
        ),
        compiler_params=pltpu.CompilerParams(dimension_semantics=("arbitrary",), vmem_limit_bytes=60 << 20),
        cost_estimate=pl.CostEstimate(
            flops=10 * width * length * regions, bytes_accessed=full.size * 2 + 12 * width * regions,
            transcendentals=0),
    )(at, full, weights, prior, full)


def schur_kernel(at_ref, left_ref, weight_ref, prior_ref, inner_ref, full_ref, out_ref, turned):
    week, mine = at_ref[0], at_ref[1]
    tile = pl.program_id(0)
    slots, length, width = left_ref.shape
    columns = full_ref.shape[2]

    @pl.when(week == 1)
    def _():
        @pl.when(tile == 0)
        def _():
            for k in range(slots):
                flat = left_ref[k].T.astype(jnp.float32) * weight_ref[k][None, :]
                if k < 2:
                    at = pl.ds(k * length, length)
                    inner = inner_ref[0, :, at].astype(jnp.float32) + inner_ref[1, :, at].astype(jnp.float32)
                    flat = flat - inner * weight_ref[3 + k][None, :]
                turned[k] = flat.astype(turned.dtype)

        total = jnp.dot(turned[0], full_ref[0], preferred_element_type=jnp.float32)
        for k in range(1, slots):
            total = total + jnp.dot(turned[k], full_ref[k], preferred_element_type=jnp.float32)
        row_ids = lax.broadcasted_iota(jnp.int32, (width, columns), 0) + mine * width
        col_ids = lax.broadcasted_iota(jnp.int32, (width, columns), 1) + tile * columns
        total = total + jnp.where(row_ids == col_ids, prior_ref[:, :1], 0.0)
        out_ref[...] = total.astype(out_ref.dtype)


def schur_rows(at, full, weights, prior, inner):
    _, length, regions = full.shape
    width = prior.shape[0]
    columns = min(512, regions)
    whole = pl.Buffered(1)
    return pl.pallas_call(
        schur_kernel,
        out_shape=jax.ShapeDtypeStruct((width, regions), jnp.bfloat16),
        grid_spec=pltpu.PrefetchScalarGridSpec(
            num_scalar_prefetch=1,
            grid=(regions // columns,),
            in_specs=[
                pl.BlockSpec((3, length, width), lambda j, at: (0, 0, at[1]), pipeline_mode=whole),
                pl.BlockSpec(weights.shape, lambda j, at: (0, 0)),
                pl.BlockSpec(prior.shape, lambda j, at: (0, 0)),
                pl.BlockSpec(inner.shape, lambda j, at: (0, 0, 0), pipeline_mode=whole),
                pl.BlockSpec((3, length, columns), lambda j, at: (0, 0, jnp.where(at[0] == 1, j, 0))),
            ],
            out_specs=pl.BlockSpec((width, columns), lambda j, at: (0, j)),
            scratch_shapes=[pltpu.VMEM((3, width, length), full.dtype)],
        ),
        compiler_params=pltpu.CompilerParams(dimension_semantics=("arbitrary",), vmem_limit_bytes=60 << 20),
        cost_estimate=pl.CostEstimate(
            flops=6 * width * length * regions, bytes_accessed=6 * length * regions, transcendentals=0),
    )(at, full, weights, prior, inner, full)


def body(sensitivity, reach, obs_weight, prior_precision, pivot_solve):
    week = lax.axis_index(WEEK)
    n_week, n_col = lax.axis_size(WEEK), lax.axis_size(COL)
    local = sensitivity[0]
    lags, length, width = local.shape
    mine = lax.axis_index(ROW) * n_col + lax.axis_index(COL)

    lag = jnp.arange(8)[:, None]
    own_weight = jnp.where((reach >= lag) & (week >= lag) & (lag < lags), obs_weight, 0.0)
    full, panel, inner, by_week = gather(local, pivot_solve, own_weight, 0)
    by_week = by_week[:, :lags]
    later = jnp.concatenate([by_week, jnp.zeros((lags, lags, length), by_week.dtype)])
    here = lax.dynamic_slice(later, (week, 0, 0), (lags, lags, length))
    weights = jnp.stack([here[0, 0], here[1, 1], here[2, 2], here[0, 1], here[1, 2], here[0, 2]])

    at = jnp.stack([week, mine]).astype(jnp.int32)
    prior = jnp.broadcast_to(prior_precision[0][:, None], (width, 128))
    out = schur_rows(at, full, weights, prior, inner)
    quarter = out.shape[1] // n_week
    schur = out[:, quarter : 2 * quarter]
    moved = [(w, lax.ppermute(out[:, w * quarter : (w + 1) * quarter], WEEK, [(1, w)])) for w in (2, 3, 0)]
    h = bands(at, full, weights, prior)
    for w, block in moved:
        schur = jnp.where(week == w, block, schur)
    return (h[None], panel, schur.astype(jnp.float32))


def solution(mesh):
    placed = (
        P(WEEK, None, None, (ROW, COL)),
        P(WEEK, None),
        P(WEEK, None),
        P(WEEK, (ROW, COL)),
        P(WEEK, (ROW, COL)),
    )
    return jax.shard_map(
        body,
        mesh=mesh,
        in_specs=placed,
        out_specs=(
            P(WEEK, None, (ROW, COL), None),
            P((ROW, COL), WEEK),
            P((ROW, COL), WEEK),
        ),
        check_vma=False,
    )
```

```python
import functools

import jax
import jax.numpy as jnp
from jax import lax
from jax.experimental import pallas as pl
from jax.experimental.pallas import tpu as pltpu
from jax.sharding import PartitionSpec as P

ROW, COL, WEEK = "row", "col", "week"
DMA = pltpu.SemaphoreType.DMA

UNITS = 5
UNIT_SLOT = ((0, 0, 0, 0), (0, 0, 0, 0), (1, 1, 3, 3), (1, 2, 2, 3), (2, 0, 0, 2))
UNIT_HALF = ((0, 0, 0, 0), (1, 1, 1, 1), (0, 0, 1, 0), (1, 0, 1, 1), (0, 0, 0, 1))
LOCAL = {
    0: ((0, 0),) * 4,
    1: ((0, 1),) * 4,
    2: (None, None, (1, 1), (1, 0)),
    3: (None, None, (2, 1), (1, 1)),
    4: (None, None, None, (2, 1)),
}
FIRST = ((1, 1, 0, 0, 2), (1, 1, 1, 0, 3), (2, 2, 0, 0, 4), (2, 1, 0, 1, 2), (3, 2, 0, 1, 3))
ONWARD = (
    ((2, 1, 3, 0), (3, 1, 3, 1), (4, 1, 4, 2), (4, 2, 2, 4)),
    ((2, 2, 3, 3), (3, 3, 2, 0)),
    ((2, 1, 1, 3), (3, 0, 2, 0)),
    ((2, 2, 1, 0), (3, 2, 1, 1), (4, 2, 4, 2), (4, 1, 2, 4)),
)
RELAY = {0: (1, 1, 4), 3: (0, 2, 4)}
FLOWS = 6


def pick(week, values):
    out = jnp.int32(values[0])
    for k, value in enumerate(values[1:], 1):
        out = jnp.where(week == k, jnp.int32(value), out)
    return out


def contract_last(left, right):
    return lax.dot_general(left, right, (((1,), (1,)), ((), ())), preferred_element_type=jnp.float32)


def gather_kernel(n_row, n_col, x_ref, pivot_ref, weight_ref, f_ref, panel_ref, inner_ref, weights_ref,
                  own, put_sem, first_s, first_r, z_s, z_r, pair_s, cross_s, cross_r, y_s, y_r, flow_s, flow_r,
                  low, piv, high, part, came_z, came_y, whole, turned, pan, inn, inn_in, wall,
                  low_s, low_r, piv_s, piv_r, high_s, high_r, loc, half_s, half_r, sum_s, sum_r,
                  all_s, all_r, back_s, back_r, pan_s, pan_r, inn_s, inn_r, wt_s, wt_r):
    row, col, week = lax.axis_index(ROW), lax.axis_index(COL), lax.axis_index(WEEK)
    _, length, width = x_ref.shape
    half = length // 2
    n = n_row * n_col
    peers = range(1, n_col)
    n_week = 4
    pair = row + 1 - 2 * lax.rem(row, 2)
    opp = jnp.where(row < 2, 2, 1)
    end = jnp.where(row < 2, 3, 0)
    inside = (row == 1) | (row == 2)
    outside = (row == 0) | (row == 3)
    middle = (week == 1) | (week == 2)
    edge = (week == 0) | (week == n_week - 1)

    barrier = pltpu.get_barrier_semaphore()
    for k in (1, n_row - 1):
        pl.semaphore_signal(barrier, inc=1, device_id={ROW: lax.rem(row + k, n_row)})
    for k in peers:
        pl.semaphore_signal(barrier, inc=1, device_id={COL: lax.rem(col + k, n_col)})
    for k in range(1, n_week):
        pl.semaphore_signal(barrier, inc=1, device_id={WEEK: lax.rem(week + k, n_week)})
    pl.semaphore_signal(barrier, inc=1, device_id={WEEK: n_week - 1 - week, ROW: pair})
    pl.semaphore_wait(barrier, 2 + (n_col - 1) + (n_week - 1) + 1)

    slots = [pick(week, UNIT_SLOT[u]) for u in range(UNITS)]
    starts = [pl.multiple_of(pick(week, UNIT_HALF[u]) * half, half) for u in range(UNITS)]

    def slab(at_row, at_col):
        return at_row * n_col + at_col

    mine, far = slab(row, col), slab(pair, col)

    def cell(slot, start, s):
        at = pl.ds(pl.multiple_of(s * width, width), width)
        return f_ref.at[slot, pl.ds(start, half), at]

    def place(u, s):
        return cell(slots[u], starts[u], s)

    def active(u, body):
        if u < 4:
            body()
        else:
            pl.when(edge)(body)

    def other(k):
        return lax.rem(col + n_col - k, n_col)

    def remote(ref, s_sem, r_sem, device, to=None):
        return pltpu.make_async_remote_copy(ref, ref if to is None else to, s_sem, r_sem, device_id=device)

    def to_pair(u, s, hop):
        return remote(place(u, s), pair_s.at[u, hop], z_r.at[u, hop], {ROW: pair})

    def to_opp(u, s, hop):
        return remote(place(u, s), z_s.at[u, hop], z_r.at[u, hop], {ROW: opp})

    def cross(u, k):
        return remote(place(u, slab(row, other(k))), cross_s.at[u, k - 1], cross_r.at[u, k - 1], {ROW: pair})

    def side(u, s, hop, k):
        return remote(place(u, s), y_s.at[u, hop, k - 1], y_r.at[u, hop, k - 1], {COL: lax.rem(col + k, n_col)})

    def aside(u, s, hop):
        for k in peers:
            side(u, s, hop, k).start()

    def flows(w, u, s):
        for i, (unit, to_week, to_slot, flow) in enumerate(ONWARD[w]):
            if unit == u:
                start = UNIT_HALF[u][w] * half
                yield remote(cell(UNIT_SLOT[u][w], start, s), flow_s.at[i, s], flow_r.at[flow, s],
                             {WEEK: jnp.int32(to_week)}, cell(to_slot, start, s))

    def spread(u, s, act="start"):
        for w in range(n_week):
            if any(unit == u for unit, *_ in ONWARD[w]):
                @pl.when(week == w)
                def _(w=w):
                    for copy in flows(w, u, s):
                        copy.start() if act == "start" else copy.wait_send()

    def relay(s, act="start"):
        for w, (h, to_week, to_slot) in RELAY.items():
            @pl.when(week == w)
            def _(w=w, h=h, to_week=to_week, to_slot=to_slot):
                ref = cell(2, h * half, s)
                copy = remote(ref, flow_s.at[4, s], flow_r.at[5, s], {WEEK: jnp.int32(to_week)},
                              cell(to_slot, h * half, s))
                if act == "start":
                    remote(ref, flow_s.at[0, s], flow_r.at[0, s], {WEEK: jnp.int32(to_week)}).wait_recv()
                    copy.start()
                else:
                    copy.wait_send()

    def relays(at_row):
        relay(slab(at_row, col))
        for k in peers:
            relay(slab(at_row, other(k)))

    def first(act):
        for w, lag, h, to_week, u in FIRST:
            @pl.when(week == w)
            def _(lag=lag, h=h, to_week=to_week, u=u):
                copy = remote(x_ref.at[lag, pl.ds(h * half, half), :], first_s.at[u], first_r.at[u],
                              {WEEK: jnp.int32(to_week)}, cell(UNIT_SLOT[u][to_week], h * half, mine))
                copy.start() if act == "start" else copy.wait_send()

    def take(u, w):
        lag, h = LOCAL[u][w]
        return pltpu.make_async_copy(x_ref.at[lag, pl.ds(h * half, half), :], own.at[u], put_sem.at[u])

    def put(u):
        return pltpu.make_async_copy(own.at[u], place(u, mine), put_sem.at[u])

    def local(u, body):
        weeks = [w for w in range(n_week) if LOCAL[u][w] is not None]
        if len({LOCAL[u][w] for w in weeks}) == 1 and len(weeks) == n_week:
            body(weeks[0])
        else:
            for w in weeks:
                pl.when(week == w)(functools.partial(body, w))

    slabs = (mine, far)
    side_of = jnp.where(row == 2, 1, 0)
    members = 2 * n_col
    chunk = 2 * length // members
    slices = pivot_ref.shape[0]

    def op_rows(op):
        return pl.ds(op * length, length)

    def low_copy(src, j, op, i, device):
        return remote(src, low_s.at[j, op, i], low_r.at[j, op], device, low.at[j, op_rows(op), :])

    def high_copy(src, j, op, i, device):
        return remote(src, high_s.at[j, op, i], high_r.at[j, op], device, high.at[j, op_rows(op), :])

    def to_week(w):
        return {WEEK: jnp.int32(w)}

    def pivot_out():
        return remote(pivot_ref, piv_s.at[0], piv_r.at[0], {ROW: pair}, piv.at[1])

    def local_copy(src, dst, i):
        return pltpu.make_async_copy(src, dst, loc.at[i])

    def weight_copy(k):
        return remote(weight_ref, wt_s.at[k - 1], wt_r.at[k - 1], {WEEK: lax.rem(week + k, n_week)}, wall.at[week])

    ROLES = ((1, 0, 1, 0, 2, 1), (2, 1, 2, 3, 1, 0))

    def by_role(body):
        for w, *role in ROLES:
            pl.when(week == w)(functools.partial(body, *role))

    def early():
        for k in range(1, n_week):
            weight_copy(k).start()
        pltpu.make_async_copy(weight_ref, wall.at[week], wt_s.at[n_week - 1]).start()

        @pl.when(outside)
        def _():
            by_role(lambda op, lag, *_: low_copy(x_ref.at[lag], 1, op, 0, {ROW: pair}).start())
            pivot_out().start()

        @pl.when(inside)
        def _():
            local_copy(pivot_ref, piv.at[0], 0).start()

            def send(op, lag, near, across, _):
                low_copy(x_ref.at[lag], 0, op, 0, to_week(across)).start()
                low_copy(x_ref.at[lag], 0, op, 1, to_week(near)).start()
                local_copy(x_ref.at[lag], low.at[0, op_rows(op), :], 1).start()

            by_role(send)

    def spread_low():
        def send(op, lag, near, across, theirs):
            ref = low.at[1, op_rows(op), :]
            low_copy(ref, 1, op, 0, to_week(across)).wait_recv()
            low_copy(ref, 1, op, 0, to_week(across)).start()
            low_copy(ref, 1, op, 1, to_week(near)).start()
            for j in range(2):
                ref = low.at[j, op_rows(theirs), :]
                low_copy(ref, j, theirs, 0, to_week(near)).wait_recv()
                low_copy(ref, j, theirs, 0, to_week(near)).start()
            local_copy(x_ref.at[lag], low.at[0, op_rows(op), :], 1).wait()

        by_role(send)

        @pl.when(edge)
        def _():
            for j in range(2):
                for op in range(2):
                    low_copy(low.at[j, op_rows(op), :], j, op, 0, to_week(1)).wait_recv()

        pivot_out().wait_recv()
        local_copy(pivot_ref, piv.at[0], 0).wait()

    def rows_of(m, count=1):
        return pl.ds(pl.multiple_of(m * chunk, chunk), count * chunk)

    def half_copy(k):
        away = rows_of((1 - side_of) * n_col + lax.rem(col + k, n_col))
        return remote(part.at[away, :], half_s.at[k], half_r.at[k], {ROW: opp}, came_z.at[k])

    def sum_copy(k):
        to = lax.rem(col + k, n_col)
        return remote(part.at[rows_of(side_of * n_col + to), :], sum_s.at[k - 1], sum_r.at[k - 1], {COL: to},
                      came_y.at[k - 1])

    me = side_of * n_col + col

    def all_copy(k):
        return remote(whole.at[rows_of(me), :], all_s.at[k - 1], all_r.at[k - 1], {COL: lax.rem(col + k, n_col)})

    def back_copy(k):
        ref = whole.at[rows_of(side_of * n_col + other(k)), :]
        return remote(ref, back_s.at[k], back_r.at[k], {ROW: opp})

    by_turn = (*peers, 0)

    def make_part():
        def fill(m):
            at = rows_of(m)
            total = contract_last(low[0, at, :], piv[0]) + contract_last(low[1, at, :], piv[1])
            part[at, :] = total.astype(part.dtype)

        for k in by_turn:
            fill((1 - side_of) * n_col + lax.rem(col + k, n_col))
            half_copy(k).start()

        @pl.loop(0, n_col)
        def _(m):
            fill(side_of * n_col + m)

    def add_half(k):
        half_copy(k).wait_recv()
        at = rows_of(side_of * n_col + lax.rem(col + k, n_col))
        total = part[at, :].astype(jnp.float32) + came_z[k].astype(jnp.float32)
        part[at, :] = total.astype(part.dtype)
        if k:
            sum_copy(k).start()

    def make_whole():
        for k in peers:
            sum_copy(k).wait_recv()
        total = part[rows_of(me), :].astype(jnp.float32)
        for k in peers:
            total = total + came_y[k - 1].astype(jnp.float32)
        whole[rows_of(me), :] = total.astype(whole.dtype)
        back_copy(0).start()
        for k in peers:
            all_copy(k).start()

    def pass_whole():
        for k in peers:
            all_copy(k).wait_recv()
            back_copy(k).start()

    def column(slot, s):
        return f_ref.at[slot, :, pl.ds(pl.multiple_of(s * width, width), width)]

    def start_high():
        @pl.when(middle)
        def _():
            for s in slabs:
                ref = cell(0, 0, s)
                remote(ref, flow_s.at[0, s], flow_r.at[3, s], {ROW: pair}).wait_recv()

        @pl.when(week == 1)
        def _():
            for j, s in enumerate(slabs):
                high_copy(column(0, s), j, 0, 0, to_week(2)).start()
                high_copy(column(0, s), j, 0, 1, to_week(0)).start()
                high_copy(column(1, s), j, 1, 0, to_week(0)).start()
                local_copy(column(0, s), high.at[j, op_rows(0), :], 2 + j).start()
                local_copy(column(1, s), high.at[j, op_rows(1), :], 4 + j).start()

        @pl.when(week == 2)
        def _():
            for j, s in enumerate(slabs):
                high_copy(column(3, s), j, 1, 0, to_week(3)).start()
                local_copy(column(3, s), high.at[j, op_rows(1), :], 4 + j).start()

    def wait_high():
        for j, s in enumerate(slabs):
            @pl.when(week == 1)
            def _(j=j, s=s):
                local_copy(column(0, s), high.at[j, op_rows(0), :], 2 + j).wait()

            @pl.when(week != 1)
            def _(j=j):
                high_copy(high.at[j, op_rows(0), :], j, 0, 0, to_week(3)).wait_recv()

            @pl.when(week == 2)
            def _(j=j):
                high_copy(high.at[j, op_rows(0), :], j, 0, 0, to_week(3)).start()

            @pl.when(middle)
            def _(j=j, s=s):
                local_copy(column(1, s), high.at[j, op_rows(1), :], 4 + j).wait()

            @pl.when(edge)
            def _(j=j):
                high_copy(high.at[j, op_rows(1), :], j, 1, 0, to_week(3)).wait_recv()

    def panel_out():
        return remote(pan.at[1], pan_s.at[0], pan_r.at[0], {ROW: pair}, panel_ref)

    def inner_near(j):
        return remote(inn.at[j], inn_s.at[j], inn_r.at[j], {WEEK: jnp.where(week == 0, 1, 2)}, inn_in.at[j])

    def inner_far(j, i):
        device = {WEEK: jnp.int32(1)} if j == 0 else {WEEK: jnp.int32(1), ROW: pair}
        return remote(inn.at[j], inn_s.at[j], inn_r.at[2 + i], device, inner_ref.at[i])

    def own_weight():
        return pltpu.make_async_copy(weight_ref, wall.at[week], wt_s.at[n_week - 1])

    def turn_high():
        wait_high()
        for k in range(1, n_week):
            weight_copy(k).wait_recv()
        own_weight().wait()
        step = min(length, 512)
        for j in range(2):
            for op in range(2):
                for at in range(0, length, step):
                    rows = pl.ds(op * length + at, step)
                    flat = high[j, rows, :].T.astype(jnp.float32) * wall[1 + op, 1 + op, pl.ds(at, step)][None, :]
                    turned[j, :, rows] = flat.astype(turned.dtype)

    tile = min(slices, 256)

    def wait_whole():
        for k in range(n_col):
            back_copy(k).wait_recv()

    def make_panel(j):
        @pl.loop(0, slices // tile)
        def _(i):
            at = pl.ds(pl.multiple_of(i * tile, tile), tile)
            pan[j, :, at] = jnp.dot(turned[j], whole[:, at], preferred_element_type=jnp.float32).astype(pan.dtype)

        if j == 0:
            local_copy(pan.at[0], panel_ref, 0).start()
        else:
            panel_out().start()

    def make_inner(j):
        @pl.loop(0, 2 * length // tile)
        def _(i):
            at = pl.ds(pl.multiple_of(i * tile, tile), tile)
            inn[j, :, at] = contract_last(pan[j], whole[at, :]).astype(inn.dtype)

        pl.when(edge)(lambda: inner_near(j).start())

    def join_inner(j):
        @pl.when(middle)
        def _():
            inner_near(j).wait_recv()
            inn[j] = (inn[j].astype(jnp.float32) + inn_in[j].astype(jnp.float32)).astype(inn.dtype)
            pl.when(week == 2)(lambda: inner_far(j, 1).start())

            @pl.when(week == 1)
            def _():
                if j == 1:
                    inner_far(1, 0).start()
                else:
                    local_copy(inn.at[0], inner_ref.at[0], 1).start()

    first("start")
    for u in range(UNITS):
        local(u, lambda w, u=u: take(u, w).start())
    early()
    for u in range(UNITS):
        def move(w, u=u):
            take(u, w).wait()
            put(u).start()

        local(u, move)

    for u in range(UNITS):
        local(u, lambda w, u=u: put(u).wait())
        for _, _, _, week_of, unit in FIRST:
            if unit == u:
                @pl.when(week == week_of)
                def _(u=u):
                    remote(place(u, mine), first_s.at[u], first_r.at[u], {ROW: pair}).wait_recv()

        def begin(u=u):
            @pl.when(inside)
            def _():
                to_opp(u, mine, 0).start()
                to_pair(u, mine, 0).start()

            pl.when(outside)(lambda: to_pair(u, mine, 1).start())
            aside(u, mine, 0)

        active(u, begin)
        pl.when(outside)(lambda u=u: spread(u, mine))

    def from_side(u, at_row, hop, onward=None):
        def body():
            for k in peers:
                side(u, mine, hop, k).wait_recv()
                if onward is not None:
                    onward(k)
                spread(u, slab(at_row, other(k)))

        active(u, body)

    def arrived(u, s, hop, then):
        def body():
            to_pair(u, s, hop).wait_recv()
            then()
            spread(u, s)

        active(u, body)

    @pl.when(outside)
    def _():
        for u in range(UNITS):
            from_side(u, row, 0, lambda k, u=u: cross(u, k).start())
        for hop, at_row in enumerate((pair, opp, end)):
            s = slab(at_row, col)
            for u in range(UNITS):
                arrived(u, s, hop, lambda u=u, s=s, hop=hop: aside(u, s, hop + 1))
                if hop:
                    from_side(u, (pair, opp)[hop - 1], hop)
                if hop == 2 and u == 2:
                    relays(row)
                    relays(pair)
        for u in range(UNITS):
            from_side(u, end, 3)
        relays(opp)
        relays(end)

    @pl.when(inside)
    def _():
        def cross_in(u):
            def body():
                for k in peers:
                    cross(u, k).wait_recv()
                    spread(u, slab(pair, other(k)))

            active(u, body)

        def near_one(u):
            s = slab(opp, col)

            def then():
                to_pair(u, s, 1).start()
                aside(u, s, 1)

            arrived(u, s, 0, then)

        def far_one(u):
            s = slab(end, col)

            def then():
                to_pair(u, s, 2).start()
                aside(u, s, 2)

            arrived(u, s, 2, then)

        def pass_on(u):
            active(u, lambda: to_opp(u, far, 2).start())

        def outer_one(u):
            arrived(u, far, 1, lambda: None)

        near_one(0)
        near_one(1)
        spread_low()
        make_part()
        for u in range(UNITS):
            spread(u, mine)
        near_one(2)
        for u in range(2):
            outer_one(u)
            pass_on(u)
        for k in peers:
            add_half(k)
        for u in range(3, UNITS):
            near_one(u)
        for u in range(2, UNITS):
            outer_one(u)
        for u in range(UNITS):
            from_side(u, row, 0)
        add_half(0)
        make_whole()
        far_one(0)
        pass_on(2)
        far_one(1)
        pass_whole()
        for u in range(3, UNITS):
            pass_on(u)
        start_high()
        for u in range(UNITS):
            from_side(u, opp, 1)
        for u in range(UNITS):
            cross_in(u)
        far_one(2)
        turn_high()
        wait_whole()
        make_panel(1)
        make_inner(1)
        make_panel(0)
        make_inner(0)
        for u in range(3, UNITS):
            far_one(u)
        relays(row)
        relays(pair)
        join_inner(1)
        join_inner(0)
        for u in range(UNITS):
            from_side(u, end, 2)
        relays(opp)
        relays(end)

    @pl.when(middle)
    def _():
        for s in range(n):
            for flow in range(FLOWS):
                def arrive(s=s, flow=flow):
                    ref = cell(0, 0, s)
                    remote(ref, flow_s.at[0, s], flow_r.at[flow, s], {ROW: pair}).wait_recv()

                if flow == 3:
                    pl.when(outside | ((mine != s) & (far != s)))(arrive)
                else:
                    arrive()

    @pl.when(week == 1)
    def _():
        inner_far(1, 1).wait_recv()
        pl.when(outside)(lambda: inner_far(1, 0).wait_recv())

    @pl.when(outside)
    def _():
        panel_out().wait_recv()
        for k in range(1, n_week):
            weight_copy(k).wait_recv()
        own_weight().wait()
        by_role(lambda op, lag, *_: low_copy(x_ref.at[lag], 1, op, 0, {ROW: pair}).wait_send())
        pivot_out().wait_send()

    weights_out = pltpu.make_async_copy(wall, weights_ref, wt_s.at[n_week - 1])
    weights_out.start()
    for k in range(1, n_week):
        weight_copy(k).wait_send()

    @pl.when(inside)
    def _():
        def sent(op, lag, near, across, theirs):
            for j in range(2):
                for i in range(2):
                    low_copy(x_ref.at[0], j, op, i, to_week(0)).wait_send()
                low_copy(x_ref.at[0], j, theirs, 0, to_week(0)).wait_send()

        by_role(sent)
        for k in range(n_col):
            half_copy(k).wait_send()
        for k in peers:
            sum_copy(k).wait_send()
            all_copy(k).wait_send()
        for k in range(n_col):
            back_copy(k).wait_send()

        @pl.when(week == 1)
        def _():
            for j, s in enumerate(slabs):
                high_copy(column(0, s), j, 0, 0, to_week(2)).wait_send()
                high_copy(column(0, s), j, 0, 1, to_week(0)).wait_send()
                high_copy(column(1, s), j, 1, 0, to_week(0)).wait_send()

        @pl.when(week == 2)
        def _():
            for j, s in enumerate(slabs):
                high_copy(column(3, s), j, 1, 0, to_week(3)).wait_send()
                high_copy(high.at[j, op_rows(0), :], j, 0, 0, to_week(3)).wait_send()

        local_copy(pan.at[0], panel_ref, 0).wait()
        panel_out().wait_send()
        for j in range(2):
            pl.when(edge)(lambda j=j: inner_near(j).wait_send())
            pl.when(week == 2)(lambda j=j: inner_far(j, 1).wait_send())

        @pl.when(week == 1)
        def _():
            inner_far(1, 0).wait_send()
            local_copy(inn.at[0], inner_ref.at[0], 1).wait()

    first("wait")
    for u in range(UNITS):
        def finish(u=u):
            for k in peers:
                for hop in range(3):
                    side(u, mine, hop, k).wait_send()

            @pl.when(outside)
            def _():
                to_pair(u, mine, 1).wait_send()
                for k in peers:
                    side(u, mine, 3, k).wait_send()
                    cross(u, k).wait_send()

            @pl.when(inside)
            def _():
                to_opp(u, mine, 0).wait_send()
                to_opp(u, far, 2).wait_send()
                for hop in range(3):
                    to_pair(u, mine, hop).wait_send()

        active(u, finish)
        if u >= 2:
            for s in range(n):
                spread(u, s, "wait")
    for s in range(n):
        relay(s, "wait")
    weights_out.wait()


def gather(x, pivot, weight, collective_id):
    n_row, n_col = lax.axis_size(ROW), lax.axis_size(COL)
    _, length, width = x.shape
    slices = pivot.shape[0]
    n = n_row * n_col
    assert n_row == 4 and lax.axis_size(WEEK) == 4
    sides = (UNITS, n_col - 1)
    vmem = functools.partial(lambda *shape: pltpu.VMEM(shape, x.dtype))
    sent = length * width * 2 * (n - 1) * 9 // 4
    hbm = pl.BlockSpec(memory_space=pl.ANY)
    return pl.pallas_call(
        functools.partial(gather_kernel, n_row, n_col),
        out_shape=(
            jax.ShapeDtypeStruct((5, length, width * n), x.dtype),
            jax.ShapeDtypeStruct((width, slices), x.dtype),
            jax.ShapeDtypeStruct((2, width, 2 * length), x.dtype),
            jax.ShapeDtypeStruct((4, *weight.shape), weight.dtype),
        ),
        in_specs=[hbm] * 3,
        out_specs=(hbm,) * 4,
        scratch_shapes=[
            pltpu.VMEM((UNITS, length // 2, width), x.dtype), DMA((UNITS,)), DMA((UNITS,)), DMA((UNITS,)),
            DMA((UNITS, 3)), DMA((UNITS, 3)), DMA((UNITS, 3)), DMA(sides), DMA(sides),
            DMA((UNITS, 4, n_col - 1)), DMA((UNITS, 4, n_col - 1)), DMA((5, n)), DMA((FLOWS, n)),
            vmem(2, 2 * length, width), vmem(2, slices, width), vmem(2, 2 * length, width),
            vmem(2 * length, slices), vmem(n_col, length // n_col, slices),
            vmem(n_col - 1, length // n_col, slices),
            vmem(2 * length, slices),
            vmem(2, width, 2 * length), vmem(2, width, slices), vmem(2, width, 2 * length),
            vmem(2, width, 2 * length), pltpu.VMEM((4, *weight.shape), weight.dtype),
            DMA((2, 2, 2)), DMA((2, 2)), DMA((1,)), DMA((1,)), DMA((2, 2, 2)), DMA((2, 2)), DMA((6,)),
            DMA((n_col,)), DMA((n_col,)), DMA((n_col - 1,)), DMA((n_col - 1,)),
            DMA((n_col - 1,)), DMA((n_col - 1,)), DMA((n_col,)), DMA((n_col,)),
            DMA((1,)), DMA((1,)), DMA((2,)), DMA((4,)), DMA((4,)), DMA((3,)),
        ],
        compiler_params=pltpu.CompilerParams(
            collective_id=collective_id, has_side_effects=True, vmem_limit_bytes=60 << 20),
        cost_estimate=pl.CostEstimate(flops=0, bytes_accessed=sent * 8, transcendentals=0),
    )(x, pivot, weight)


TERMS = (
    (((0, 0, 0), (1, 1, 1), (2, 2, 2)), (), ()),
    (((0, 0, 0), (1, 1, 1), (2, 2, 2)), ((0, 3, 3), (1, 4, 4)), ()),
    (((0, 0, 0), (1, 1, 1)), ((0, 3, 3), (1, 4, 4)), ((0, 2, 5),)),
    (((0, 0, 0),), ((0, 3, 3),), ((0, 2, 5),)),
)
HAVE = tuple(tuple(any(right == slot for band in week for _, right, _ in band) for week in TERMS) for slot in range(5))


def when_tile(at_ref, tile, columns, width, body):
    first = at_ref[1] * width

    @pl.when(first // columns == tile)
    def _():
        body(pl.ds(pl.multiple_of(lax.rem(first, columns), width), width))


def diagonal(prior_ref, width):
    rows = lax.broadcasted_iota(jnp.int32, (width, width), 0)
    cols = lax.broadcasted_iota(jnp.int32, (width, width), 1)
    return jnp.where(rows == cols, prior_ref[:, :1], 0.0)


def bands_kernel(at_ref, left_ref, weight_ref, prior_ref, *refs):
    full_refs, out_ref, turned = refs[:5], refs[5], refs[6]
    week = at_ref[0]
    tile = pl.program_id(0)
    width = left_ref.shape[2]
    columns = out_ref.shape[2]

    for w, by_band in enumerate(TERMS):
        @pl.when(week == w)
        def _(by_band=by_band):
            @pl.when(tile == 0)
            def _():
                for band in by_band:
                    for slot, _, p in band:
                        flat = left_ref[slot].T.astype(jnp.float32) * weight_ref[p][None, :]
                        turned[p] = flat.astype(turned.dtype)

            for i, band in enumerate(by_band):
                if band:
                    total = None
                    for _, right, p in band:
                        term = jnp.dot(turned[p], full_refs[right][...], preferred_element_type=jnp.float32)
                        total = term if total is None else total + term
                    out_ref[i] = total
                else:
                    out_ref[i] = jnp.zeros(out_ref.shape[1:], out_ref.dtype)

    def add(at):
        out_ref[0, :, at] += diagonal(prior_ref, width)

    when_tile(at_ref, tile, columns, width, add)


def bands(at, full, weights, prior, columns):
    slots, length, regions = full.shape
    width = prior.shape[0]

    def right(slot):
        def index(j, at):
            here = functools.reduce(jnp.logical_or, [at[0] == w for w in range(4) if HAVE[slot][w]])
            return slot, 0, jnp.where(here, j, 0)

        return pl.BlockSpec((None, length, columns), index)

    return pl.pallas_call(
        bands_kernel,
        out_shape=jax.ShapeDtypeStruct((3, width, regions), jnp.float32),
        grid_spec=pltpu.PrefetchScalarGridSpec(
            num_scalar_prefetch=1,
            grid=(regions // columns,),
            in_specs=[
                pl.BlockSpec((3, length, width), lambda j, at: (0, 0, at[1]), pipeline_mode=pl.Buffered(1)),
                pl.BlockSpec(weights.shape, lambda j, at: (0, 0)),
                pl.BlockSpec(prior.shape, lambda j, at: (0, 0)),
                *[right(slot) for slot in range(slots)],
            ],
            out_specs=pl.BlockSpec((3, width, columns), lambda j, at: (0, 0, j)),
            scratch_shapes=[pltpu.VMEM((6, width, length), full.dtype)],
        ),
        compiler_params=pltpu.CompilerParams(dimension_semantics=("arbitrary",), vmem_limit_bytes=60 << 20),
        cost_estimate=pl.CostEstimate(
            flops=10 * width * length * regions, bytes_accessed=full.size * 2 + 12 * width * regions,
            transcendentals=0),
    )(at, full, weights, prior, *[full] * slots)


def schur_kernel(at_ref, left_ref, weight_ref, prior_ref, inner_ref, *refs):
    full_refs, out_refs, turned, total = refs[:3], refs[3:-2], refs[-2], refs[-1]
    week = at_ref[0]
    tile = pl.program_id(0)
    slots, length, width = left_ref.shape
    columns = total.shape[1]
    tiles = pl.num_programs(0) // len(out_refs)

    @pl.when(week == 1)
    def _():
        @pl.when(tile == 0)
        def _():
            for k in range(slots):
                flat = left_ref[k].T.astype(jnp.float32) * weight_ref[k][None, :]
                if k < 2:
                    at = pl.ds(k * length, length)
                    inner = inner_ref[0, :, at].astype(jnp.float32) + inner_ref[1, :, at].astype(jnp.float32)
                    flat = flat - inner * weight_ref[3 + k][None, :]
                turned[k] = flat.astype(turned.dtype)

        block = jnp.dot(turned[0], full_refs[0][...], preferred_element_type=jnp.float32)
        for k in range(1, slots):
            block = block + jnp.dot(turned[k], full_refs[k][...], preferred_element_type=jnp.float32)
        total[...] = block

        def add(at):
            total[:, at] += diagonal(prior_ref, width)

        when_tile(at_ref, tile, columns, width, add)
        for q, out_ref in enumerate(out_refs):
            @pl.when(tile // tiles == q)
            def _(out_ref=out_ref):
                out_ref[...] = total[...].astype(out_ref.dtype)


def schur_rows(at, full, weights, prior, inner, columns):
    _, length, regions = full.shape
    width = prior.shape[0]
    quarters = 4
    columns = min(columns, regions // quarters)
    tiles = regions // quarters // columns
    whole = pl.Buffered(1)

    def part(q):
        return pl.BlockSpec((width, columns), lambda j, at: (0, jnp.clip(j - q * tiles, 0, tiles - 1)))

    def right(slot):
        return pl.BlockSpec((None, length, columns), lambda j, at: (slot, 0, jnp.where(at[0] == 1, j, 0)))

    return pl.pallas_call(
        schur_kernel,
        out_shape=[jax.ShapeDtypeStruct((width, regions // quarters), jnp.bfloat16)] * quarters,
        grid_spec=pltpu.PrefetchScalarGridSpec(
            num_scalar_prefetch=1,
            grid=(regions // columns,),
            in_specs=[
                pl.BlockSpec((3, length, width), lambda j, at: (0, 0, at[1]), pipeline_mode=whole),
                pl.BlockSpec(weights.shape, lambda j, at: (0, 0)),
                pl.BlockSpec(prior.shape, lambda j, at: (0, 0)),
                pl.BlockSpec(inner.shape, lambda j, at: (0, 0, 0), pipeline_mode=whole),
                *[right(slot) for slot in range(3)],
            ],
            out_specs=[part(q) for q in range(quarters)],
            scratch_shapes=[pltpu.VMEM((3, width, length), full.dtype), pltpu.VMEM((width, columns), jnp.float32)],
        ),
        compiler_params=pltpu.CompilerParams(dimension_semantics=("arbitrary",), vmem_limit_bytes=60 << 20),
        cost_estimate=pl.CostEstimate(
            flops=6 * width * length * regions, bytes_accessed=6 * length * regions, transcendentals=0),
    )(at, full, weights, prior, inner, *[full] * 3)


def body(sensitivity, reach, obs_weight, prior_precision, pivot_solve):
    week = lax.axis_index(WEEK)
    n_week, n_col = lax.axis_size(WEEK), lax.axis_size(COL)
    local = sensitivity[0]
    lags, length, width = local.shape
    mine = lax.axis_index(ROW) * n_col + lax.axis_index(COL)

    lag = jnp.arange(8)[:, None]
    own_weight = jnp.where((reach >= lag) & (week >= lag) & (lag < lags), obs_weight, 0.0)
    full, panel, inner, by_week = gather(local, pivot_solve, own_weight, 0)
    by_week = by_week[:, :lags]
    later = jnp.concatenate([by_week, jnp.zeros((lags, lags, length), by_week.dtype)])
    here = lax.dynamic_slice(later, (week, 0, 0), (lags, lags, length))
    weights = jnp.stack([here[0, 0], here[1, 1], here[2, 2], here[0, 1], here[1, 2], here[0, 2]])

    at = jnp.stack([week, mine]).astype(jnp.int32)
    prior = jnp.broadcast_to(prior_precision[0][:, None], (width, 128))
    columns = max(min(1024, full.shape[2] // n_week), width)
    rows = schur_rows(at, full, weights, prior, inner, columns)
    moved = [(w, lax.ppermute(rows[w], WEEK, [(1, w)])) for w in (2, 3, 0)]
    h = bands(at, full, weights, prior, max(min(512, full.shape[2] // n_week), width))
    schur = rows[1]
    for w, block in moved:
        schur = jnp.where(week == w, block, schur)
    return (h[None], panel, schur.astype(jnp.float32))


def solution(mesh):
    placed = (
        P(WEEK, None, None, (ROW, COL)),
        P(WEEK, None),
        P(WEEK, None),
        P(WEEK, (ROW, COL)),
        P(WEEK, (ROW, COL)),
    )
    return jax.shard_map(
        body,
        mesh=mesh,
        in_specs=placed,
        out_specs=(
            P(WEEK, None, (ROW, COL), None),
            P((ROW, COL), WEEK),
            P((ROW, COL), WEEK),
        ),
        check_vma=False,
    )
```

```python
import functools

import jax
import jax.numpy as jnp
from jax import lax
from jax.experimental import pallas as pl
from jax.experimental.pallas import tpu as pltpu
from jax.sharding import PartitionSpec as P

ROW, COL, WEEK = "row", "col", "week"
DMA = pltpu.SemaphoreType.DMA

UNITS = 5
ALL, MIDDLE, EDGE = range(3)
ORDER = ((0, ALL), (1, ALL), (2, MIDDLE), (4, EDGE), (2, EDGE), (3, ALL))
UNIT_SLOT = ((0, 0, 0, 0), (0, 0, 0, 0), (1, 1, 3, 3), (1, 2, 2, 3), (2, 0, 0, 2))
UNIT_HALF = ((0, 0, 0, 0), (1, 1, 1, 1), (0, 0, 1, 0), (1, 0, 1, 1), (0, 0, 0, 1))
LOCAL = {
    0: ((0, 0),) * 4,
    1: ((0, 1),) * 4,
    2: (None, None, (1, 1), (1, 0)),
    3: (None, None, (2, 1), (1, 1)),
    4: (None, None, None, (2, 1)),
}
FIRST = ((1, 1, 0, 0, 2), (1, 1, 1, 0, 3), (2, 2, 0, 0, 4), (2, 1, 0, 1, 2), (3, 2, 0, 1, 3))
ONWARD = (
    ((2, 1, 3, 0), (3, 1, 3, 1), (4, 1, 4, 2), (4, 2, 2, 4)),
    ((2, 2, 3, 3), (3, 3, 2, 0)),
    ((2, 1, 1, 3), (3, 0, 2, 0)),
    ((2, 2, 1, 0), (3, 2, 1, 1), (4, 2, 4, 2), (4, 1, 2, 4)),
)
RELAY = {0: (1, 1, 4), 3: (0, 2, 4)}
FLOWS = 6


TERMS = (
    (((0, 0, 0), (1, 1, 1), (2, 2, 2)), (), ()),
    (((0, 0, 0), (1, 1, 1), (2, 2, 2)), ((0, 3, 3), (1, 4, 4)), ()),
    (((0, 0, 0), (1, 1, 1)), ((0, 3, 3), (1, 4, 4)), ((0, 2, 5),)),
    (((0, 0, 0),), ((0, 3, 3),), ((0, 2, 5),)),
)
HAVE = tuple(tuple(any(right == slot for band in week for _, right, _ in band) for week in TERMS) for slot in range(5))
SCALE = ((0, 0), (1, 1), (2, 2), (0, 1), (1, 2), (0, 2))


def pick(week, values):
    out = jnp.int32(values[0])
    for k, value in enumerate(values[1:], 1):
        out = jnp.where(week == k, jnp.int32(value), out)
    return out


def contract_last(left, right):
    return lax.dot_general(left, right, (((1,), (1,)), ((), ())), preferred_element_type=jnp.float32)


def gather_kernel(n_row, n_col, x_ref, pivot_ref, weight_ref, f_ref, panel_ref, inner_ref, left_ref,
                  own, put_sem, first_s, first_r, z_s, z_r, pair_s, cross_s, cross_r, y_s, y_r, flow_s, flow_r,
                  low, piv, high, part, came_z, came_y, whole, turned, pan, inn, inn_in, wall,
                  low_s, low_r, piv_s, piv_r, high_s, high_r, loc, half_s, half_r, sum_s, sum_r,
                  all_s, all_r, back_s, back_r, pan_s, pan_r, inn_s, inn_r, wt_s, wt_r, flat, left, left_s):
    row, col, week = lax.axis_index(ROW), lax.axis_index(COL), lax.axis_index(WEEK)
    _, length, width = x_ref.shape
    half = length // 2
    n = n_row * n_col
    peers = range(1, n_col)
    n_week = 4
    pair = row + 1 - 2 * lax.rem(row, 2)
    opp = jnp.where(row < 2, 2, 1)
    end = jnp.where(row < 2, 3, 0)
    inside = (row == 1) | (row == 2)
    outside = (row == 0) | (row == 3)
    middle = (week == 1) | (week == 2)
    edge = (week == 0) | (week == n_week - 1)

    barrier = pltpu.get_barrier_semaphore()
    for k in (1, n_row - 1):
        pl.semaphore_signal(barrier, inc=1, device_id={ROW: lax.rem(row + k, n_row)})
    for k in peers:
        pl.semaphore_signal(barrier, inc=1, device_id={COL: lax.rem(col + k, n_col)})
    for k in range(1, n_week):
        pl.semaphore_signal(barrier, inc=1, device_id={WEEK: lax.rem(week + k, n_week)})
    pl.semaphore_signal(barrier, inc=1, device_id={WEEK: n_week - 1 - week, ROW: pair})
    pl.semaphore_wait(barrier, 2 + (n_col - 1) + (n_week - 1) + 1)

    slots = [pick(week, UNIT_SLOT[u]) for u in range(UNITS)]
    starts = [pl.multiple_of(pick(week, UNIT_HALF[u]) * half, half) for u in range(UNITS)]

    def slab(at_row, at_col):
        return at_row * n_col + at_col

    mine, far = slab(row, col), slab(pair, col)

    def cell(slot, start, s):
        at = pl.ds(pl.multiple_of(s * width, width), width)
        return f_ref.at[slot, pl.ds(start, half), at]

    def place(u, s):
        return cell(slots[u], starts[u], s)

    def active(u, body):
        if u < 4:
            body()
        else:
            pl.when(edge)(body)

    def during(item, body):
        if item[1] == ALL:
            body(item[0])
        else:
            pl.when(middle if item[1] == MIDDLE else edge)(functools.partial(body, item[0]))

    def other(k):
        return lax.rem(col + n_col - k, n_col)

    def remote(ref, s_sem, r_sem, device, to=None):
        return pltpu.make_async_remote_copy(ref, ref if to is None else to, s_sem, r_sem, device_id=device)

    def to_pair(u, s, hop):
        return remote(place(u, s), pair_s.at[u, hop], z_r.at[u, hop], {ROW: pair})

    def to_opp(u, s, hop):
        return remote(place(u, s), z_s.at[u, hop], z_r.at[u, hop], {ROW: opp})

    def cross(u, k):
        return remote(place(u, slab(row, other(k))), cross_s.at[u, k - 1], cross_r.at[u, k - 1], {ROW: pair})

    def side(u, s, hop, k):
        return remote(place(u, s), y_s.at[u, hop, k - 1], y_r.at[u, hop, k - 1], {COL: lax.rem(col + k, n_col)})

    def aside(u, s, hop):
        for k in peers:
            side(u, s, hop, k).start()

    def flows(w, u, s):
        for i, (unit, to_week, to_slot, flow) in enumerate(ONWARD[w]):
            if unit == u:
                start = UNIT_HALF[u][w] * half
                yield remote(cell(UNIT_SLOT[u][w], start, s), flow_s.at[i, s], flow_r.at[flow, s],
                             {WEEK: jnp.int32(to_week)}, cell(to_slot, start, s))

    def spread(u, s, act="start"):
        for w in range(n_week):
            if any(unit == u for unit, *_ in ONWARD[w]):
                @pl.when(week == w)
                def _(w=w):
                    for copy in flows(w, u, s):
                        copy.start() if act == "start" else copy.wait_send()

    def relay(s, act="start"):
        for w, (h, to_week, to_slot) in RELAY.items():
            @pl.when(week == w)
            def _(w=w, h=h, to_week=to_week, to_slot=to_slot):
                ref = cell(2, h * half, s)
                copy = remote(ref, flow_s.at[4, s], flow_r.at[5, s], {WEEK: jnp.int32(to_week)},
                              cell(to_slot, h * half, s))
                if act == "start":
                    remote(ref, flow_s.at[0, s], flow_r.at[0, s], {WEEK: jnp.int32(to_week)}).wait_recv()
                    copy.start()
                else:
                    copy.wait_send()

    def relays(at_row):
        relay(slab(at_row, col))
        for k in peers:
            relay(slab(at_row, other(k)))

    def first(act):
        for w, lag, h, to_week, u in FIRST:
            @pl.when(week == w)
            def _(lag=lag, h=h, to_week=to_week, u=u):
                copy = remote(x_ref.at[lag, pl.ds(h * half, half), :], first_s.at[u], first_r.at[u],
                              {WEEK: jnp.int32(to_week)}, cell(UNIT_SLOT[u][to_week], h * half, mine))
                copy.start() if act == "start" else copy.wait_send()

    def take(u, w):
        lag, h = LOCAL[u][w]
        return pltpu.make_async_copy(x_ref.at[lag, pl.ds(h * half, half), :], own.at[u], put_sem.at[u])

    def put(u):
        return pltpu.make_async_copy(own.at[u], place(u, mine), put_sem.at[u])

    def local(u, body):
        weeks = [w for w in range(n_week) if LOCAL[u][w] is not None]
        if len({LOCAL[u][w] for w in weeks}) == 1 and len(weeks) == n_week:
            body(weeks[0])
        else:
            for w in weeks:
                pl.when(week == w)(functools.partial(body, w))

    slabs = (mine, far)
    side_of = jnp.where(row == 2, 1, 0)
    members = 2 * n_col
    chunk = 2 * length // members
    slices = pivot_ref.shape[0]

    def op_rows(op):
        return pl.ds(op * length, length)

    def low_copy(src, j, op, i, device):
        return remote(src, low_s.at[j, op, i], low_r.at[j, op], device, low.at[j, op_rows(op), :])

    def high_copy(src, j, op, i, device):
        return remote(src, high_s.at[j, op, i], high_r.at[j, op], device, high.at[j, op_rows(op), :])

    def to_week(w):
        return {WEEK: jnp.int32(w)}

    def pivot_out():
        return remote(pivot_ref, piv_s.at[0], piv_r.at[0], {ROW: pair}, piv.at[1])

    def local_copy(src, dst, i):
        return pltpu.make_async_copy(src, dst, loc.at[i])

    def weight_copy(k):
        return remote(weight_ref, wt_s.at[k - 1], wt_r.at[k - 1], {WEEK: lax.rem(week + k, n_week)}, wall.at[week])

    ROLES = ((1, 0, 1, 0, 2, 1), (2, 1, 2, 3, 1, 0))

    def by_role(body):
        for w, *role in ROLES:
            pl.when(week == w)(functools.partial(body, *role))

    def early():
        for k in range(1, n_week):
            weight_copy(k).start()
        pltpu.make_async_copy(weight_ref, wall.at[week], wt_s.at[n_week - 1]).start()

        @pl.when(outside)
        def _():
            by_role(lambda op, lag, *_: low_copy(x_ref.at[lag], 1, op, 0, {ROW: pair}).start())
            pivot_out().start()

        @pl.when(inside)
        def _():
            local_copy(pivot_ref, piv.at[0], 0).start()

            def send(op, lag, near, across, _):
                low_copy(x_ref.at[lag], 0, op, 0, to_week(across)).start()
                low_copy(x_ref.at[lag], 0, op, 1, to_week(near)).start()
                local_copy(x_ref.at[lag], low.at[0, op_rows(op), :], 1).start()

            by_role(send)

    def spread_low():
        def send(op, lag, near, across, theirs):
            ref = low.at[1, op_rows(op), :]
            low_copy(ref, 1, op, 0, to_week(across)).wait_recv()
            low_copy(ref, 1, op, 0, to_week(across)).start()
            low_copy(ref, 1, op, 1, to_week(near)).start()
            for j in range(2):
                ref = low.at[j, op_rows(theirs), :]
                low_copy(ref, j, theirs, 0, to_week(near)).wait_recv()
                low_copy(ref, j, theirs, 0, to_week(near)).start()
            local_copy(x_ref.at[lag], low.at[0, op_rows(op), :], 1).wait()

        by_role(send)

        @pl.when(edge)
        def _():
            for j in range(2):
                for op in range(2):
                    low_copy(low.at[j, op_rows(op), :], j, op, 0, to_week(1)).wait_recv()

        pivot_out().wait_recv()
        local_copy(pivot_ref, piv.at[0], 0).wait()

    def rows_of(m, count=1):
        return pl.ds(pl.multiple_of(m * chunk, chunk), count * chunk)

    def half_copy(k):
        away = rows_of((1 - side_of) * n_col + lax.rem(col + k, n_col))
        return remote(part.at[away, :], half_s.at[k], half_r.at[k], {ROW: opp}, came_z.at[k])

    def sum_copy(k):
        to = lax.rem(col + k, n_col)
        return remote(part.at[rows_of(side_of * n_col + to), :], sum_s.at[k - 1], sum_r.at[k - 1], {COL: to},
                      came_y.at[k - 1])

    me = side_of * n_col + col

    def all_copy(k):
        return remote(whole.at[rows_of(me), :], all_s.at[k - 1], all_r.at[k - 1], {COL: lax.rem(col + k, n_col)})

    def back_copy(k):
        ref = whole.at[rows_of(side_of * n_col + other(k)), :]
        return remote(ref, back_s.at[k], back_r.at[k], {ROW: opp})

    by_turn = (*peers, 0)

    def make_part():
        def fill(m):
            at = rows_of(m)
            total = contract_last(low[0, at, :], piv[0]) + contract_last(low[1, at, :], piv[1])
            part[at, :] = total.astype(part.dtype)

        for k in by_turn:
            fill((1 - side_of) * n_col + lax.rem(col + k, n_col))
            half_copy(k).start()

        @pl.loop(0, n_col)
        def _(m):
            fill(side_of * n_col + m)

    def add_half(k):
        half_copy(k).wait_recv()
        at = rows_of(side_of * n_col + lax.rem(col + k, n_col))
        total = part[at, :].astype(jnp.float32) + came_z[k].astype(jnp.float32)
        part[at, :] = total.astype(part.dtype)
        if k:
            sum_copy(k).start()

    def make_whole():
        for k in peers:
            sum_copy(k).wait_recv()
        total = part[rows_of(me), :].astype(jnp.float32)
        for k in peers:
            total = total + came_y[k - 1].astype(jnp.float32)
        whole[rows_of(me), :] = total.astype(whole.dtype)
        back_copy(0).start()
        for k in peers:
            all_copy(k).start()

    def pass_whole():
        for k in peers:
            all_copy(k).wait_recv()
            back_copy(k).start()

    def column(slot, s):
        return f_ref.at[slot, :, pl.ds(pl.multiple_of(s * width, width), width)]

    def flow_in(flow, s):
        remote(cell(0, 0, s), flow_s.at[0, s], flow_r.at[flow, s], {ROW: pair}).wait_recv()

    def own_flows():
        @pl.when(middle)
        def _():
            for flow in range(FLOWS - 1):
                flow_in(flow, mine)

    def left_out():
        return pltpu.make_async_copy(left, left_ref, left_s.at[3])

    def turn_left():
        for k in range(1, n_week):
            weight_copy(k).wait_recv()
        own_weight().wait()
        for w, by_band in enumerate(TERMS):
            @pl.when(week == w)
            def _(w=w, by_band=by_band):
                items = [item for band in by_band for item in band]
                slots_used = sorted({slot for slot, _, _ in items})
                for slot in slots_used:
                    pltpu.make_async_copy(column(slot, mine), flat.at[slot], left_s.at[slot]).start()
                for slot in slots_used:
                    pltpu.make_async_copy(column(slot, mine), flat.at[slot], left_s.at[slot]).wait()
                for slot, _, p in items:
                    lag = SCALE[p][0]
                    scale = wall[w + lag, SCALE[p][1], :]
                    left[p] = (flat[slot].T.astype(jnp.float32) * scale[None, :]).astype(left.dtype)

        left_out().start()

    def start_high():
        pl.when(middle)(lambda: flow_in(3, far))

        @pl.when(week == 1)
        def _():
            for j, s in enumerate(slabs):
                high_copy(column(0, s), j, 0, 0, to_week(2)).start()
                high_copy(column(0, s), j, 0, 1, to_week(0)).start()
                high_copy(column(1, s), j, 1, 0, to_week(0)).start()
                local_copy(column(0, s), high.at[j, op_rows(0), :], 2 + j).start()
                local_copy(column(1, s), high.at[j, op_rows(1), :], 4 + j).start()

        @pl.when(week == 2)
        def _():
            for j, s in enumerate(slabs):
                high_copy(column(3, s), j, 1, 0, to_week(3)).start()
                local_copy(column(3, s), high.at[j, op_rows(1), :], 4 + j).start()

    def wait_high():
        for j, s in enumerate(slabs):
            @pl.when(week == 1)
            def _(j=j, s=s):
                local_copy(column(0, s), high.at[j, op_rows(0), :], 2 + j).wait()

            @pl.when(week != 1)
            def _(j=j):
                high_copy(high.at[j, op_rows(0), :], j, 0, 0, to_week(3)).wait_recv()

            @pl.when(week == 2)
            def _(j=j):
                high_copy(high.at[j, op_rows(0), :], j, 0, 0, to_week(3)).start()

            @pl.when(middle)
            def _(j=j, s=s):
                local_copy(column(1, s), high.at[j, op_rows(1), :], 4 + j).wait()

            @pl.when(edge)
            def _(j=j):
                high_copy(high.at[j, op_rows(1), :], j, 1, 0, to_week(3)).wait_recv()

    def panel_out():
        return remote(pan.at[1], pan_s.at[0], pan_r.at[0], {ROW: pair}, panel_ref)

    def inner_near(j):
        return remote(inn.at[j], inn_s.at[j], inn_r.at[j], {WEEK: jnp.where(week == 0, 1, 2)}, inn_in.at[j])

    def inner_far(j, i):
        device = {WEEK: jnp.int32(1)} if j == 0 else {WEEK: jnp.int32(1), ROW: pair}
        return remote(inn.at[j], inn_s.at[j], inn_r.at[2 + i], device, inner_ref.at[i])

    def own_weight():
        return pltpu.make_async_copy(weight_ref, wall.at[week], wt_s.at[n_week - 1])

    def turn_high():
        wait_high()
        step = min(length, 512)
        for j in range(2):
            for op in range(2):
                for at in range(0, length, step):
                    rows = pl.ds(op * length + at, step)
                    flat = high[j, rows, :].T.astype(jnp.float32) * wall[1 + op, 1 + op, pl.ds(at, step)][None, :]
                    turned[j, :, rows] = flat.astype(turned.dtype)

    tile = min(slices, 256)

    def wait_whole():
        for k in range(n_col):
            back_copy(k).wait_recv()

    def make_panel(j):
        @pl.loop(0, slices // tile)
        def _(i):
            at = pl.ds(pl.multiple_of(i * tile, tile), tile)
            pan[j, :, at] = jnp.dot(turned[j], whole[:, at], preferred_element_type=jnp.float32).astype(pan.dtype)

        if j == 0:
            local_copy(pan.at[0], panel_ref, 0).start()
        else:
            panel_out().start()

    def make_inner(j):
        @pl.loop(0, 2 * length // tile)
        def _(i):
            at = pl.ds(pl.multiple_of(i * tile, tile), tile)
            inn[j, :, at] = contract_last(pan[j], whole[at, :]).astype(inn.dtype)

        pl.when(edge)(lambda: inner_near(j).start())

    def join_inner(j):
        @pl.when(middle)
        def _():
            inner_near(j).wait_recv()
            for op in range(2):
                at = op_rows(op)
                both = inn[j, :, at].astype(jnp.float32) + inn_in[j, :, at].astype(jnp.float32)
                inn[j, :, at] = (both * wall[1 + op, 1 + op, :][None, :]).astype(inn.dtype)

            pl.when(week == 2)(lambda: inner_far(j, 1).start())

            @pl.when(week == 1)
            def _():
                if j == 1:
                    inner_far(1, 0).start()
                else:
                    local_copy(inn.at[0], inner_ref.at[0], 1).start()

    first("start")
    for u in range(UNITS):
        local(u, lambda w, u=u: take(u, w).start())
    early()
    for u in range(UNITS):
        def move(w, u=u):
            take(u, w).wait()
            put(u).start()

        local(u, move)

    def begin(u):
        local(u, lambda w: put(u).wait())
        for _, _, _, week_of, unit in FIRST:
            if unit == u:
                @pl.when(week == week_of)
                def _():
                    remote(place(u, mine), first_s.at[u], first_r.at[u], {ROW: pair}).wait_recv()

        @pl.when(inside)
        def _():
            to_opp(u, mine, 0).start()
            to_pair(u, mine, 0).start()

        pl.when(outside)(lambda: to_pair(u, mine, 1).start())
        aside(u, mine, 0)
        pl.when(outside)(lambda: spread(u, mine))

    for item in ORDER:
        during(item, begin)

    def from_side(item, at_row, hop, onward=None):
        def body(u):
            for k in peers:
                side(u, mine, hop, k).wait_recv()
                if onward is not None:
                    onward(u, k)
                spread(u, slab(at_row, other(k)))

        during(item, body)

    def arrived(item, s, hop, then):
        def body(u):
            to_pair(u, s, hop).wait_recv()
            then(u)
            spread(u, s)

        during(item, body)

    @pl.when(outside)
    def _():
        for item in ORDER:
            from_side(item, row, 0, lambda u, k: cross(u, k).start())
        for hop, at_row in enumerate((pair, opp, end)):
            s = slab(at_row, col)
            for i, item in enumerate(ORDER):
                arrived(item, s, hop, lambda u, s=s, hop=hop: aside(u, s, hop + 1))
                if hop:
                    from_side(item, (pair, opp)[hop - 1], hop)
                if hop == 2 and i == 3:
                    relays(row)
                    relays(pair)
                    own_flows()
                    turn_left()
                if hop == 2 and i >= 2:
                    from_side(ORDER[i - 2], end, 3)
        relays(opp)
        for item in ORDER[-2:]:
            from_side(item, end, 3)
        relays(end)

    @pl.when(inside)
    def _():
        def cross_in(item):
            def body(u):
                for k in peers:
                    cross(u, k).wait_recv()
                    spread(u, slab(pair, other(k)))

            during(item, body)

        def hand(item, at_row, hop):
            s = slab(at_row, col)

            def then(u):
                to_pair(u, s, hop).start()
                aside(u, s, hop)

            arrived(item, s, 2 * hop - 2, then)

        def near_one(item):
            hand(item, opp, 1)

        def far_one(item):
            hand(item, end, 2)

        def pass_on(item):
            during(item, lambda u: to_opp(u, far, 2).start())

        def outer_one(item):
            arrived(item, far, 1, lambda u: None)

        start, middle_part, last = ORDER[:2], ORDER[2:4], ORDER[4:]
        for item in start:
            near_one(item)
        spread_low()
        make_part()
        for item in ORDER:
            during(item, lambda u: spread(u, mine))
        for item in middle_part:
            near_one(item)
        for item in start:
            outer_one(item)
            pass_on(item)
        for k in peers:
            add_half(k)
        for item in last:
            near_one(item)
        for item in (*middle_part, *last):
            outer_one(item)
        for item in ORDER:
            from_side(item, row, 0)
        add_half(0)
        make_whole()
        far_one(start[0])
        for item in middle_part:
            pass_on(item)
        far_one(start[1])
        pass_whole()
        for item in last:
            pass_on(item)
        own_flows()
        start_high()
        for item in ORDER:
            from_side(item, opp, 1)
        for item in ORDER:
            cross_in(item)
        relays(row)
        turn_left()
        for item in middle_part:
            far_one(item)
        for item in start:
            from_side(item, end, 2)
        turn_high()
        wait_whole()
        make_panel(1)
        make_inner(1)
        far_one(last[0])
        for item in middle_part:
            from_side(item, end, 2)
        make_panel(0)
        make_inner(0)
        for item in last[1:]:
            far_one(item)
        relays(pair)
        join_inner(1)
        join_inner(0)
        relays(opp)
        for item in last:
            from_side(item, end, 2)
        relays(end)

    @pl.when(middle)
    def _():
        for s in range(n):
            for flow in range(FLOWS):
                def arrive(s=s, flow=flow):
                    ref = cell(0, 0, s)
                    remote(ref, flow_s.at[0, s], flow_r.at[flow, s], {ROW: pair}).wait_recv()

                if flow == 3:
                    pl.when((mine != s) & (outside | (far != s)))(arrive)
                elif flow < FLOWS - 1:
                    pl.when(mine != s)(arrive)
                else:
                    arrive()

    @pl.when(week == 1)
    def _():
        inner_far(1, 1).wait_recv()
        pl.when(outside)(lambda: inner_far(1, 0).wait_recv())

    @pl.when(outside)
    def _():
        panel_out().wait_recv()
        by_role(lambda op, lag, *_: low_copy(x_ref.at[lag], 1, op, 0, {ROW: pair}).wait_send())
        pivot_out().wait_send()

    for k in range(1, n_week):
        weight_copy(k).wait_send()

    @pl.when(inside)
    def _():
        def sent(op, lag, near, across, theirs):
            for j in range(2):
                for i in range(2):
                    low_copy(x_ref.at[0], j, op, i, to_week(0)).wait_send()
                low_copy(x_ref.at[0], j, theirs, 0, to_week(0)).wait_send()

        by_role(sent)
        for k in range(n_col):
            half_copy(k).wait_send()
        for k in peers:
            sum_copy(k).wait_send()
            all_copy(k).wait_send()
        for k in range(n_col):
            back_copy(k).wait_send()

        @pl.when(week == 1)
        def _():
            for j, s in enumerate(slabs):
                high_copy(column(0, s), j, 0, 0, to_week(2)).wait_send()
                high_copy(column(0, s), j, 0, 1, to_week(0)).wait_send()
                high_copy(column(1, s), j, 1, 0, to_week(0)).wait_send()

        @pl.when(week == 2)
        def _():
            for j, s in enumerate(slabs):
                high_copy(column(3, s), j, 1, 0, to_week(3)).wait_send()
                high_copy(high.at[j, op_rows(0), :], j, 0, 0, to_week(3)).wait_send()

        local_copy(pan.at[0], panel_ref, 0).wait()
        panel_out().wait_send()
        for j in range(2):
            pl.when(edge)(lambda j=j: inner_near(j).wait_send())
            pl.when(week == 2)(lambda j=j: inner_far(j, 1).wait_send())

        @pl.when(week == 1)
        def _():
            inner_far(1, 0).wait_send()
            local_copy(inn.at[0], inner_ref.at[0], 1).wait()

    first("wait")
    for u in range(UNITS):
        def finish(u=u):
            for k in peers:
                for hop in range(3):
                    side(u, mine, hop, k).wait_send()

            @pl.when(outside)
            def _():
                to_pair(u, mine, 1).wait_send()
                for k in peers:
                    side(u, mine, 3, k).wait_send()
                    cross(u, k).wait_send()

            @pl.when(inside)
            def _():
                to_opp(u, mine, 0).wait_send()
                to_opp(u, far, 2).wait_send()
                for hop in range(3):
                    to_pair(u, mine, hop).wait_send()

        active(u, finish)
        if u >= 2:
            for s in range(n):
                spread(u, s, "wait")
    for s in range(n):
        relay(s, "wait")
    left_out().wait()


def gather(x, pivot, weight, collective_id):
    n_row, n_col = lax.axis_size(ROW), lax.axis_size(COL)
    _, length, width = x.shape
    slices = pivot.shape[0]
    n = n_row * n_col
    assert n_row == 4 and lax.axis_size(WEEK) == 4
    sides = (UNITS, n_col - 1)
    vmem = functools.partial(lambda *shape: pltpu.VMEM(shape, x.dtype))
    sent = length * width * 2 * (n - 1) * 9 // 4
    hbm = pl.BlockSpec(memory_space=pl.ANY)
    return pl.pallas_call(
        functools.partial(gather_kernel, n_row, n_col),
        out_shape=(
            jax.ShapeDtypeStruct((5, length, width * n), x.dtype),
            jax.ShapeDtypeStruct((width, slices), x.dtype),
            jax.ShapeDtypeStruct((2, width, 2 * length), x.dtype),
            jax.ShapeDtypeStruct((len(SCALE), width, length), x.dtype),
        ),
        in_specs=[hbm] * 3,
        out_specs=(hbm,) * 4,
        scratch_shapes=[
            pltpu.VMEM((UNITS, length // 2, width), x.dtype), DMA((UNITS,)), DMA((UNITS,)), DMA((UNITS,)),
            DMA((UNITS, 3)), DMA((UNITS, 3)), DMA((UNITS, 3)), DMA(sides), DMA(sides),
            DMA((UNITS, 4, n_col - 1)), DMA((UNITS, 4, n_col - 1)), DMA((5, n)), DMA((FLOWS, n)),
            vmem(2, 2 * length, width), vmem(2, slices, width), vmem(2, 2 * length, width),
            vmem(2 * length, slices), vmem(n_col, length // n_col, slices),
            vmem(n_col - 1, length // n_col, slices),
            vmem(2 * length, slices),
            vmem(2, width, 2 * length), vmem(2, width, slices), vmem(2, width, 2 * length),
            vmem(2, width, 2 * length), pltpu.VMEM((4, *weight.shape), weight.dtype),
            DMA((2, 2, 2)), DMA((2, 2)), DMA((1,)), DMA((1,)), DMA((2, 2, 2)), DMA((2, 2)), DMA((6,)),
            DMA((n_col,)), DMA((n_col,)), DMA((n_col - 1,)), DMA((n_col - 1,)),
            DMA((n_col - 1,)), DMA((n_col - 1,)), DMA((n_col,)), DMA((n_col,)),
            DMA((1,)), DMA((1,)), DMA((2,)), DMA((4,)), DMA((4,)), DMA((3,)),
            vmem(3, length, width), vmem(len(SCALE), width, length), DMA((4,)),
        ],
        compiler_params=pltpu.CompilerParams(
            collective_id=collective_id, has_side_effects=True, vmem_limit_bytes=60 << 20),
        cost_estimate=pl.CostEstimate(flops=0, bytes_accessed=sent * 8, transcendentals=0),
    )(x, pivot, weight)


def when_tile(at_ref, tile, columns, width, body):
    first = at_ref[1] * width

    @pl.when(first // columns == tile)
    def _():
        body(pl.ds(pl.multiple_of(lax.rem(first, columns), width), width))


def diagonal(prior_ref, width):
    rows = lax.broadcasted_iota(jnp.int32, (width, width), 0)
    cols = lax.broadcasted_iota(jnp.int32, (width, width), 1)
    return jnp.where(rows == cols, prior_ref[:, :1], 0.0)


def bands_kernel(at_ref, left_ref, prior_ref, *refs):
    full_refs, out_ref = refs[:5], refs[5]
    week = at_ref[0]
    tile = pl.program_id(0)
    width = left_ref.shape[1]
    columns = out_ref.shape[2]

    for w, by_band in enumerate(TERMS):
        @pl.when(week == w)
        def _(by_band=by_band):
            for i, band in enumerate(by_band):
                if band:
                    total = None
                    for _, right, p in band:
                        term = jnp.dot(left_ref[p], full_refs[right][...], preferred_element_type=jnp.float32)
                        total = term if total is None else total + term
                    out_ref[i] = total
                else:
                    out_ref[i] = jnp.zeros(out_ref.shape[1:], out_ref.dtype)

    def add(at):
        out_ref[0, :, at] += diagonal(prior_ref, width)

    when_tile(at_ref, tile, columns, width, add)


def bands(at, full, left, prior, columns):
    slots, length, regions = full.shape
    width = prior.shape[0]

    def right(slot):
        def index(j, at):
            here = functools.reduce(jnp.logical_or, [at[0] == w for w in range(4) if HAVE[slot][w]])
            return slot, 0, jnp.where(here, j, 0)

        return pl.BlockSpec((None, length, columns), index)

    return pl.pallas_call(
        bands_kernel,
        out_shape=jax.ShapeDtypeStruct((3, width, regions), jnp.float32),
        grid_spec=pltpu.PrefetchScalarGridSpec(
            num_scalar_prefetch=1,
            grid=(regions // columns,),
            in_specs=[
                pl.BlockSpec(left.shape, lambda j, at: (0, 0, 0), pipeline_mode=pl.Buffered(1)),
                pl.BlockSpec(prior.shape, lambda j, at: (0, 0)),
                *[right(slot) for slot in range(slots)],
            ],
            out_specs=pl.BlockSpec((3, width, columns), lambda j, at: (0, 0, j)),
        ),
        compiler_params=pltpu.CompilerParams(dimension_semantics=("arbitrary",), vmem_limit_bytes=60 << 20),
        cost_estimate=pl.CostEstimate(
            flops=10 * width * length * regions, bytes_accessed=full.size * 2 + 12 * width * regions,
            transcendentals=0),
    )(at, left, prior, *[full] * slots)


def schur_kernel(at_ref, left_ref, prior_ref, inner_ref, *refs):
    full_refs, out_refs, turned, total = refs[:3], refs[3:-2], refs[-2], refs[-1]
    week = at_ref[0]
    tile = pl.program_id(0)
    slots, width, length = left_ref.shape
    columns = total.shape[1]
    tiles = pl.num_programs(0) // len(out_refs)

    @pl.when(week == 1)
    def _():
        @pl.when(tile == 0)
        def _():
            for k in range(2):
                at = pl.ds(k * length, length)
                inner = inner_ref[0, :, at].astype(jnp.float32) + inner_ref[1, :, at].astype(jnp.float32)
                turned[k] = (left_ref[k].astype(jnp.float32) - inner).astype(turned.dtype)

        block = jnp.dot(turned[0], full_refs[0][...], preferred_element_type=jnp.float32)
        block = block + jnp.dot(turned[1], full_refs[1][...], preferred_element_type=jnp.float32)
        block = block + jnp.dot(left_ref[2], full_refs[2][...], preferred_element_type=jnp.float32)
        total[...] = block

        def add(at):
            total[:, at] += diagonal(prior_ref, width)

        when_tile(at_ref, tile, columns, width, add)
        for q, out_ref in enumerate(out_refs):
            @pl.when(tile // tiles == q)
            def _(out_ref=out_ref):
                out_ref[...] = total[...].astype(out_ref.dtype)


def schur_rows(at, full, left, prior, inner, columns):
    _, length, regions = full.shape
    width = prior.shape[0]
    quarters = 4
    columns = min(columns, regions // quarters)
    tiles = regions // quarters // columns
    whole = pl.Buffered(1)

    def part(q):
        return pl.BlockSpec((width, columns), lambda j, at: (0, jnp.clip(j - q * tiles, 0, tiles - 1)))

    def right(slot):
        return pl.BlockSpec((None, length, columns), lambda j, at: (slot, 0, jnp.where(at[0] == 1, j, 0)))

    return pl.pallas_call(
        schur_kernel,
        out_shape=[jax.ShapeDtypeStruct((width, regions // quarters), jnp.bfloat16)] * quarters,
        grid_spec=pltpu.PrefetchScalarGridSpec(
            num_scalar_prefetch=1,
            grid=(regions // columns,),
            in_specs=[
                pl.BlockSpec((3, width, length), lambda j, at: (0, 0, 0), pipeline_mode=whole),
                pl.BlockSpec(prior.shape, lambda j, at: (0, 0)),
                pl.BlockSpec(inner.shape, lambda j, at: (0, 0, 0), pipeline_mode=whole),
                *[right(slot) for slot in range(3)],
            ],
            out_specs=[part(q) for q in range(quarters)],
            scratch_shapes=[pltpu.VMEM((2, width, length), full.dtype), pltpu.VMEM((width, columns), jnp.float32)],
        ),
        compiler_params=pltpu.CompilerParams(dimension_semantics=("arbitrary",), vmem_limit_bytes=60 << 20),
        cost_estimate=pl.CostEstimate(
            flops=6 * width * length * regions, bytes_accessed=6 * length * regions, transcendentals=0),
    )(at, left, prior, inner, *[full] * 3)


def body(sensitivity, reach, obs_weight, prior_precision, pivot_solve):
    week = lax.axis_index(WEEK)
    n_week, n_col = lax.axis_size(WEEK), lax.axis_size(COL)
    local = sensitivity[0]
    lags, length, width = local.shape
    mine = lax.axis_index(ROW) * n_col + lax.axis_index(COL)

    lag = jnp.arange(8)[:, None]
    own_weight = jnp.where((reach >= lag) & (week >= lag) & (lag < lags), obs_weight, 0.0)
    full, panel, inner, left = gather(local, pivot_solve, own_weight, 0)
    at = jnp.stack([week, mine]).astype(jnp.int32)
    prior = jnp.broadcast_to(prior_precision[0][:, None], (width, 128))
    columns = max(min(1024, full.shape[2] // n_week), width)
    rows = schur_rows(at, full, left, prior, inner, columns)
    moved = [(w, lax.ppermute(rows[w], WEEK, [(1, w)])) for w in (2, 3, 0)]
    h = bands(at, full, left, prior, max(min(512, full.shape[2] // n_week), width))
    schur = rows[1]
    for w, block in moved:
        schur = jnp.where(week == w, block, schur)
    return (h[None], panel, schur.astype(jnp.float32))


def solution(mesh):
    placed = (
        P(WEEK, None, None, (ROW, COL)),
        P(WEEK, None),
        P(WEEK, None),
        P(WEEK, (ROW, COL)),
        P(WEEK, (ROW, COL)),
    )
    return jax.shard_map(
        body,
        mesh=mesh,
        in_specs=placed,
        out_specs=(
            P(WEEK, None, (ROW, COL), None),
            P((ROW, COL), WEEK),
            P((ROW, COL), WEEK),
        ),
        check_vma=False,
    )
```

```python
import functools

import jax
import jax.numpy as jnp
from jax import lax
from jax.experimental import pallas as pl
from jax.experimental.pallas import tpu as pltpu
from jax.sharding import PartitionSpec as P

ROW, COL, WEEK = "row", "col", "week"
DMA = pltpu.SemaphoreType.DMA

UNITS = 5
ALL, MIDDLE, EDGE = range(3)
ORDER = ((0, ALL), (1, ALL), (2, MIDDLE), (4, EDGE), (2, EDGE), (3, ALL))
UNIT_SLOT = ((0, 0, 0, 0), (0, 0, 0, 0), (1, 1, 3, 3), (1, 2, 2, 3), (2, 0, 0, 2))
UNIT_HALF = ((0, 0, 0, 0), (1, 1, 1, 1), (0, 0, 1, 0), (1, 0, 1, 1), (0, 0, 0, 1))
LOCAL = {
    0: ((0, 0),) * 4,
    1: ((0, 1),) * 4,
    2: (None, None, (1, 1), (1, 0)),
    3: (None, None, (2, 1), (1, 1)),
    4: (None, None, None, (2, 1)),
}
FIRST = ((1, 1, 0, 0, 2), (1, 1, 1, 0, 3), (2, 2, 0, 0, 4), (2, 1, 0, 1, 2), (3, 2, 0, 1, 3))
ONWARD = (
    ((2, 1, 3, 0), (3, 1, 3, 1), (4, 1, 4, 2), (4, 2, 2, 4)),
    ((2, 2, 3, 3), (3, 3, 2, 0)),
    ((2, 1, 1, 3), (3, 0, 2, 0)),
    ((2, 2, 1, 0), (3, 2, 1, 1), (4, 2, 4, 2), (4, 1, 2, 4)),
)
RELAY = {0: (1, 1, 4), 3: (0, 2, 4)}
FLOWS = 6


TERMS = (
    (((0, 0, 0), (1, 1, 1), (2, 2, 2)), (), ()),
    (((0, 0, 0), (1, 1, 1), (2, 2, 2)), ((0, 3, 3), (1, 4, 4)), ()),
    (((0, 0, 0), (1, 1, 1)), ((0, 3, 3), (1, 4, 4)), ((0, 2, 5),)),
    (((0, 0, 0),), ((0, 3, 3),), ((0, 2, 5),)),
)
HAVE = tuple(tuple(any(right == slot for band in week for _, right, _ in band) for week in TERMS) for slot in range(5))
SCALE = ((0, 0), (1, 1), (2, 2), (0, 1), (1, 2), (0, 2))


def pick(week, values):
    out = jnp.int32(values[0])
    for k, value in enumerate(values[1:], 1):
        out = jnp.where(week == k, jnp.int32(value), out)
    return out


def contract_last(left, right):
    return lax.dot_general(left, right, (((1,), (1,)), ((), ())), preferred_element_type=jnp.float32)


def gather_kernel(n_row, n_col, x_ref, pivot_ref, weight_ref, f_ref, panel_ref, inner_ref, left_ref,
                  own, put_sem, first_s, first_r, z_s, z_r, pair_s, cross_s, cross_r, y_s, y_r, flow_s, flow_r,
                  low, piv, high, part, came_z, came_y, whole, turned, pan, inn, inn_in, wall,
                  low_s, low_r, piv_s, piv_r, high_s, high_r, loc, half_s, half_r, sum_s, sum_r,
                  all_s, all_r, back_s, back_r, pan_s, pan_r, inn_s, inn_r, wt_s, wt_r, flat, left, left_s):
    row, col, week = lax.axis_index(ROW), lax.axis_index(COL), lax.axis_index(WEEK)
    _, length, width = x_ref.shape
    half = length // 2
    n = n_row * n_col
    peers = range(1, n_col)
    n_week = 4
    pair = row + 1 - 2 * lax.rem(row, 2)
    opp = jnp.where(row < 2, 2, 1)
    end = jnp.where(row < 2, 3, 0)
    inside = (row == 1) | (row == 2)
    outside = (row == 0) | (row == 3)
    middle = (week == 1) | (week == 2)
    edge = (week == 0) | (week == n_week - 1)

    barrier = pltpu.get_barrier_semaphore()
    for k in (1, n_row - 1):
        pl.semaphore_signal(barrier, inc=1, device_id={ROW: lax.rem(row + k, n_row)})
    for k in peers:
        pl.semaphore_signal(barrier, inc=1, device_id={COL: lax.rem(col + k, n_col)})
    for k in range(1, n_week):
        pl.semaphore_signal(barrier, inc=1, device_id={WEEK: lax.rem(week + k, n_week)})
    pl.semaphore_signal(barrier, inc=1, device_id={WEEK: n_week - 1 - week, ROW: pair})
    pl.semaphore_wait(barrier, 2 + (n_col - 1) + (n_week - 1) + 1)

    slots = [pick(week, UNIT_SLOT[u]) for u in range(UNITS)]
    starts = [pl.multiple_of(pick(week, UNIT_HALF[u]) * half, half) for u in range(UNITS)]

    def slab(at_row, at_col):
        return at_row * n_col + at_col

    mine, far = slab(row, col), slab(pair, col)

    def cell(slot, start, s):
        at = pl.ds(pl.multiple_of(s * width, width), width)
        return f_ref.at[slot, pl.ds(start, half), at]

    def place(u, s):
        return cell(slots[u], starts[u], s)

    def active(u, body):
        if u < 4:
            body()
        else:
            pl.when(edge)(body)

    def during(item, body):
        if item[1] == ALL:
            body(item[0])
        else:
            pl.when(middle if item[1] == MIDDLE else edge)(functools.partial(body, item[0]))

    def other(k):
        return lax.rem(col + n_col - k, n_col)

    def remote(ref, s_sem, r_sem, device, to=None):
        return pltpu.make_async_remote_copy(ref, ref if to is None else to, s_sem, r_sem, device_id=device)

    def to_pair(u, s, hop):
        return remote(place(u, s), pair_s.at[u, hop], z_r.at[u, hop], {ROW: pair})

    def to_opp(u, s, hop):
        return remote(place(u, s), z_s.at[u, hop], z_r.at[u, hop], {ROW: opp})

    def cross(u, k):
        return remote(place(u, slab(row, other(k))), cross_s.at[u, k - 1], cross_r.at[u, k - 1], {ROW: pair})

    def side(u, s, hop, k):
        return remote(place(u, s), y_s.at[u, hop, k - 1], y_r.at[u, hop, k - 1], {COL: lax.rem(col + k, n_col)})

    def aside(u, s, hop):
        for k in peers:
            side(u, s, hop, k).start()

    def flows(w, u, s):
        for i, (unit, to_week, to_slot, flow) in enumerate(ONWARD[w]):
            if unit == u:
                start = UNIT_HALF[u][w] * half
                yield remote(cell(UNIT_SLOT[u][w], start, s), flow_s.at[i, s], flow_r.at[flow, s],
                             {WEEK: jnp.int32(to_week)}, cell(to_slot, start, s))

    def spread(u, s, act="start"):
        for w in range(n_week):
            if any(unit == u for unit, *_ in ONWARD[w]):
                @pl.when(week == w)
                def _(w=w):
                    for copy in flows(w, u, s):
                        copy.start() if act == "start" else copy.wait_send()

    def relay(s, act="start"):
        for w, (h, to_week, to_slot) in RELAY.items():
            @pl.when(week == w)
            def _(w=w, h=h, to_week=to_week, to_slot=to_slot):
                ref = cell(2, h * half, s)
                copy = remote(ref, flow_s.at[4, s], flow_r.at[5, s], {WEEK: jnp.int32(to_week)},
                              cell(to_slot, h * half, s))
                if act == "start":
                    remote(ref, flow_s.at[0, s], flow_r.at[0, s], {WEEK: jnp.int32(to_week)}).wait_recv()
                    copy.start()
                else:
                    copy.wait_send()

    def relays(at_row):
        relay(slab(at_row, col))
        for k in peers:
            relay(slab(at_row, other(k)))

    def first(act):
        for w, lag, h, to_week, u in FIRST:
            @pl.when(week == w)
            def _(lag=lag, h=h, to_week=to_week, u=u):
                copy = remote(x_ref.at[lag, pl.ds(h * half, half), :], first_s.at[u], first_r.at[u],
                              {WEEK: jnp.int32(to_week)}, cell(UNIT_SLOT[u][to_week], h * half, mine))
                copy.start() if act == "start" else copy.wait_send()

    def take(u, w):
        lag, h = LOCAL[u][w]
        return pltpu.make_async_copy(x_ref.at[lag, pl.ds(h * half, half), :], own.at[u], put_sem.at[u])

    def put(u):
        return pltpu.make_async_copy(own.at[u], place(u, mine), put_sem.at[u])

    def local(u, body):
        weeks = [w for w in range(n_week) if LOCAL[u][w] is not None]
        if len({LOCAL[u][w] for w in weeks}) == 1 and len(weeks) == n_week:
            body(weeks[0])
        else:
            for w in weeks:
                pl.when(week == w)(functools.partial(body, w))

    slabs = (mine, far)
    side_of = jnp.where(row == 2, 1, 0)
    members = 2 * n_col
    chunk = 2 * length // members
    slices = pivot_ref.shape[0]

    def op_rows(op):
        return pl.ds(op * length, length)

    def low_copy(src, j, op, i, device):
        return remote(src, low_s.at[j, op, i], low_r.at[j, op], device, low.at[j, op_rows(op), :])

    def high_copy(src, j, op, i, device):
        return remote(src, high_s.at[j, op, i], high_r.at[j, op], device, high.at[j, op_rows(op), :])

    def to_week(w):
        return {WEEK: jnp.int32(w)}

    def pivot_out():
        return remote(pivot_ref, piv_s.at[0], piv_r.at[0], {ROW: pair}, piv.at[1])

    def local_copy(src, dst, i):
        return pltpu.make_async_copy(src, dst, loc.at[i])

    def weight_copy(k):
        return remote(weight_ref, wt_s.at[k - 1], wt_r.at[k - 1], {WEEK: lax.rem(week + k, n_week)}, wall.at[week])

    ROLES = ((1, 0, 1, 0, 2, 1), (2, 1, 2, 3, 1, 0))

    def by_role(body):
        for w, *role in ROLES:
            pl.when(week == w)(functools.partial(body, *role))

    def early():
        for k in range(1, n_week):
            weight_copy(k).start()
        pltpu.make_async_copy(weight_ref, wall.at[week], wt_s.at[n_week - 1]).start()

        @pl.when(outside)
        def _():
            by_role(lambda op, lag, *_: low_copy(x_ref.at[lag], 1, op, 0, {ROW: pair}).start())
            pivot_out().start()

        @pl.when(inside)
        def _():
            local_copy(pivot_ref, piv.at[0], 0).start()

            def send(op, lag, near, across, _):
                low_copy(x_ref.at[lag], 0, op, 0, to_week(across)).start()
                low_copy(x_ref.at[lag], 0, op, 1, to_week(near)).start()
                local_copy(x_ref.at[lag], low.at[0, op_rows(op), :], 1).start()

            by_role(send)

    def spread_low():
        def send(op, lag, near, across, theirs):
            ref = low.at[1, op_rows(op), :]
            low_copy(ref, 1, op, 0, to_week(across)).wait_recv()
            low_copy(ref, 1, op, 0, to_week(across)).start()
            low_copy(ref, 1, op, 1, to_week(near)).start()
            for j in range(2):
                ref = low.at[j, op_rows(theirs), :]
                low_copy(ref, j, theirs, 0, to_week(near)).wait_recv()
                low_copy(ref, j, theirs, 0, to_week(near)).start()
            local_copy(x_ref.at[lag], low.at[0, op_rows(op), :], 1).wait()

        by_role(send)

        @pl.when(edge)
        def _():
            for j in range(2):
                for op in range(2):
                    low_copy(low.at[j, op_rows(op), :], j, op, 0, to_week(1)).wait_recv()

        pivot_out().wait_recv()
        local_copy(pivot_ref, piv.at[0], 0).wait()

    def rows_of(m, count=1):
        return pl.ds(pl.multiple_of(m * chunk, chunk), count * chunk)

    def half_copy(k):
        away = rows_of((1 - side_of) * n_col + lax.rem(col + k, n_col))
        return remote(part.at[away, :], half_s.at[k], half_r.at[k], {ROW: opp}, came_z.at[k])

    def sum_copy(k):
        to = lax.rem(col + k, n_col)
        return remote(part.at[rows_of(side_of * n_col + to), :], sum_s.at[k - 1], sum_r.at[k - 1], {COL: to},
                      came_y.at[k - 1])

    me = side_of * n_col + col

    def all_copy(k):
        return remote(whole.at[rows_of(me), :], all_s.at[k - 1], all_r.at[k - 1], {COL: lax.rem(col + k, n_col)})

    def back_copy(k):
        ref = whole.at[rows_of(side_of * n_col + other(k)), :]
        return remote(ref, back_s.at[k], back_r.at[k], {ROW: opp})

    by_turn = (*peers, 0)

    def make_part():
        def fill(m):
            at = rows_of(m)
            total = contract_last(low[0, at, :], piv[0]) + contract_last(low[1, at, :], piv[1])
            part[at, :] = total.astype(part.dtype)

        for k in by_turn:
            fill((1 - side_of) * n_col + lax.rem(col + k, n_col))
            half_copy(k).start()

        @pl.loop(0, n_col)
        def _(m):
            fill(side_of * n_col + m)

    def add_half(k):
        half_copy(k).wait_recv()
        at = rows_of(side_of * n_col + lax.rem(col + k, n_col))
        total = part[at, :].astype(jnp.float32) + came_z[k].astype(jnp.float32)
        part[at, :] = total.astype(part.dtype)
        if k:
            sum_copy(k).start()

    def make_whole():
        for k in peers:
            sum_copy(k).wait_recv()
        total = part[rows_of(me), :].astype(jnp.float32)
        for k in peers:
            total = total + came_y[k - 1].astype(jnp.float32)
        whole[rows_of(me), :] = total.astype(whole.dtype)
        back_copy(0).start()
        for k in peers:
            all_copy(k).start()

    def pass_whole():
        for k in peers:
            all_copy(k).wait_recv()
            back_copy(k).start()

    def column(slot, s):
        return f_ref.at[slot, :, pl.ds(pl.multiple_of(s * width, width), width)]

    def flow_in(flow, s):
        remote(cell(0, 0, s), flow_s.at[0, s], flow_r.at[flow, s], {ROW: pair}).wait_recv()

    def own_flows():
        @pl.when(middle)
        def _():
            for flow in range(FLOWS - 1):
                flow_in(flow, mine)

    def left_out():
        return pltpu.make_async_copy(left, left_ref, left_s.at[3])

    def turn_left():
        for k in range(1, n_week):
            weight_copy(k).wait_recv()
        own_weight().wait()
        for w, by_band in enumerate(TERMS):
            @pl.when(week == w)
            def _(w=w, by_band=by_band):
                items = [item for band in by_band for item in band]
                slots_used = sorted({slot for slot, _, _ in items})
                for slot in slots_used:
                    pltpu.make_async_copy(column(slot, mine), flat.at[slot], left_s.at[slot]).start()
                for slot in slots_used:
                    pltpu.make_async_copy(column(slot, mine), flat.at[slot], left_s.at[slot]).wait()
                for slot, _, p in items:
                    lag = SCALE[p][0]
                    scale = wall[w + lag, SCALE[p][1], :]
                    left[p] = (flat[slot].T.astype(jnp.float32) * scale[None, :]).astype(left.dtype)

        left_out().start()

    def start_high():
        pl.when(middle)(lambda: flow_in(3, far))

        @pl.when(week == 1)
        def _():
            for j, s in enumerate(slabs):
                high_copy(column(0, s), j, 0, 0, to_week(2)).start()
                high_copy(column(0, s), j, 0, 1, to_week(0)).start()
                high_copy(column(1, s), j, 1, 0, to_week(0)).start()
                local_copy(column(0, s), high.at[j, op_rows(0), :], 2 + j).start()
                local_copy(column(1, s), high.at[j, op_rows(1), :], 4 + j).start()

        @pl.when(week == 2)
        def _():
            for j, s in enumerate(slabs):
                high_copy(column(3, s), j, 1, 0, to_week(3)).start()
                local_copy(column(3, s), high.at[j, op_rows(1), :], 4 + j).start()

    def wait_high():
        for j, s in enumerate(slabs):
            @pl.when(week == 1)
            def _(j=j, s=s):
                local_copy(column(0, s), high.at[j, op_rows(0), :], 2 + j).wait()

            @pl.when(week != 1)
            def _(j=j):
                high_copy(high.at[j, op_rows(0), :], j, 0, 0, to_week(3)).wait_recv()

            @pl.when(week == 2)
            def _(j=j):
                high_copy(high.at[j, op_rows(0), :], j, 0, 0, to_week(3)).start()

            @pl.when(middle)
            def _(j=j, s=s):
                local_copy(column(1, s), high.at[j, op_rows(1), :], 4 + j).wait()

            @pl.when(edge)
            def _(j=j):
                high_copy(high.at[j, op_rows(1), :], j, 1, 0, to_week(3)).wait_recv()

    def panel_out():
        return remote(pan.at[1], pan_s.at[0], pan_r.at[0], {ROW: pair}, panel_ref)

    def inner_near(j):
        return remote(inn.at[j], inn_s.at[j], inn_r.at[j], {WEEK: jnp.where(week == 0, 1, 2)}, inn_in.at[j])

    def inner_far(j, i):
        device = {WEEK: jnp.int32(1)} if j == 0 else {WEEK: jnp.int32(1), ROW: pair}
        return remote(inn.at[j], inn_s.at[j], inn_r.at[2 + i], device, inner_ref.at[i])

    def own_weight():
        return pltpu.make_async_copy(weight_ref, wall.at[week], wt_s.at[n_week - 1])

    def turn_high():
        wait_high()
        step = min(length, 512)
        for j in range(2):
            for op in range(2):
                for at in range(0, length, step):
                    rows = pl.ds(op * length + at, step)
                    flat = high[j, rows, :].T.astype(jnp.float32) * wall[1 + op, 1 + op, pl.ds(at, step)][None, :]
                    turned[j, :, rows] = flat.astype(turned.dtype)

    tile = min(slices, 256)

    def wait_whole():
        for k in range(n_col):
            back_copy(k).wait_recv()

    def make_panel(j):
        @pl.loop(0, slices // tile)
        def _(i):
            at = pl.ds(pl.multiple_of(i * tile, tile), tile)
            pan[j, :, at] = jnp.dot(turned[j], whole[:, at], preferred_element_type=jnp.float32).astype(pan.dtype)

        if j == 0:
            local_copy(pan.at[0], panel_ref, 0).start()
        else:
            pl.when(middle)(lambda: panel_out().start())

    def make_inner(j):
        @pl.loop(0, 2 * length // tile)
        def _(i):
            at = pl.ds(pl.multiple_of(i * tile, tile), tile)
            inn[j, :, at] = contract_last(pan[j], whole[at, :]).astype(inn.dtype)

        pl.when(edge)(lambda: inner_near(j).start())

    def join_inner(j):
        @pl.when(middle)
        def _():
            inner_near(j).wait_recv()
            for op in range(2):
                at = op_rows(op)
                both = inn[j, :, at].astype(jnp.float32) + inn_in[j, :, at].astype(jnp.float32)
                inn[j, :, at] = (both * wall[1 + op, 1 + op, :][None, :]).astype(inn.dtype)

            pl.when(week == 2)(lambda: inner_far(j, 1).start())

            @pl.when(week == 1)
            def _():
                if j == 1:
                    inner_far(1, 0).start()
                else:
                    local_copy(inn.at[0], inner_ref.at[0], 1).start()

    first("start")
    for u in range(UNITS):
        local(u, lambda w, u=u: take(u, w).start())
    early()
    for u in range(UNITS):
        def move(w, u=u):
            take(u, w).wait()
            put(u).start()

        local(u, move)

    def begin(u):
        local(u, lambda w: put(u).wait())
        for _, _, _, week_of, unit in FIRST:
            if unit == u:
                @pl.when(week == week_of)
                def _():
                    remote(place(u, mine), first_s.at[u], first_r.at[u], {ROW: pair}).wait_recv()

        @pl.when(inside)
        def _():
            to_opp(u, mine, 0).start()
            to_pair(u, mine, 0).start()

        pl.when(outside)(lambda: to_pair(u, mine, 1).start())
        aside(u, mine, 0)
        pl.when(outside)(lambda: spread(u, mine))

    for item in ORDER:
        during(item, begin)

    def from_side(item, at_row, hop, onward=None):
        def body(u):
            for k in peers:
                side(u, mine, hop, k).wait_recv()
                if onward is not None:
                    onward(u, k)
                spread(u, slab(at_row, other(k)))

        during(item, body)

    def arrived(item, s, hop, then):
        def body(u):
            to_pair(u, s, hop).wait_recv()
            then(u)
            spread(u, s)

        during(item, body)

    @pl.when(outside)
    def _():
        for item in ORDER:
            from_side(item, row, 0, lambda u, k: cross(u, k).start())
        for hop, at_row in enumerate((pair, opp, end)):
            s = slab(at_row, col)
            for i, item in enumerate(ORDER):
                arrived(item, s, hop, lambda u, s=s, hop=hop: aside(u, s, hop + 1))
                if hop:
                    from_side(item, (pair, opp)[hop - 1], hop)
                if hop == 2 and i == 3:
                    relays(row)
                    relays(pair)
                    own_flows()
                    turn_left()
                if hop == 2 and i >= 2:
                    from_side(ORDER[i - 2], end, 3)
        relays(opp)
        for item in ORDER[-2:]:
            from_side(item, end, 3)
        relays(end)

    @pl.when(inside)
    def _():
        def cross_in(item):
            def body(u):
                for k in peers:
                    cross(u, k).wait_recv()
                    spread(u, slab(pair, other(k)))

            during(item, body)

        def hand(item, at_row, hop):
            s = slab(at_row, col)

            def then(u):
                to_pair(u, s, hop).start()
                aside(u, s, hop)

            arrived(item, s, 2 * hop - 2, then)

        def near_one(item):
            hand(item, opp, 1)

        def far_one(item):
            hand(item, end, 2)

        def pass_on(item):
            during(item, lambda u: to_opp(u, far, 2).start())

        def outer_one(item):
            arrived(item, far, 1, lambda u: None)

        start, middle_part, last = ORDER[:2], ORDER[2:4], ORDER[4:]
        for item in start:
            near_one(item)
        spread_low()
        make_part()
        for item in ORDER:
            during(item, lambda u: spread(u, mine))
        for item in middle_part:
            near_one(item)
        for item in start:
            outer_one(item)
            pass_on(item)
        for k in peers:
            add_half(k)
        for item in last:
            near_one(item)
        for item in (*middle_part, *last):
            outer_one(item)
        for item in ORDER:
            from_side(item, row, 0)
        add_half(0)
        make_whole()
        far_one(start[0])
        for item in middle_part:
            pass_on(item)
        far_one(start[1])
        pass_whole()
        for item in last:
            pass_on(item)
        own_flows()
        start_high()
        for item in ORDER:
            from_side(item, opp, 1)
        for item in ORDER:
            cross_in(item)
        relays(row)
        turn_left()
        for item in middle_part:
            far_one(item)
        for item in start:
            from_side(item, end, 2)
        turn_high()
        wait_whole()
        make_panel(1)
        make_inner(1)
        far_one(last[0])
        for item in middle_part:
            from_side(item, end, 2)
        make_panel(0)
        make_inner(0)
        for item in last[1:]:
            far_one(item)
        pl.when(edge)(lambda: panel_out().start())
        relays(pair)
        join_inner(1)
        join_inner(0)
        relays(opp)
        for item in last:
            from_side(item, end, 2)
        relays(end)

    @pl.when(middle)
    def _():
        for s in range(n):
            for flow in range(FLOWS):
                def arrive(s=s, flow=flow):
                    ref = cell(0, 0, s)
                    remote(ref, flow_s.at[0, s], flow_r.at[flow, s], {ROW: pair}).wait_recv()

                if flow == 3:
                    pl.when((mine != s) & (outside | (far != s)))(arrive)
                elif flow < FLOWS - 1:
                    pl.when(mine != s)(arrive)
                else:
                    arrive()

    @pl.when(week == 1)
    def _():
        inner_far(1, 1).wait_recv()
        pl.when(outside)(lambda: inner_far(1, 0).wait_recv())

    @pl.when(outside)
    def _():
        panel_out().wait_recv()
        by_role(lambda op, lag, *_: low_copy(x_ref.at[lag], 1, op, 0, {ROW: pair}).wait_send())
        pivot_out().wait_send()

    for k in range(1, n_week):
        weight_copy(k).wait_send()

    @pl.when(inside)
    def _():
        def sent(op, lag, near, across, theirs):
            for j in range(2):
                for i in range(2):
                    low_copy(x_ref.at[0], j, op, i, to_week(0)).wait_send()
                low_copy(x_ref.at[0], j, theirs, 0, to_week(0)).wait_send()

        by_role(sent)
        for k in range(n_col):
            half_copy(k).wait_send()
        for k in peers:
            sum_copy(k).wait_send()
            all_copy(k).wait_send()
        for k in range(n_col):
            back_copy(k).wait_send()

        @pl.when(week == 1)
        def _():
            for j, s in enumerate(slabs):
                high_copy(column(0, s), j, 0, 0, to_week(2)).wait_send()
                high_copy(column(0, s), j, 0, 1, to_week(0)).wait_send()
                high_copy(column(1, s), j, 1, 0, to_week(0)).wait_send()

        @pl.when(week == 2)
        def _():
            for j, s in enumerate(slabs):
                high_copy(column(3, s), j, 1, 0, to_week(3)).wait_send()
                high_copy(high.at[j, op_rows(0), :], j, 0, 0, to_week(3)).wait_send()

        local_copy(pan.at[0], panel_ref, 0).wait()
        panel_out().wait_send()
        for j in range(2):
            pl.when(edge)(lambda j=j: inner_near(j).wait_send())
            pl.when(week == 2)(lambda j=j: inner_far(j, 1).wait_send())

        @pl.when(week == 1)
        def _():
            inner_far(1, 0).wait_send()
            local_copy(inn.at[0], inner_ref.at[0], 1).wait()

    first("wait")
    for u in range(UNITS):
        def finish(u=u):
            for k in peers:
                for hop in range(3):
                    side(u, mine, hop, k).wait_send()

            @pl.when(outside)
            def _():
                to_pair(u, mine, 1).wait_send()
                for k in peers:
                    side(u, mine, 3, k).wait_send()
                    cross(u, k).wait_send()

            @pl.when(inside)
            def _():
                to_opp(u, mine, 0).wait_send()
                to_opp(u, far, 2).wait_send()
                for hop in range(3):
                    to_pair(u, mine, hop).wait_send()

        active(u, finish)
        if u >= 2:
            for s in range(n):
                spread(u, s, "wait")
    for s in range(n):
        relay(s, "wait")
    left_out().wait()


def gather(x, pivot, weight, collective_id):
    n_row, n_col = lax.axis_size(ROW), lax.axis_size(COL)
    _, length, width = x.shape
    slices = pivot.shape[0]
    n = n_row * n_col
    assert n_row == 4 and lax.axis_size(WEEK) == 4
    sides = (UNITS, n_col - 1)
    vmem = functools.partial(lambda *shape: pltpu.VMEM(shape, x.dtype))
    sent = length * width * 2 * (n - 1) * 9 // 4
    hbm = pl.BlockSpec(memory_space=pl.ANY)
    return pl.pallas_call(
        functools.partial(gather_kernel, n_row, n_col),
        out_shape=(
            jax.ShapeDtypeStruct((5, length, width * n), x.dtype),
            jax.ShapeDtypeStruct((width, slices), x.dtype),
            jax.ShapeDtypeStruct((2, width, 2 * length), x.dtype),
            jax.ShapeDtypeStruct((len(SCALE), width, length), x.dtype),
        ),
        in_specs=[hbm] * 3,
        out_specs=(hbm,) * 4,
        scratch_shapes=[
            pltpu.VMEM((UNITS, length // 2, width), x.dtype), DMA((UNITS,)), DMA((UNITS,)), DMA((UNITS,)),
            DMA((UNITS, 3)), DMA((UNITS, 3)), DMA((UNITS, 3)), DMA(sides), DMA(sides),
            DMA((UNITS, 4, n_col - 1)), DMA((UNITS, 4, n_col - 1)), DMA((5, n)), DMA((FLOWS, n)),
            vmem(2, 2 * length, width), vmem(2, slices, width), vmem(2, 2 * length, width),
            vmem(2 * length, slices), vmem(n_col, length // n_col, slices),
            vmem(n_col - 1, length // n_col, slices),
            vmem(2 * length, slices),
            vmem(2, width, 2 * length), vmem(2, width, slices), vmem(2, width, 2 * length),
            vmem(2, width, 2 * length), pltpu.VMEM((4, *weight.shape), weight.dtype),
            DMA((2, 2, 2)), DMA((2, 2)), DMA((1,)), DMA((1,)), DMA((2, 2, 2)), DMA((2, 2)), DMA((6,)),
            DMA((n_col,)), DMA((n_col,)), DMA((n_col - 1,)), DMA((n_col - 1,)),
            DMA((n_col - 1,)), DMA((n_col - 1,)), DMA((n_col,)), DMA((n_col,)),
            DMA((1,)), DMA((1,)), DMA((2,)), DMA((4,)), DMA((4,)), DMA((3,)),
            vmem(3, length, width), vmem(len(SCALE), width, length), DMA((4,)),
        ],
        compiler_params=pltpu.CompilerParams(
            collective_id=collective_id, has_side_effects=True, vmem_limit_bytes=60 << 20),
        cost_estimate=pl.CostEstimate(flops=0, bytes_accessed=sent * 8, transcendentals=0),
    )(x, pivot, weight)


def when_tile(at_ref, tile, columns, width, body):
    first = at_ref[1] * width

    @pl.when(first // columns == tile)
    def _():
        body(pl.ds(pl.multiple_of(lax.rem(first, columns), width), width))


def diagonal(prior_ref, width):
    rows = lax.broadcasted_iota(jnp.int32, (width, width), 0)
    cols = lax.broadcasted_iota(jnp.int32, (width, width), 1)
    return jnp.where(rows == cols, prior_ref[:, :1], 0.0)


def bands_kernel(at_ref, left_ref, prior_ref, *refs):
    full_refs, out_ref = refs[:5], refs[5]
    week = at_ref[0]
    tile = pl.program_id(0)
    width = left_ref.shape[1]
    columns = out_ref.shape[2]

    for w, by_band in enumerate(TERMS):
        @pl.when(week == w)
        def _(by_band=by_band):
            for i, band in enumerate(by_band):
                if band:
                    total = None
                    for _, right, p in band:
                        term = jnp.dot(left_ref[p], full_refs[right][...], preferred_element_type=jnp.float32)
                        total = term if total is None else total + term
                    out_ref[i] = total
                else:
                    out_ref[i] = jnp.zeros(out_ref.shape[1:], out_ref.dtype)

    def add(at):
        out_ref[0, :, at] += diagonal(prior_ref, width)

    when_tile(at_ref, tile, columns, width, add)


def bands(at, full, left, prior, columns):
    slots, length, regions = full.shape
    width = prior.shape[0]

    def right(slot):
        def index(j, at):
            here = functools.reduce(jnp.logical_or, [at[0] == w for w in range(4) if HAVE[slot][w]])
            return slot, 0, jnp.where(here, j, 0)

        return pl.BlockSpec((None, length, columns), index)

    return pl.pallas_call(
        bands_kernel,
        out_shape=jax.ShapeDtypeStruct((3, width, regions), jnp.float32),
        grid_spec=pltpu.PrefetchScalarGridSpec(
            num_scalar_prefetch=1,
            grid=(regions // columns,),
            in_specs=[
                pl.BlockSpec(left.shape, lambda j, at: (0, 0, 0), pipeline_mode=pl.Buffered(1)),
                pl.BlockSpec(prior.shape, lambda j, at: (0, 0)),
                *[right(slot) for slot in range(slots)],
            ],
            out_specs=pl.BlockSpec((3, width, columns), lambda j, at: (0, 0, j)),
        ),
        compiler_params=pltpu.CompilerParams(dimension_semantics=("arbitrary",), vmem_limit_bytes=60 << 20),
        cost_estimate=pl.CostEstimate(
            flops=10 * width * length * regions, bytes_accessed=full.size * 2 + 12 * width * regions,
            transcendentals=0),
    )(at, left, prior, *[full] * slots)


def schur_kernel(at_ref, left_ref, prior_ref, inner_ref, *refs):
    full_refs, out_refs, turned, total = refs[:3], refs[3:-2], refs[-2], refs[-1]
    week = at_ref[0]
    tile = pl.program_id(0)
    slots, width, length = left_ref.shape
    columns = total.shape[1]
    tiles = pl.num_programs(0) // len(out_refs)

    @pl.when(week == 1)
    def _():
        @pl.when(tile == 0)
        def _():
            for k in range(2):
                at = pl.ds(k * length, length)
                inner = inner_ref[0, :, at].astype(jnp.float32) + inner_ref[1, :, at].astype(jnp.float32)
                turned[k] = (left_ref[k].astype(jnp.float32) - inner).astype(turned.dtype)

        block = jnp.dot(turned[0], full_refs[0][...], preferred_element_type=jnp.float32)
        block = block + jnp.dot(turned[1], full_refs[1][...], preferred_element_type=jnp.float32)
        block = block + jnp.dot(left_ref[2], full_refs[2][...], preferred_element_type=jnp.float32)
        total[...] = block

        def add(at):
            total[:, at] += diagonal(prior_ref, width)

        when_tile(at_ref, tile, columns, width, add)
        for q, out_ref in enumerate(out_refs):
            @pl.when(tile // tiles == q)
            def _(out_ref=out_ref):
                out_ref[...] = total[...].astype(out_ref.dtype)


def schur_rows(at, full, left, prior, inner, columns):
    _, length, regions = full.shape
    width = prior.shape[0]
    quarters = 4
    columns = min(columns, regions // quarters)
    tiles = regions // quarters // columns
    whole = pl.Buffered(1)

    def part(q):
        return pl.BlockSpec((width, columns), lambda j, at: (0, jnp.clip(j - q * tiles, 0, tiles - 1)))

    def right(slot):
        return pl.BlockSpec((None, length, columns), lambda j, at: (slot, 0, jnp.where(at[0] == 1, j, 0)))

    return pl.pallas_call(
        schur_kernel,
        out_shape=[jax.ShapeDtypeStruct((width, regions // quarters), jnp.bfloat16)] * quarters,
        grid_spec=pltpu.PrefetchScalarGridSpec(
            num_scalar_prefetch=1,
            grid=(regions // columns,),
            in_specs=[
                pl.BlockSpec((3, width, length), lambda j, at: (0, 0, 0), pipeline_mode=whole),
                pl.BlockSpec(prior.shape, lambda j, at: (0, 0)),
                pl.BlockSpec(inner.shape, lambda j, at: (0, 0, 0), pipeline_mode=whole),
                *[right(slot) for slot in range(3)],
            ],
            out_specs=[part(q) for q in range(quarters)],
            scratch_shapes=[pltpu.VMEM((2, width, length), full.dtype), pltpu.VMEM((width, columns), jnp.float32)],
        ),
        compiler_params=pltpu.CompilerParams(dimension_semantics=("arbitrary",), vmem_limit_bytes=60 << 20),
        cost_estimate=pl.CostEstimate(
            flops=6 * width * length * regions, bytes_accessed=6 * length * regions, transcendentals=0),
    )(at, left, prior, inner, *[full] * 3)


def body(sensitivity, reach, obs_weight, prior_precision, pivot_solve):
    week = lax.axis_index(WEEK)
    n_week, n_col = lax.axis_size(WEEK), lax.axis_size(COL)
    local = sensitivity[0]
    lags, length, width = local.shape
    mine = lax.axis_index(ROW) * n_col + lax.axis_index(COL)

    lag = jnp.arange(8)[:, None]
    own_weight = jnp.where((reach >= lag) & (week >= lag) & (lag < lags), obs_weight, 0.0)
    full, panel, inner, left = gather(local, pivot_solve, own_weight, 0)
    at = jnp.stack([week, mine]).astype(jnp.int32)
    prior = jnp.broadcast_to(prior_precision[0][:, None], (width, 128))
    columns = max(min(1024, full.shape[2] // n_week), width)
    rows = schur_rows(at, full, left, prior, inner, columns)
    moved = [(w, lax.ppermute(rows[w], WEEK, [(1, w)])) for w in (2, 3, 0)]
    h = bands(at, full, left, prior, max(min(512, full.shape[2] // n_week), width))
    schur = rows[1]
    for w, block in moved:
        schur = jnp.where(week == w, block, schur)
    return (h[None], panel, schur.astype(jnp.float32))


def solution(mesh):
    placed = (
        P(WEEK, None, None, (ROW, COL)),
        P(WEEK, None),
        P(WEEK, None),
        P(WEEK, (ROW, COL)),
        P(WEEK, (ROW, COL)),
    )
    return jax.shard_map(
        body,
        mesh=mesh,
        in_specs=placed,
        out_specs=(
            P(WEEK, None, (ROW, COL), None),
            P((ROW, COL), WEEK),
            P((ROW, COL), WEEK),
        ),
        check_vma=False,
    )
```
